32 devices in a mesh: fsdp: 4 (over x, core), ctx: 4 (over z), tp: 2 (over y).
Axes of the slice: x: 2, y: 2, z: 4, core: 2. Of those that a mesh axis runs over, the one named last changes fastest.
Arguments:
- layer_input: bfloat16 [4096, 2048], P(('fsdp', 'ctx', 'tp')), may hold values from -6 to 6
- cotangent: bfloat16 [4096, 2048], P(('fsdp', 'ctx', 'tp')), may hold values from -6 to 6
- lengths: int32 [4, 2], P('fsdp'), may hold values from 0 to 1024, as said below
- attn_norm: bfloat16 [2048], replicated, may hold values from 0.5 to 1.5
- query_norm_gain: bfloat16 [128], replicated, may hold values from 0.25 to 1.75
- k_norm: bfloat16 [128], replicated, may hold values from 0.25 to 1.75
- w_query: bfloat16 [2048, 2048], P('fsdp', 'tp'), may hold values from -0.125 to 0.125
- key_weight: bfloat16 [2048, 1024], P('fsdp', 'tp'), may hold values from -0.125 to 0.125
- value_weight: bfloat16 [2048, 1024], P('fsdp', 'tp'), may hold values from -0.125 to 0.125
- w_out_gate: bfloat16 [2048, 2048], P('fsdp', 'tp'), may hold values from -0.125 to 0.125
- w_output: bfloat16 [2048, 2048], P(('tp', 'fsdp')), may hold values from -2 to 2
- ffn_norm: bfloat16 [2048], replicated, may hold values from 0.5 to 1.5
- w_gate: bfloat16 [2048, 6144], P('fsdp', 'tp'), may hold values from -0.125 to 0.125
- w_up: bfloat16 [2048, 6144], P('fsdp', 'tp'), may hold values from -0.125 to 0.125
- w_down: bfloat16 [6144, 2048], P(('tp', 'fsdp')), may hold values from -0.078125 to 0.078125
Outputs:
- layer_output: bfloat16 [4096, 2048], P(('fsdp', 'ctx', 'tp'))
- input_grad: bfloat16 [4096, 2048], P(('fsdp', 'ctx', 'tp'))
- grad_attn_norm: float32 [2048], replicated
- grad_q_norm: float32 [128], replicated
- grad_k_norm: float32 [128], replicated
- grad_w_query: float32 [2048, 2048], P('fsdp', 'tp')
- grad_w_key: float32 [2048, 1024], P('fsdp', 'tp')
- grad_w_value: float32 [2048, 1024], P('fsdp', 'tp')
- grad_w_out_gate: float32 [2048, 2048], P('fsdp', 'tp')
- grad_w_output: float32 [2048, 2048], P(('tp', 'fsdp'))
- grad_ffn_norm: float32 [2048], replicated
- grad_w_gate: float32 [2048, 6144], P('fsdp', 'tp')
- grad_w_up: float32 [2048, 6144], P('fsdp', 'tp')
- grad_w_down: float32 [6144, 2048], P(('tp', 'fsdp'))
The draws below stay inside these ranges and needn't reach their ends.
Inputs may be any that keep to these rules, and one draw needn't show every extreme that they name: `lengths`: per packed row the first count is at least 512 and the two counts add up to at most 1024; some row holds a single sequence of 1024 tokens.
All inputs are finite; a program needn't handle non-finite values.
Results may differ from the reference program's by a relative error of at most 0.024.
Values may be sent and summed in bfloat16 or wider, within the bound.
No kernel may reach another device: no remote copies, remote signals or barrier semaphores. Data moves between devices by JAX's collectives and lax.ppermute only.
A program may use at most 448 MiB of HBM per device.

```python
import jax
import jax.numpy as jnp
from jax import lax

MODEL_WIDTH = 2048
QUERY_HEADS = 16
KEY_VALUE_HEADS = 8
HEAD_SIZE = 128
FF = 6144
ROW = 1024
ROWS = 4
TOKENS = 4096


def draw_lengths(key, part):
    first_key, second_key = jax.random.split(jax.random.fold_in(key, 17))
    first_len = jax.random.randint(first_key, (ROWS,), ROW // 2, ROW + 1)
    first_len = first_len.at[0].set(ROW)
    second_len = jax.random.randint(second_key, (ROWS,), 0, ROW - first_len + 1)
    return jnp.stack([first_len, second_len], axis=1).astype(jnp.int32)


def shard_levels(stream_key, dims, cuts, least, high):
    level, own = 1.0, jax.random.fold_in(stream_key, 6)
    for axis_at, parts in cuts:
        heights = jnp.exp(jax.random.uniform(jax.random.fold_in(own, axis_at), (parts,), jnp.float32, least / len(cuts), high / len(cuts)))
        level = level * jnp.repeat(heights, dims[axis_at] // parts).reshape([-1 if axis == axis_at else 1 for axis in range(len(dims))])
    return level


def bell_draw(rng, extent, deviation, most, shards=(), kind=jnp.bfloat16):
    entries = jax.random.normal(rng, extent, jnp.float32) * deviation
    if len(shards) > 0:
        entries = shard_levels(rng, extent, shards, -0.22, 0.18) * entries
    return jnp.clip(entries, min=-most, max=most).astype(kind)


def setup_inputs(seed: int = 0) -> dict:
    keys = jax.random.split(jax.random.key(seed), 16)
    return {
        "layer_input": bell_draw(keys[0], (TOKENS, MODEL_WIDTH), 1.0, 6.0, ((0, 32),)),
        "cotangent": bell_draw(keys[1], (TOKENS, MODEL_WIDTH), 1.0, 6.0, ((0, 32),)),
        "lengths": draw_lengths(jax.random.fold_in(keys[15], 71), 0),
        "attn_norm": jnp.clip(1.0 + 0.1 * jax.random.normal(keys[3], (MODEL_WIDTH,), jnp.float32), 0.5, 1.5).astype(jnp.bfloat16),
        "query_norm_gain": jnp.clip(1.0 + 0.15 * jax.random.normal(keys[4], (HEAD_SIZE,), jnp.float32), 0.25, 1.75).astype(jnp.bfloat16),
        "k_norm": jnp.clip(1.0 + 0.15 * jax.random.normal(keys[5], (HEAD_SIZE,), jnp.float32), 0.25, 1.75).astype(jnp.bfloat16),
        "w_query": bell_draw(keys[6], (MODEL_WIDTH, QUERY_HEADS * HEAD_SIZE), MODEL_WIDTH ** -0.5, 0.125, ((0, 4), (1, 2))),
        "key_weight": bell_draw(keys[7], (MODEL_WIDTH, KEY_VALUE_HEADS * HEAD_SIZE), MODEL_WIDTH ** -0.5, 0.125, ((0, 4), (1, 2))),
        "value_weight": bell_draw(keys[8], (MODEL_WIDTH, KEY_VALUE_HEADS * HEAD_SIZE), MODEL_WIDTH ** -0.5, 0.125, ((0, 4), (1, 2))),
        "w_out_gate": bell_draw(keys[9], (MODEL_WIDTH, QUERY_HEADS * HEAD_SIZE), MODEL_WIDTH ** -0.5, 0.125, ((0, 4), (1, 2))),
        "w_output": bell_draw(keys[10], (QUERY_HEADS * HEAD_SIZE, MODEL_WIDTH), (max(QUERY_HEADS * HEAD_SIZE // 256, 1)) ** -0.5, 2.0, ((0, 8),)),
        "ffn_norm": jnp.clip(1.0 + 0.1 * jax.random.normal(keys[11], (MODEL_WIDTH,), jnp.float32), 0.5, 1.5).astype(jnp.bfloat16),
        "w_gate": bell_draw(keys[12], (MODEL_WIDTH, FF), MODEL_WIDTH ** -0.5, 0.125, ((0, 4), (1, 2))),
        "w_up": bell_draw(keys[13], (MODEL_WIDTH, FF), MODEL_WIDTH ** -0.5, 0.125, ((0, 4), (1, 2))),
        "w_down": bell_draw(keys[14], (FF, MODEL_WIDTH), FF ** -0.5, 0.078125, ((0, 8),)),
    }


EPSILON = 1e-06
ROPE_BASE = 1000000.0
NEG_FILL = -1e+30

@jax.custom_vjp
def reduced_precision(v):
    return lax.optimization_barrier(v.astype(jnp.bfloat16)).astype(jnp.float32)

@jax.custom_vjp
def reduced_backward(v):
    return v

def low_keep(v):
    return (reduced_precision(v), None)

def low_pass(kept, grad):
    return (grad,)

def back_keep(v):
    return (v, None)

def back_low(kept, grad):
    return (reduced_precision(grad),)
reduced_precision.defvjp(low_keep, low_pass)
reduced_backward.defvjp(back_keep, back_low)

def matrix_product(left_side, right_side):
    return jnp.dot(left_side, right_side, precision=lax.Precision.HIGHEST, preferred_element_type=jnp.float32)

def apply_rms_norm(values, gain_vec):
    return values * lax.rsqrt(lax.optimization_barrier(jnp.mean(values * values, axis=-1, keepdims=True)) + EPSILON) * gain_vec

def apply_rotary(values, token_position):
    half_size = values.shape[-1] // 2
    frequency = jnp.power(ROPE_BASE, -jnp.arange(half_size, dtype=jnp.float32) / half_size)
    angle = token_position.astype(jnp.float32)[:, None] * frequency[None, :]
    cosine = jnp.cos(angle)[:, None, :]
    sine = jnp.sin(angle)[:, None, :]
    first_half = values[..., :half_size]
    second_half = values[..., half_size:]
    return jnp.concatenate([first_half * cosine - second_half * sine, second_half * cosine + first_half * sine], axis=-1)

def attention(query_rotated, key_rot, value_reduced, segment):
    slot_total_count = query_rotated.shape[0]
    block_length = min(512, slot_total_count)
    slot_ids = jnp.arange(slot_total_count, dtype=jnp.int32)
    query_block_list = query_rotated.reshape(slot_total_count // block_length, block_length, KEY_VALUE_HEADS, QUERY_HEADS // KEY_VALUE_HEADS, HEAD_SIZE)
    slot_blocks = slot_ids.reshape(slot_total_count // block_length, block_length)
    segment_blocks = segment.reshape(slot_total_count // block_length, block_length)
    score_scale = HEAD_SIZE ** (-0.5)

    def one_block(block_items):
        query_part, query_slots, query_segment = block_items
        raw_scores = jnp.einsum('qhgd,khd->hgqk', query_part, key_rot, precision=lax.Precision.HIGHEST)
        scores = reduced_backward(raw_scores) * score_scale
        allowed = (query_segment[:, None] == segment[None, :]) & (slot_ids[None, :] <= query_slots[:, None])
        masked = jnp.where(allowed, scores, NEG_FILL)
        top_score = lax.optimization_barrier(jnp.max(masked, axis=-1, keepdims=True))
        weights = jnp.where(allowed, jnp.exp(masked - top_score), 0.0)
        prob_low = reduced_precision(weights / lax.optimization_barrier(jnp.sum(weights, axis=-1, keepdims=True)))
        return jnp.einsum('hgqk,khd->qhgd', prob_low, value_reduced, precision=lax.Precision.HIGHEST)
    mixed_all = lax.map(jax.checkpoint(one_block), (query_block_list, slot_blocks, segment_blocks))
    return mixed_all.reshape(slot_total_count, QUERY_HEADS * HEAD_SIZE)

def layer_row(inputs, attn_norm, query_norm_gain, k_norm, w_query, key_weight, value_weight, w_out_gate, w_output, ffn_norm, w_gate, w_up, w_down, segment, token_position, valid_rows):
    slot_total_count = inputs.shape[0]
    first_normed = reduced_precision(apply_rms_norm(inputs, attn_norm))
    query_rows = reduced_backward(matrix_product(first_normed, w_query)).reshape(slot_total_count, QUERY_HEADS, HEAD_SIZE)
    key_projected = reduced_backward(matrix_product(first_normed, key_weight)).reshape(slot_total_count, KEY_VALUE_HEADS, HEAD_SIZE)
    value_reduced = reduced_precision(reduced_backward(matrix_product(first_normed, value_weight))).reshape(slot_total_count, KEY_VALUE_HEADS, HEAD_SIZE)
    gate_logits = reduced_backward(matrix_product(first_normed, w_out_gate))
    query_rotated = reduced_precision(apply_rotary(apply_rms_norm(query_rows, query_norm_gain), token_position)).reshape(slot_total_count, KEY_VALUE_HEADS, QUERY_HEADS // KEY_VALUE_HEADS, HEAD_SIZE)
    key_rot = reduced_precision(apply_rotary(apply_rms_norm(key_projected, k_norm), token_position))
    mixed = reduced_backward(attention(query_rotated, key_rot, value_reduced, segment))
    gated_mix = reduced_precision(mixed * jax.nn.sigmoid(gate_logits))
    attn_out = reduced_backward(matrix_product(gated_mix, w_output))
    hidden_in = inputs + valid_rows * attn_out
    normed_two = reduced_precision(apply_rms_norm(hidden_in, ffn_norm))
    gate_pre = reduced_backward(matrix_product(normed_two, w_gate))
    up_pre = reduced_backward(matrix_product(normed_two, w_up))
    hidden_act = reduced_precision(jax.nn.silu(gate_pre) * up_pre)
    ffn_out = reduced_backward(matrix_product(hidden_act, w_down))
    return hidden_in + valid_rows * ffn_out

def reference(layer_input, cotangent, lengths, attn_norm, query_norm_gain, k_norm, w_query, key_weight, value_weight, w_out_gate, w_output, ffn_norm, w_gate, w_up, w_down):
    weight_list = tuple((weight_item.astype(jnp.float32) for weight_item in (attn_norm, query_norm_gain, k_norm, w_query, key_weight, value_weight, w_out_gate, w_output, ffn_norm, w_gate, w_up, w_down)))
    inputs = layer_input.astype(jnp.float32).reshape(ROWS, ROW, MODEL_WIDTH)
    cot_rows = cotangent.astype(jnp.float32).reshape(ROWS, ROW, MODEL_WIDTH)
    slot_ids = jnp.arange(ROW, dtype=jnp.int32)

    def one_row(totals, row_items):
        row_input, row_cot, row_lengths = row_items
        first_len = row_lengths[0]
        second_len = row_lengths[1]
        segment = jnp.where(slot_ids < first_len, 0, jnp.where(slot_ids < first_len + second_len, 1, 2)).astype(jnp.int32)
        seg_begin = jnp.where(segment == 0, 0, jnp.where(segment == 1, first_len, first_len + second_len)).astype(jnp.int32)
        token_position = slot_ids - seg_begin
        valid_rows = (segment < 2).astype(jnp.float32)[:, None]

        def forward(row_values, *params):
            return layer_row(row_values, *params, segment, token_position, valid_rows)
        result, pull_back = jax.vjp(forward, row_input, *weight_list)
        row_grads = pull_back(row_cot * valid_rows)
        totals = tuple((running + grad_item for running, grad_item in zip(totals, row_grads[1:])))
        return (totals, (result.astype(jnp.bfloat16), row_grads[0].astype(jnp.bfloat16)))
    zero_grads = tuple((jnp.zeros(weight_item.shape, jnp.float32) for weight_item in weight_list))
    totals, row_outs = lax.scan(one_row, zero_grads, (inputs, cot_rows, lengths))
    layer_output = row_outs[0].reshape(TOKENS, MODEL_WIDTH)
    input_grad = row_outs[1].reshape(TOKENS, MODEL_WIDTH)
    return (layer_output, input_grad, totals[0], totals[1], totals[2], totals[3], totals[4], totals[5], totals[6], totals[7], totals[8], totals[9], totals[10], totals[11])
```

```python
import jax
import jax.numpy as jnp
from jax import lax
from jax.sharding import PartitionSpec as P

HEAD_SIZE = 128


EPSILON = 1e-06
ROPE_BASE = 1000000.0
NEG_FILL = -1e30


def as_sent(value):

    def short(part):
        return part.astype(jnp.bfloat16) if part.dtype == jnp.float32 else part

    return jax.tree.map(short, value)


def apply_rms_norm(values, gain_vec):
    return (
        values * lax.rsqrt(jnp.mean(values * values, axis=-1, keepdims=True) + EPSILON) * gain_vec
    )


def norm_back(values, gain_vec, grad_in):
    row_scale = lax.rsqrt(jnp.mean(values * values, axis=-1, keepdims=True) + EPSILON)
    unit_rows = values * row_scale
    scaled = grad_in * gain_vec
    back_rows = row_scale * (
        scaled - unit_rows * jnp.mean(scaled * unit_rows, axis=-1, keepdims=True)
    )
    gain_grad = jnp.sum((grad_in * unit_rows).reshape(-1, values.shape[-1]), axis=0)
    return (back_rows, gain_grad)


def apply_rotary(values, token_position, direction):
    half_size = values.shape[-1] // 2
    frequency = jnp.power(ROPE_BASE, -jnp.arange(half_size, dtype=jnp.float32) / half_size)
    angle = token_position.astype(jnp.float32)[:, None] * frequency[None, :]
    cosine = jnp.cos(angle)[:, None, :]
    sine = direction * jnp.sin(angle)[:, None, :]
    first_half = values[..., :half_size]
    second_half = values[..., half_size:]
    return jnp.concatenate(
        [first_half * cosine - second_half * sine, second_half * cosine + first_half * sine],
        axis=-1,
    )


def segment_of(slot_ids, lengths):
    first_len = lengths[0, 0]
    second_len = lengths[0, 1]
    return jnp.where(slot_ids < first_len, 0, jnp.where(slot_ids < first_len + second_len, 1, 2))


def position_of(slot_ids, segment, lengths):
    seg_begin = jnp.where(
        segment == 0, 0, jnp.where(segment == 1, lengths[0, 0], lengths[0, 0] + lengths[0, 1])
    )
    return slot_ids - seg_begin


def to_block(local_part):
    return lax.all_gather(local_part, "tp", axis=0, tiled=True)


def to_share(partial_rows):
    return lax.psum_scatter(
        partial_rows.astype(jnp.bfloat16), "tp", scatter_dimension=0, tiled=True
    ).astype(jnp.float32)


def fold_product(left_rows, weight_set):
    pieces = jax.tree.map(
        lambda a: lax.all_gather(a, "fsdp", axis=0, tiled=True), as_sent(weight_set)
    )
    return tuple(
        (
            jnp.dot(left_rows, weight_part, preferred_element_type=jnp.float32)
            for weight_part in pieces
        )
    )


def back_product(grad_rows, weight_set):
    pieces = jax.tree.map(
        lambda a: lax.all_gather(a, "fsdp", axis=0, tiled=True), as_sent(weight_set)
    )
    result = lax.dot_general(
        grad_rows[0], pieces[0], (((1,), (1,)), ((), ())), preferred_element_type=jnp.float32
    )
    for grad_part, weight_part in zip(grad_rows[1:], pieces[1:]):
        result = result + lax.dot_general(
            grad_part, weight_part, (((1,), (1,)), ((), ())), preferred_element_type=jnp.float32
        )
    return result


def weight_grads(left_rows, grad_rows):
    widths = [grad_part.shape[1] for grad_part in grad_rows]
    shared = lax.psum_scatter(
        jnp.concatenate(
            [
                lax.dot_general(
                    left_rows,
                    grad_part,
                    (((0,), (0,)), ((), ())),
                    preferred_element_type=jnp.float32,
                )
                for grad_part in grad_rows
            ],
            axis=1,
        ).astype(jnp.bfloat16),
        "fsdp",
        scatter_dimension=0,
        tiled=True,
    )
    summed = lax.psum(shared, "ctx").astype(jnp.float32)
    pieces = []
    offset = 0
    for column_width in widths:
        pieces.append(summed[:, offset : offset + column_width])
        offset = offset + column_width
    return tuple(pieces)


def body(
    layer_input,
    cotangent,
    lengths,
    attn_norm,
    query_norm_gain,
    k_norm,
    w_query,
    key_weight,
    value_weight,
    w_out_gate,
    w_output,
    ffn_norm,
    w_gate,
    w_up,
    w_down,
):
    local_rows = layer_input.shape[0]
    block_rows = local_rows * lax.axis_size("tp")
    query_heads = w_query.shape[1] // HEAD_SIZE
    kv_heads = key_weight.shape[1] // HEAD_SIZE
    groups = query_heads // kv_heads
    score_scale = HEAD_SIZE ** (-0.5)
    block_first = lax.axis_index("ctx") * block_rows
    own_slots = (
        block_first + lax.axis_index("tp") * local_rows + jnp.arange(local_rows, dtype=jnp.int32)
    )
    own_valid = (segment_of(own_slots, lengths) < 2).astype(jnp.float32)[:, None]
    query_slots = block_first + jnp.arange(block_rows, dtype=jnp.int32)
    query_segment = segment_of(query_slots, lengths)
    query_position = position_of(query_slots, query_segment, lengths)
    inputs = layer_input.astype(jnp.float32)
    gain_one = attn_norm.astype(jnp.float32)
    gain_two = ffn_norm.astype(jnp.float32)
    query_gain = query_norm_gain.astype(jnp.float32)
    key_gain = k_norm.astype(jnp.float32)
    first_normed = to_block(apply_rms_norm(inputs, gain_one).astype(jnp.bfloat16))
    query_rows, key_projected, value_proj, gate_logits = fold_product(
        first_normed, (w_query, key_weight, value_weight, w_out_gate)
    )
    query_heads_raw = query_rows.reshape(block_rows, query_heads, HEAD_SIZE)
    key_heads_raw = key_projected.reshape(block_rows, kv_heads, HEAD_SIZE)
    query_rotated = apply_rotary(
        apply_rms_norm(query_heads_raw, query_gain), query_position, 1.0
    ).astype(jnp.bfloat16)
    key_rot = apply_rotary(apply_rms_norm(key_heads_raw, key_gain), query_position, 1.0).astype(
        jnp.bfloat16
    )
    query_grouped = query_rotated.reshape(block_rows, kv_heads, groups, HEAD_SIZE)
    key_flat = key_rot.reshape(block_rows, kv_heads * HEAD_SIZE)
    value_reduced = value_proj.astype(jnp.bfloat16)

    def key_mask(piece_rows):
        key_slots = jnp.arange(piece_rows, dtype=jnp.int32)
        key_segment = segment_of(key_slots, lengths)
        return (query_segment[:, None] == key_segment[None, :]) & (
            key_slots[None, :] <= query_slots[:, None]
        )

    head_shape = (kv_heads, groups, block_rows)
    running_top = jnp.full(head_shape + (1,), NEG_FILL, jnp.float32)
    key_piece = lax.all_gather(key_flat, "ctx", axis=0, tiled=True)
    value_piece = lax.all_gather(value_reduced, "ctx", axis=0, tiled=True)
    piece_rows = key_piece.shape[0]
    allowed = key_mask(piece_rows)
    raw_scores = jnp.einsum(
        "qhgd,khd->hgqk",
        query_grouped,
        key_piece.reshape(piece_rows, kv_heads, HEAD_SIZE),
        preferred_element_type=jnp.float32,
    )
    scores = jnp.where(allowed, raw_scores * score_scale, NEG_FILL)
    new_top = jnp.maximum(running_top, jnp.max(scores, axis=-1, keepdims=True))
    weights = jnp.where(allowed, jnp.exp(scores - new_top), 0.0)
    running_total = jnp.sum(weights, axis=-1, keepdims=True)
    mixed_sum = jnp.einsum(
        "hgqk,khd->hgqd",
        weights.astype(jnp.bfloat16),
        value_piece.reshape(piece_rows, kv_heads, HEAD_SIZE),
        preferred_element_type=jnp.float32,
    )
    mixed_sum, running_top, running_total = (mixed_sum, new_top, running_total)
    log_total = running_top + jnp.log(running_total)
    attended = jnp.transpose(mixed_sum / running_total, (2, 0, 1, 3))
    attended_rows = attended.reshape(block_rows, query_heads * HEAD_SIZE)
    gate_sig = jax.nn.sigmoid(gate_logits)
    gated_mix = (attended_rows * gate_sig).astype(jnp.bfloat16)
    attn_share = to_share(fold_product(gated_mix, (w_output,))[0])
    hidden_in = inputs + own_valid * attn_share
    normed_two = to_block(apply_rms_norm(hidden_in, gain_two).astype(jnp.bfloat16))
    gate_pre, up_pre = fold_product(normed_two, (w_gate, w_up))
    gate_sigmoid = jax.nn.sigmoid(gate_pre)
    activated = gate_pre * gate_sigmoid
    hidden_act = (activated * up_pre).astype(jnp.bfloat16)
    ffn_share = to_share(fold_product(hidden_act, (w_down,))[0])
    layer_output = (hidden_in + own_valid * ffn_share).astype(jnp.bfloat16)
    out_grad = cotangent.astype(jnp.float32) * own_valid
    ffn_grad = to_block(out_grad.astype(jnp.bfloat16))
    hidden_grad = back_product((ffn_grad,), (w_down,))
    grad_w_down = weight_grads(hidden_act, (ffn_grad,))[0]
    gate_grad = (
        hidden_grad * up_pre * gate_sigmoid * (1.0 + gate_pre * (1.0 - gate_sigmoid))
    ).astype(jnp.bfloat16)
    up_grad = (hidden_grad * activated).astype(jnp.bfloat16)
    normed_two_grad = to_share(back_product((gate_grad, up_grad), (w_gate, w_up)))
    grad_w_gate, grad_w_up = weight_grads(normed_two, (gate_grad, up_grad))
    back_two, gain_two_grad = norm_back(hidden_in, gain_two, normed_two_grad)
    hidden_total_grad = out_grad + back_two
    attn_grad = to_block((own_valid * hidden_total_grad).astype(jnp.bfloat16))
    gated_grad = back_product((attn_grad,), (w_output,))
    grad_w_output = weight_grads(gated_mix, (attn_grad,))[0]
    mixed_grad = (gated_grad * gate_sig).astype(jnp.bfloat16)
    gate_logit_grad = (gated_grad * attended_rows * gate_sig * (1.0 - gate_sig)).astype(
        jnp.bfloat16
    )
    mixed_grad_heads = mixed_grad.reshape(block_rows, kv_heads, groups, HEAD_SIZE)
    delta_rows = jnp.transpose(
        jnp.sum(mixed_grad_heads.astype(jnp.float32) * attended, axis=-1), (1, 2, 0)
    )[..., None]
    key_piece = lax.all_gather(key_flat, "ctx", axis=0, tiled=True)
    value_piece = lax.all_gather(value_reduced, "ctx", axis=0, tiled=True)
    piece_rows = key_piece.shape[0]
    key_view = key_piece.reshape(piece_rows, kv_heads, HEAD_SIZE)
    value_view = value_piece.reshape(piece_rows, kv_heads, HEAD_SIZE)
    allowed = key_mask(piece_rows)
    raw_scores = jnp.einsum(
        "qhgd,khd->hgqk", query_grouped, key_view, preferred_element_type=jnp.float32
    )
    soft_vals = jnp.where(allowed, jnp.exp(raw_scores * score_scale - log_total), 0.0)
    prob_grad = jnp.einsum(
        "qhgd,khd->hgqk", mixed_grad_heads, value_view, preferred_element_type=jnp.float32
    )
    score_grad = (soft_vals * (prob_grad - delta_rows) * score_scale).astype(jnp.bfloat16)
    query_acc = jnp.einsum(
        "hgqk,khd->qhgd", score_grad, key_view, preferred_element_type=jnp.float32
    )
    key_part = jnp.einsum(
        "hgqk,qhgd->khd", score_grad, query_grouped, preferred_element_type=jnp.float32
    ).reshape(piece_rows, kv_heads * HEAD_SIZE)
    value_part = jnp.einsum(
        "hgqk,qhgd->khd",
        soft_vals.astype(jnp.bfloat16),
        mixed_grad_heads,
        preferred_element_type=jnp.float32,
    ).reshape(piece_rows, kv_heads * HEAD_SIZE)
    kv_acc = jnp.concatenate([key_part, value_part], axis=1)
    query_acc, kv_acc = (query_acc, kv_acc)
    kv_own = lax.psum_scatter(
        kv_acc.astype(jnp.bfloat16), "ctx", scatter_dimension=0, tiled=True
    ).astype(jnp.float32)
    key_rot_grad = kv_own[:, : kv_heads * HEAD_SIZE].reshape(block_rows, kv_heads, HEAD_SIZE)
    value_grad = kv_own[:, kv_heads * HEAD_SIZE :].astype(jnp.bfloat16)
    key_back, key_gain_grad = norm_back(
        key_heads_raw, key_gain, apply_rotary(key_rot_grad, query_position, -1.0)
    )
    query_back, query_gain_grad = norm_back(
        query_heads_raw,
        query_gain,
        apply_rotary(query_acc.reshape(block_rows, query_heads, HEAD_SIZE), query_position, -1.0),
    )
    query_grad = query_back.reshape(block_rows, query_heads * HEAD_SIZE).astype(jnp.bfloat16)
    key_grad = key_back.reshape(block_rows, kv_heads * HEAD_SIZE).astype(jnp.bfloat16)
    attn_in_grads = (query_grad, key_grad, value_grad, gate_logit_grad)
    normed_one_grad = to_share(
        back_product(attn_in_grads, (w_query, key_weight, value_weight, w_out_gate))
    )
    grad_w_query, grad_w_key, grad_w_value, grad_w_out_gate = weight_grads(
        first_normed, attn_in_grads
    )
    back_one, gain_one_grad = norm_back(inputs, gain_one, normed_one_grad)
    input_grad = (hidden_total_grad + back_one).astype(jnp.bfloat16)
    gain_totals = lax.psum(
        (gain_one_grad, query_gain_grad, key_gain_grad, gain_two_grad), ("fsdp", "ctx", "tp")
    )
    return (
        layer_output,
        input_grad,
        gain_totals[0],
        gain_totals[1],
        gain_totals[2],
        grad_w_query,
        grad_w_key,
        grad_w_value,
        grad_w_out_gate,
        grad_w_output,
        gain_totals[3],
        grad_w_gate,
        grad_w_up,
        grad_w_down,
    )


def xor_pairs(count, mask):
    return [(i, i ^ mask) for i in range(count)]


def swap_plane(value, fsdp_mask, tp_mask):
    fsdp_size, tp_size = lax.axis_size("fsdp"), lax.axis_size("tp")
    if tp_mask == 0:
        return lax.ppermute(value, "fsdp", xor_pairs(fsdp_size, fsdp_mask))
    if fsdp_mask == 0:
        return lax.ppermute(value, "tp", xor_pairs(tp_size, tp_mask))
    return lax.ppermute(
        value,
        ("fsdp", "tp"),
        xor_pairs(fsdp_size * tp_size, fsdp_mask * tp_size + tp_mask),
    )


def swap_ranks(value):
    size = lax.axis_size("fsdp")
    pairs = [(a * size + b, b * size + a) for a in range(size) for b in range(size)]
    return lax.ppermute(value, ("fsdp", "ctx"), pairs)


PIECES = ((0, 0), (0, 1), (2, 0), (2, 1))


def plane_gather(own):
    near = [own if masks == (0, 0) else swap_plane(own, *masks) for masks in PIECES]
    far = [swap_plane(piece, 1, 0) for piece in near]
    return jnp.concatenate(near + far, axis=0)


def plane_scatter(near_part, far_part):
    rows = near_part.shape[0] // 4
    half = near_part + swap_plane(far_part.astype(jnp.bfloat16), 1, 0).astype(jnp.float32)
    total = half[:rows]
    for place in range(1, 4):
        piece = half[place * rows : (place + 1) * rows].astype(jnp.bfloat16)
        total = total + swap_plane(piece, *PIECES[place]).astype(jnp.float32)
    return total


def dot_nn(a, b):
    return jnp.dot(a, b, preferred_element_type=jnp.float32)


def dot_nt(a, b):
    return lax.dot_general(a, b, (((1,), (1,)), ((), ())), preferred_element_type=jnp.float32)


def dot_tn(a, b):
    return lax.dot_general(a, b, (((0,), (0,)), ((), ())), preferred_element_type=jnp.float32)


def scatter_product(rows, weight, dot):
    half = rows.shape[0] // 2
    far_part = dot(rows[half:], weight)
    near_part = dot(rows[:half], weight)
    return plane_scatter(near_part, far_part)


def chain_sum(part):
    low = part.astype(jnp.bfloat16)
    place = lax.axis_index("ctx")
    inward = lax.ppermute(low, "ctx", [(0, 1), (3, 2)])
    pair = (low.astype(jnp.float32) + inward.astype(jnp.float32)).astype(jnp.bfloat16)
    across = lax.ppermute(pair, "ctx", [(1, 2), (2, 1)])
    total = (pair.astype(jnp.float32) + across.astype(jnp.float32)).astype(jnp.bfloat16)
    outward = lax.ppermute(total, "ctx", [(1, 0), (2, 3)])
    inner = (place == 1) | (place == 2)
    return jnp.where(inner, total, outward).astype(jnp.float32)


def all_sum(value):
    for axis, mask in (("fsdp", 1), ("fsdp", 2), ("tp", 1), ("ctx", 1), ("ctx", 2)):
        value = value + lax.ppermute(value, axis, xor_pairs(lax.axis_size(axis), mask))
    return value


def weight_columns(weights, owner):
    parts = []
    for weight in weights:
        width = weight.shape[1] // lax.axis_size("fsdp")
        parts.append(lax.dynamic_slice_in_dim(weight, owner * width, width, 1))
    return jnp.concatenate(parts, axis=1)


def fetch_weights(weights):
    me, size = lax.axis_index("fsdp"), lax.axis_size("fsdp")
    rows = weights[0].shape[0]
    whole = None
    for mask in range(size):
        part = weight_columns(weights, me ^ mask)
        if mask:
            part = swap_plane(part, mask, 0)
        if whole is None:
            whole = jnp.zeros((rows * size, part.shape[1]), part.dtype)
        whole = lax.dynamic_update_slice_in_dim(whole, part, (me ^ mask) * rows, 0)
    return whole


def return_grads(left, right, widths):
    me, size = lax.axis_index("fsdp"), lax.axis_size("fsdp")
    rows = left.shape[1] // size
    outs = [jnp.zeros((rows, width * size), jnp.float32) for width in widths]
    for mask in range(size):
        columns = lax.dynamic_slice_in_dim(left, (me ^ mask) * rows, rows, 1)
        part = dot_tn(columns, right).astype(jnp.bfloat16)
        if mask:
            part = swap_plane(part, mask, 0)
        summed = chain_sum(part)
        offset = 0
        for place, width in enumerate(widths):
            outs[place] = lax.dynamic_update_slice_in_dim(
                outs[place], summed[:, offset : offset + width], (me ^ mask) * width, 1
            )
            offset += width
    return outs


def plane_body(
    layer_input,
    cotangent,
    lengths,
    attn_norm,
    query_norm_gain,
    k_norm,
    w_query,
    key_weight,
    value_weight,
    w_out_gate,
    w_output,
    ffn_norm,
    w_gate,
    w_up,
    w_down,
):
    fsdp_size, tp_size = lax.axis_size("fsdp"), lax.axis_size("tp")
    fsdp_at, tp_at = lax.axis_index("fsdp"), lax.axis_index("tp")
    local_rows = layer_input.shape[0]
    row_slots = local_rows * fsdp_size * tp_size
    query_heads = w_query.shape[1] // HEAD_SIZE // fsdp_size
    query_width = query_heads * HEAD_SIZE
    score_scale = HEAD_SIZE ** (-0.5)
    gain_one = attn_norm.astype(jnp.float32)
    gain_two = ffn_norm.astype(jnp.float32)
    query_gain = query_norm_gain.astype(jnp.float32)
    key_gain = k_norm.astype(jnp.float32)

    inputs = swap_ranks(layer_input).astype(jnp.float32)
    lengths = swap_ranks(lengths)
    cot = swap_ranks(cotangent).astype(jnp.float32)

    def slots_of(fsdp_index, tp_index):
        return (fsdp_index * tp_size + tp_index) * local_rows + jnp.arange(
            local_rows, dtype=jnp.int32
        )

    own_slots = slots_of(fsdp_at, tp_at)
    own_valid = (segment_of(own_slots, lengths) < 2).astype(jnp.float32)[:, None]
    slots = jnp.concatenate(
        [
            slots_of(fsdp_at ^ fsdp_mask ^ core, tp_at ^ tp_mask)
            for core in (0, 1)
            for fsdp_mask, tp_mask in PIECES
        ]
    )
    segment = segment_of(slots, lengths)
    position = position_of(slots, segment, lengths)

    first_normed = plane_gather(apply_rms_norm(inputs, gain_one).astype(jnp.bfloat16))
    attn_weights = fetch_weights((w_query, key_weight, value_weight, w_out_gate))
    out_grad = cot * own_valid
    ffn_grad = plane_gather(out_grad.astype(jnp.bfloat16))
    ffn_weights = fetch_weights((w_gate, w_up))

    projected = dot_nn(first_normed, attn_weights)
    query_raw = projected[:, :query_width].reshape(row_slots, query_heads, HEAD_SIZE)
    key_raw = projected[:, query_width : query_width + HEAD_SIZE].reshape(row_slots, 1, HEAD_SIZE)
    value_low = projected[:, query_width + HEAD_SIZE : query_width + 2 * HEAD_SIZE].astype(
        jnp.bfloat16
    )
    gate_logits = projected[:, query_width + 2 * HEAD_SIZE :]
    query_rot = apply_rotary(apply_rms_norm(query_raw, query_gain), position, 1.0).astype(
        jnp.bfloat16
    )
    key_rot = apply_rotary(apply_rms_norm(key_raw, key_gain), position, 1.0).astype(jnp.bfloat16)[
        :, 0
    ]

    allowed = (segment[:, None] == segment[None, :]) & (slots[None, :] <= slots[:, None])
    raw_scores = jnp.einsum("qgd,kd->gqk", query_rot, key_rot, preferred_element_type=jnp.float32)
    scores = jnp.where(allowed, raw_scores * score_scale, NEG_FILL)
    top = jnp.max(scores, axis=-1, keepdims=True)
    weights = jnp.where(allowed, jnp.exp(scores - top), 0.0)
    total = jnp.sum(weights, axis=-1, keepdims=True)
    mixed = jnp.einsum(
        "gqk,kd->gqd", weights.astype(jnp.bfloat16), value_low, preferred_element_type=jnp.float32
    )
    log_total = top + jnp.log(total)
    attended = jnp.transpose(mixed / total, (1, 0, 2))
    attended_rows = attended.reshape(row_slots, query_width)
    gate_sig = jax.nn.sigmoid(gate_logits)
    gated_mix = (attended_rows * gate_sig).astype(jnp.bfloat16)
    attn_share = scatter_product(gated_mix, w_output, dot_nn)
    hidden_in = inputs + own_valid * attn_share
    normed_two = plane_gather(apply_rms_norm(hidden_in, gain_two).astype(jnp.bfloat16))

    hidden_grad = dot_nt(ffn_grad, w_down)
    pre = dot_nn(normed_two, ffn_weights)
    hidden_width = w_down.shape[0]
    gate_pre, up_pre = pre[:, :hidden_width], pre[:, hidden_width:]
    gate_sigmoid = jax.nn.sigmoid(gate_pre)
    activated = gate_pre * gate_sigmoid
    hidden_act = (activated * up_pre).astype(jnp.bfloat16)
    grad_w_down = chain_sum(dot_tn(hidden_act, ffn_grad))
    gate_grad = (
        hidden_grad * up_pre * gate_sigmoid * (1.0 + gate_pre * (1.0 - gate_sigmoid))
    ).astype(jnp.bfloat16)
    up_grad = (hidden_grad * activated).astype(jnp.bfloat16)
    ffn_in_grads = jnp.concatenate([gate_grad, up_grad], axis=1)
    normed_two_grad = scatter_product(ffn_in_grads, ffn_weights, dot_nt)
    grad_w_gate, grad_w_up = return_grads(normed_two, ffn_in_grads, (hidden_width, hidden_width))
    ffn_share = scatter_product(hidden_act, w_down, dot_nn)
    layer_output = swap_ranks((hidden_in + own_valid * ffn_share).astype(jnp.bfloat16))

    back_two, gain_two_grad = norm_back(hidden_in, gain_two, normed_two_grad)
    hidden_total_grad = out_grad + back_two
    attn_grad = plane_gather((own_valid * hidden_total_grad).astype(jnp.bfloat16))
    gated_grad = dot_nt(attn_grad, w_output)
    grad_w_output = chain_sum(dot_tn(gated_mix, attn_grad))
    mixed_grad = (gated_grad * gate_sig).astype(jnp.bfloat16)
    gate_logit_grad = (gated_grad * attended_rows * gate_sig * (1.0 - gate_sig)).astype(
        jnp.bfloat16
    )
    mixed_grad_heads = mixed_grad.reshape(row_slots, query_heads, HEAD_SIZE)
    delta_rows = jnp.transpose(
        jnp.sum(mixed_grad_heads.astype(jnp.float32) * attended, axis=-1), (1, 0)
    )[..., None]
    raw_again = jnp.einsum("qgd,kd->gqk", query_rot, key_rot, preferred_element_type=jnp.float32)
    soft = jnp.where(allowed, jnp.exp(raw_again * score_scale - log_total), 0.0)
    prob_grad = jnp.einsum(
        "qgd,kd->gqk", mixed_grad_heads, value_low, preferred_element_type=jnp.float32
    )
    score_grad = (soft * (prob_grad - delta_rows) * score_scale).astype(jnp.bfloat16)
    query_rot_grad = jnp.einsum(
        "gqk,kd->qgd", score_grad, key_rot, preferred_element_type=jnp.float32
    )
    key_rot_grad = jnp.einsum(
        "gqk,qgd->kd", score_grad, query_rot, preferred_element_type=jnp.float32
    )
    value_grad = jnp.einsum(
        "gqk,qgd->kd",
        soft.astype(jnp.bfloat16),
        mixed_grad_heads,
        preferred_element_type=jnp.float32,
    ).astype(jnp.bfloat16)
    key_back, key_gain_grad = norm_back(
        key_raw, key_gain, apply_rotary(key_rot_grad[:, None], position, -1.0)
    )
    query_back, query_gain_grad = norm_back(
        query_raw, query_gain, apply_rotary(query_rot_grad, position, -1.0)
    )
    attn_in_grads = jnp.concatenate(
        [
            query_back.reshape(row_slots, query_width).astype(jnp.bfloat16),
            key_back[:, 0].astype(jnp.bfloat16),
            value_grad,
            gate_logit_grad,
        ],
        axis=1,
    )
    normed_one_grad = scatter_product(attn_in_grads, attn_weights, dot_nt)
    grad_w_query, grad_w_key, grad_w_value, grad_w_out_gate = return_grads(
        first_normed, attn_in_grads, (query_width, HEAD_SIZE, HEAD_SIZE, query_width)
    )
    back_one, gain_one_grad = norm_back(inputs, gain_one, normed_one_grad)
    input_grad = swap_ranks((hidden_total_grad + back_one).astype(jnp.bfloat16))
    model_width = layer_input.shape[1]
    gains = all_sum(
        jnp.concatenate([gain_one_grad, gain_two_grad, query_gain_grad, key_gain_grad])[None]
    )[0]
    ends = (model_width, 2 * model_width, 2 * model_width + HEAD_SIZE)
    return (
        layer_output,
        input_grad,
        gains[: ends[0]],
        gains[ends[1] : ends[2]],
        gains[ends[2] :],
        grad_w_query,
        grad_w_key,
        grad_w_value,
        grad_w_out_gate,
        grad_w_output,
        gains[ends[0] : ends[1]],
        grad_w_gate,
        grad_w_up,
        grad_w_down,
    )


def solution(mesh):
    sizes = dict(mesh.shape)
    plane = (sizes["fsdp"], sizes["ctx"], sizes["tp"]) == (4, 4, 2)
    return jax.shard_map(
        plane_body if plane else body,
        mesh=mesh,
        in_specs=(
            P(("fsdp", "ctx", "tp"), None),
            P(("fsdp", "ctx", "tp"), None),
            P("fsdp", None),
            P(),
            P(),
            P(),
            P("fsdp", "tp"),
            P("fsdp", "tp"),
            P("fsdp", "tp"),
            P("fsdp", "tp"),
            P(("tp", "fsdp"), None),
            P(),
            P("fsdp", "tp"),
            P("fsdp", "tp"),
            P(("tp", "fsdp"), None),
        ),
        out_specs=(
            P(("fsdp", "ctx", "tp"), None),
            P(("fsdp", "ctx", "tp"), None),
            P(),
            P(),
            P(),
            P("fsdp", "tp"),
            P("fsdp", "tp"),
            P("fsdp", "tp"),
            P("fsdp", "tp"),
            P(("tp", "fsdp"), None),
            P(),
            P("fsdp", "tp"),
            P("fsdp", "tp"),
            P(("tp", "fsdp"), None),
        ),
        check_vma=False,
    )
```

```python
import jax
import jax.numpy as jnp
from jax import lax
from jax.sharding import PartitionSpec as P

HEAD_SIZE = 128


EPSILON = 1e-06
ROPE_BASE = 1000000.0
NEG_FILL = -1e30


def as_sent(value):

    def short(part):
        return part.astype(jnp.bfloat16) if part.dtype == jnp.float32 else part

    return jax.tree.map(short, value)


def apply_rms_norm(values, gain_vec):
    return (
        values * lax.rsqrt(jnp.mean(values * values, axis=-1, keepdims=True) + EPSILON) * gain_vec
    )


def norm_back(values, gain_vec, grad_in):
    row_scale = lax.rsqrt(jnp.mean(values * values, axis=-1, keepdims=True) + EPSILON)
    unit_rows = values * row_scale
    scaled = grad_in * gain_vec
    back_rows = row_scale * (
        scaled - unit_rows * jnp.mean(scaled * unit_rows, axis=-1, keepdims=True)
    )
    gain_grad = jnp.sum((grad_in * unit_rows).reshape(-1, values.shape[-1]), axis=0)
    return (back_rows, gain_grad)


def apply_rotary(values, token_position, direction):
    half_size = values.shape[-1] // 2
    frequency = jnp.power(ROPE_BASE, -jnp.arange(half_size, dtype=jnp.float32) / half_size)
    angle = token_position.astype(jnp.float32)[:, None] * frequency[None, :]
    cosine = jnp.cos(angle)[:, None, :]
    sine = direction * jnp.sin(angle)[:, None, :]
    first_half = values[..., :half_size]
    second_half = values[..., half_size:]
    return jnp.concatenate(
        [first_half * cosine - second_half * sine, second_half * cosine + first_half * sine],
        axis=-1,
    )


def segment_of(slot_ids, lengths):
    first_len = lengths[0, 0]
    second_len = lengths[0, 1]
    return jnp.where(slot_ids < first_len, 0, jnp.where(slot_ids < first_len + second_len, 1, 2))


def position_of(slot_ids, segment, lengths):
    seg_begin = jnp.where(
        segment == 0, 0, jnp.where(segment == 1, lengths[0, 0], lengths[0, 0] + lengths[0, 1])
    )
    return slot_ids - seg_begin


def to_block(local_part):
    return lax.all_gather(local_part, "tp", axis=0, tiled=True)


def to_share(partial_rows):
    return lax.psum_scatter(
        partial_rows.astype(jnp.bfloat16), "tp", scatter_dimension=0, tiled=True
    ).astype(jnp.float32)


def fold_product(left_rows, weight_set):
    pieces = jax.tree.map(
        lambda a: lax.all_gather(a, "fsdp", axis=0, tiled=True), as_sent(weight_set)
    )
    return tuple(
        (
            jnp.dot(left_rows, weight_part, preferred_element_type=jnp.float32)
            for weight_part in pieces
        )
    )


def back_product(grad_rows, weight_set):
    pieces = jax.tree.map(
        lambda a: lax.all_gather(a, "fsdp", axis=0, tiled=True), as_sent(weight_set)
    )
    result = lax.dot_general(
        grad_rows[0], pieces[0], (((1,), (1,)), ((), ())), preferred_element_type=jnp.float32
    )
    for grad_part, weight_part in zip(grad_rows[1:], pieces[1:]):
        result = result + lax.dot_general(
            grad_part, weight_part, (((1,), (1,)), ((), ())), preferred_element_type=jnp.float32
        )
    return result


def weight_grads(left_rows, grad_rows):
    widths = [grad_part.shape[1] for grad_part in grad_rows]
    shared = lax.psum_scatter(
        jnp.concatenate(
            [
                lax.dot_general(
                    left_rows,
                    grad_part,
                    (((0,), (0,)), ((), ())),
                    preferred_element_type=jnp.float32,
                )
                for grad_part in grad_rows
            ],
            axis=1,
        ).astype(jnp.bfloat16),
        "fsdp",
        scatter_dimension=0,
        tiled=True,
    )
    summed = lax.psum(shared, "ctx").astype(jnp.float32)
    pieces = []
    offset = 0
    for column_width in widths:
        pieces.append(summed[:, offset : offset + column_width])
        offset = offset + column_width
    return tuple(pieces)


def body(
    layer_input,
    cotangent,
    lengths,
    attn_norm,
    query_norm_gain,
    k_norm,
    w_query,
    key_weight,
    value_weight,
    w_out_gate,
    w_output,
    ffn_norm,
    w_gate,
    w_up,
    w_down,
):
    local_rows = layer_input.shape[0]
    block_rows = local_rows * lax.axis_size("tp")
    query_heads = w_query.shape[1] // HEAD_SIZE
    kv_heads = key_weight.shape[1] // HEAD_SIZE
    groups = query_heads // kv_heads
    score_scale = HEAD_SIZE ** (-0.5)
    block_first = lax.axis_index("ctx") * block_rows
    own_slots = (
        block_first + lax.axis_index("tp") * local_rows + jnp.arange(local_rows, dtype=jnp.int32)
    )
    own_valid = (segment_of(own_slots, lengths) < 2).astype(jnp.float32)[:, None]
    query_slots = block_first + jnp.arange(block_rows, dtype=jnp.int32)
    query_segment = segment_of(query_slots, lengths)
    query_position = position_of(query_slots, query_segment, lengths)
    inputs = layer_input.astype(jnp.float32)
    gain_one = attn_norm.astype(jnp.float32)
    gain_two = ffn_norm.astype(jnp.float32)
    query_gain = query_norm_gain.astype(jnp.float32)
    key_gain = k_norm.astype(jnp.float32)
    first_normed = to_block(apply_rms_norm(inputs, gain_one).astype(jnp.bfloat16))
    query_rows, key_projected, value_proj, gate_logits = fold_product(
        first_normed, (w_query, key_weight, value_weight, w_out_gate)
    )
    query_heads_raw = query_rows.reshape(block_rows, query_heads, HEAD_SIZE)
    key_heads_raw = key_projected.reshape(block_rows, kv_heads, HEAD_SIZE)
    query_rotated = apply_rotary(
        apply_rms_norm(query_heads_raw, query_gain), query_position, 1.0
    ).astype(jnp.bfloat16)
    key_rot = apply_rotary(apply_rms_norm(key_heads_raw, key_gain), query_position, 1.0).astype(
        jnp.bfloat16
    )
    query_grouped = query_rotated.reshape(block_rows, kv_heads, groups, HEAD_SIZE)
    key_flat = key_rot.reshape(block_rows, kv_heads * HEAD_SIZE)
    value_reduced = value_proj.astype(jnp.bfloat16)

    def key_mask(piece_rows):
        key_slots = jnp.arange(piece_rows, dtype=jnp.int32)
        key_segment = segment_of(key_slots, lengths)
        return (query_segment[:, None] == key_segment[None, :]) & (
            key_slots[None, :] <= query_slots[:, None]
        )

    head_shape = (kv_heads, groups, block_rows)
    running_top = jnp.full(head_shape + (1,), NEG_FILL, jnp.float32)
    key_piece = lax.all_gather(key_flat, "ctx", axis=0, tiled=True)
    value_piece = lax.all_gather(value_reduced, "ctx", axis=0, tiled=True)
    piece_rows = key_piece.shape[0]
    allowed = key_mask(piece_rows)
    raw_scores = jnp.einsum(
        "qhgd,khd->hgqk",
        query_grouped,
        key_piece.reshape(piece_rows, kv_heads, HEAD_SIZE),
        preferred_element_type=jnp.float32,
    )
    scores = jnp.where(allowed, raw_scores * score_scale, NEG_FILL)
    new_top = jnp.maximum(running_top, jnp.max(scores, axis=-1, keepdims=True))
    weights = jnp.where(allowed, jnp.exp(scores - new_top), 0.0)
    running_total = jnp.sum(weights, axis=-1, keepdims=True)
    mixed_sum = jnp.einsum(
        "hgqk,khd->hgqd",
        weights.astype(jnp.bfloat16),
        value_piece.reshape(piece_rows, kv_heads, HEAD_SIZE),
        preferred_element_type=jnp.float32,
    )
    mixed_sum, running_top, running_total = (mixed_sum, new_top, running_total)
    log_total = running_top + jnp.log(running_total)
    attended = jnp.transpose(mixed_sum / running_total, (2, 0, 1, 3))
    attended_rows = attended.reshape(block_rows, query_heads * HEAD_SIZE)
    gate_sig = jax.nn.sigmoid(gate_logits)
    gated_mix = (attended_rows * gate_sig).astype(jnp.bfloat16)
    attn_share = to_share(fold_product(gated_mix, (w_output,))[0])
    hidden_in = inputs + own_valid * attn_share
    normed_two = to_block(apply_rms_norm(hidden_in, gain_two).astype(jnp.bfloat16))
    gate_pre, up_pre = fold_product(normed_two, (w_gate, w_up))
    gate_sigmoid = jax.nn.sigmoid(gate_pre)
    activated = gate_pre * gate_sigmoid
    hidden_act = (activated * up_pre).astype(jnp.bfloat16)
    ffn_share = to_share(fold_product(hidden_act, (w_down,))[0])
    layer_output = (hidden_in + own_valid * ffn_share).astype(jnp.bfloat16)
    out_grad = cotangent.astype(jnp.float32) * own_valid
    ffn_grad = to_block(out_grad.astype(jnp.bfloat16))
    hidden_grad = back_product((ffn_grad,), (w_down,))
    grad_w_down = weight_grads(hidden_act, (ffn_grad,))[0]
    gate_grad = (
        hidden_grad * up_pre * gate_sigmoid * (1.0 + gate_pre * (1.0 - gate_sigmoid))
    ).astype(jnp.bfloat16)
    up_grad = (hidden_grad * activated).astype(jnp.bfloat16)
    normed_two_grad = to_share(back_product((gate_grad, up_grad), (w_gate, w_up)))
    grad_w_gate, grad_w_up = weight_grads(normed_two, (gate_grad, up_grad))
    back_two, gain_two_grad = norm_back(hidden_in, gain_two, normed_two_grad)
    hidden_total_grad = out_grad + back_two
    attn_grad = to_block((own_valid * hidden_total_grad).astype(jnp.bfloat16))
    gated_grad = back_product((attn_grad,), (w_output,))
    grad_w_output = weight_grads(gated_mix, (attn_grad,))[0]
    mixed_grad = (gated_grad * gate_sig).astype(jnp.bfloat16)
    gate_logit_grad = (gated_grad * attended_rows * gate_sig * (1.0 - gate_sig)).astype(
        jnp.bfloat16
    )
    mixed_grad_heads = mixed_grad.reshape(block_rows, kv_heads, groups, HEAD_SIZE)
    delta_rows = jnp.transpose(
        jnp.sum(mixed_grad_heads.astype(jnp.float32) * attended, axis=-1), (1, 2, 0)
    )[..., None]
    key_piece = lax.all_gather(key_flat, "ctx", axis=0, tiled=True)
    value_piece = lax.all_gather(value_reduced, "ctx", axis=0, tiled=True)
    piece_rows = key_piece.shape[0]
    key_view = key_piece.reshape(piece_rows, kv_heads, HEAD_SIZE)
    value_view = value_piece.reshape(piece_rows, kv_heads, HEAD_SIZE)
    allowed = key_mask(piece_rows)
    raw_scores = jnp.einsum(
        "qhgd,khd->hgqk", query_grouped, key_view, preferred_element_type=jnp.float32
    )
    soft_vals = jnp.where(allowed, jnp.exp(raw_scores * score_scale - log_total), 0.0)
    prob_grad = jnp.einsum(
        "qhgd,khd->hgqk", mixed_grad_heads, value_view, preferred_element_type=jnp.float32
    )
    score_grad = (soft_vals * (prob_grad - delta_rows) * score_scale).astype(jnp.bfloat16)
    query_acc = jnp.einsum(
        "hgqk,khd->qhgd", score_grad, key_view, preferred_element_type=jnp.float32
    )
    key_part = jnp.einsum(
        "hgqk,qhgd->khd", score_grad, query_grouped, preferred_element_type=jnp.float32
    ).reshape(piece_rows, kv_heads * HEAD_SIZE)
    value_part = jnp.einsum(
        "hgqk,qhgd->khd",
        soft_vals.astype(jnp.bfloat16),
        mixed_grad_heads,
        preferred_element_type=jnp.float32,
    ).reshape(piece_rows, kv_heads * HEAD_SIZE)
    kv_acc = jnp.concatenate([key_part, value_part], axis=1)
    query_acc, kv_acc = (query_acc, kv_acc)
    kv_own = lax.psum_scatter(
        kv_acc.astype(jnp.bfloat16), "ctx", scatter_dimension=0, tiled=True
    ).astype(jnp.float32)
    key_rot_grad = kv_own[:, : kv_heads * HEAD_SIZE].reshape(block_rows, kv_heads, HEAD_SIZE)
    value_grad = kv_own[:, kv_heads * HEAD_SIZE :].astype(jnp.bfloat16)
    key_back, key_gain_grad = norm_back(
        key_heads_raw, key_gain, apply_rotary(key_rot_grad, query_position, -1.0)
    )
    query_back, query_gain_grad = norm_back(
        query_heads_raw,
        query_gain,
        apply_rotary(query_acc.reshape(block_rows, query_heads, HEAD_SIZE), query_position, -1.0),
    )
    query_grad = query_back.reshape(block_rows, query_heads * HEAD_SIZE).astype(jnp.bfloat16)
    key_grad = key_back.reshape(block_rows, kv_heads * HEAD_SIZE).astype(jnp.bfloat16)
    attn_in_grads = (query_grad, key_grad, value_grad, gate_logit_grad)
    normed_one_grad = to_share(
        back_product(attn_in_grads, (w_query, key_weight, value_weight, w_out_gate))
    )
    grad_w_query, grad_w_key, grad_w_value, grad_w_out_gate = weight_grads(
        first_normed, attn_in_grads
    )
    back_one, gain_one_grad = norm_back(inputs, gain_one, normed_one_grad)
    input_grad = (hidden_total_grad + back_one).astype(jnp.bfloat16)
    gain_totals = lax.psum(
        (gain_one_grad, query_gain_grad, key_gain_grad, gain_two_grad), ("fsdp", "ctx", "tp")
    )
    return (
        layer_output,
        input_grad,
        gain_totals[0],
        gain_totals[1],
        gain_totals[2],
        grad_w_query,
        grad_w_key,
        grad_w_value,
        grad_w_out_gate,
        grad_w_output,
        gain_totals[3],
        grad_w_gate,
        grad_w_up,
        grad_w_down,
    )


def xor_pairs(count, mask):
    return [(i, i ^ mask) for i in range(count)]


def swap_plane(value, fsdp_mask, tp_mask):
    fsdp_size, tp_size = lax.axis_size("fsdp"), lax.axis_size("tp")
    if tp_mask == 0:
        return lax.ppermute(value, "fsdp", xor_pairs(fsdp_size, fsdp_mask))
    if fsdp_mask == 0:
        return lax.ppermute(value, "tp", xor_pairs(tp_size, tp_mask))
    return lax.ppermute(
        value,
        ("fsdp", "tp"),
        xor_pairs(fsdp_size * tp_size, fsdp_mask * tp_size + tp_mask),
    )


def swap_ranks(value):
    size = lax.axis_size("fsdp")
    pairs = [(a * size + b, b * size + a) for a in range(size) for b in range(size)]
    return lax.ppermute(value, ("fsdp", "ctx"), pairs)


PIECES = ((0, 0), (0, 1), (2, 0), (2, 1))


def plane_pieces(own):
    return [own if masks == (0, 0) else swap_plane(own, *masks) for masks in PIECES]


def plane_gather(own, near=None):
    near = near or plane_pieces(own)
    far = [swap_plane(piece, 1, 0) for piece in near]
    return jnp.concatenate(near + far, axis=0)


def plane_gather_slow(own):
    pair = jnp.stack([own, swap_plane(own, 2, 0)])
    near = jnp.stack([pair, swap_plane(pair, 0, 1)], axis=1).reshape(-1, own.shape[1])
    return jnp.concatenate([near, swap_plane(near, 1, 0)], axis=0)


def plane_scatter(near_part, far_part):
    rows = near_part.shape[0] // 4
    half = near_part + swap_plane(far_part.astype(jnp.bfloat16), 1, 0).astype(jnp.float32)
    total = half[:rows]
    for place in range(1, 4):
        piece = half[place * rows : (place + 1) * rows].astype(jnp.bfloat16)
        total = total + swap_plane(piece, *PIECES[place]).astype(jnp.float32)
    return total


def dot_nn(a, b):
    return jnp.dot(a, b, preferred_element_type=jnp.float32)


def dot_nt(a, b):
    return lax.dot_general(a, b, (((1,), (1,)), ((), ())), preferred_element_type=jnp.float32)


def dot_tn(a, b):
    return lax.dot_general(a, b, (((0,), (0,)), ((), ())), preferred_element_type=jnp.float32)


def scatter_product(rows, weight, dot):
    half = rows.shape[0] // 2
    far_part = dot(rows[half:], weight)
    near_part = dot(rows[:half], weight)
    return plane_scatter(near_part, far_part)


INWARD, ACROSS, OUTWARD = [(0, 1), (3, 2)], [(1, 2), (2, 1)], [(1, 0), (2, 3)]


class CtxSums:
    def __init__(self):
        self.flight, self.done = [], {}

    def step(self, fresh, kept):
        old = self.flight.pop(0) if len(self.flight) > 1 else []
        names = [name for name, _ in fresh]
        low = [part.astype(jnp.bfloat16) for _, part in fresh]
        pairs = [entry[2:] for entry in old]
        pairs, low, kept = lax.optimization_barrier((pairs, low, kept))
        place = lax.axis_index("ctx")
        sent = []
        for (stage, name, _, _), (here, came) in zip(old, pairs):
            if stage == 2:
                inner = (place == 1) | (place == 2)
                self.done[name] = jnp.where(inner, here, came).astype(jnp.float32)
                continue
            both = (here.astype(jnp.float32) + came.astype(jnp.float32)).astype(jnp.bfloat16)
            moved = lax.ppermute(both, "ctx", OUTWARD if stage else ACROSS)
            sent.append((stage + 1, name, both, moved))
        for name, part in zip(names, low):
            sent.append((0, name, part, lax.ppermute(part, "ctx", INWARD)))
        self.flight.append(sent)
        return kept

    def drain(self, fresh):
        fresh = list(fresh)
        while fresh or any(self.flight):
            self.step(fresh[:1], ())
            fresh = fresh[1:]


def all_sum(value):
    for axis, mask in (("fsdp", 1), ("fsdp", 2), ("tp", 1), ("ctx", 1), ("ctx", 2)):
        value = value + lax.ppermute(value, axis, xor_pairs(lax.axis_size(axis), mask))
    return value


def after(value, *others):
    return lax.optimization_barrier((value, others))[0]


def weight_columns(weights, owner):
    parts = []
    for weight in weights:
        width = weight.shape[1] // lax.axis_size("fsdp")
        parts.append(lax.dynamic_slice_in_dim(weight, owner * width, width, 1))
    return jnp.concatenate(parts, axis=1)


def fetch_weights(weights):
    me, size = lax.axis_index("fsdp"), lax.axis_size("fsdp")
    side = lax.axis_index("ctx") % 2
    rows = weights[0].shape[0]
    half = rows // 2
    mine = [lax.dynamic_slice_in_dim(weight, side * half, half, 0) for weight in weights]
    came = [swap_plane(weight_columns(mine, me ^ mask), mask, 0) for mask in (2, 3)]
    own = weight_columns(weights, me)
    core = swap_plane(weight_columns(weights, me ^ 1), 1, 0)
    other = lax.ppermute(jnp.concatenate(came, axis=0), "ctx", xor_pairs(4, 1))
    whole = jnp.zeros((rows * size, own.shape[1]), own.dtype)
    for part, start in (
        (own, me * rows),
        (core, (me ^ 1) * rows),
        (came[0], (me ^ 2) * rows + side * half),
        (came[1], (me ^ 3) * rows + side * half),
        (other[:half], (me ^ 2) * rows + (1 - side) * half),
        (other[half:], (me ^ 3) * rows + (1 - side) * half),
    ):
        whole = lax.dynamic_update_slice_in_dim(whole, part, start, 0)
    return whole


def grad_part(left, right, mask):
    owner = lax.axis_index("fsdp") ^ mask
    rows = left.shape[1] // lax.axis_size("fsdp")
    columns = lax.dynamic_slice_in_dim(left, owner * rows, rows, 1)
    part = dot_tn(columns, right).astype(jnp.bfloat16)
    return swap_plane(part, mask, 0) if mask else part


def place_columns(parts, width):
    me, size = lax.axis_index("fsdp"), lax.axis_size("fsdp")
    whole = jnp.zeros((parts[0].shape[0], width * size), jnp.float32)
    for mask, part in enumerate(parts):
        whole = lax.dynamic_update_slice_in_dim(whole, part, (me ^ mask) * width, 1)
    return whole


def plane_body(
    layer_input,
    cotangent,
    lengths,
    attn_norm,
    query_norm_gain,
    k_norm,
    w_query,
    key_weight,
    value_weight,
    w_out_gate,
    w_output,
    ffn_norm,
    w_gate,
    w_up,
    w_down,
):
    fsdp_size, tp_size = lax.axis_size("fsdp"), lax.axis_size("tp")
    fsdp_at, tp_at = lax.axis_index("fsdp"), lax.axis_index("tp")
    local_rows = layer_input.shape[0]
    row_slots = local_rows * fsdp_size * tp_size
    query_heads = w_query.shape[1] // HEAD_SIZE // fsdp_size
    query_width = query_heads * HEAD_SIZE
    score_scale = HEAD_SIZE ** (-0.5)
    gain_one = attn_norm.astype(jnp.float32)
    gain_two = ffn_norm.astype(jnp.float32)
    query_gain = query_norm_gain.astype(jnp.float32)
    key_gain = k_norm.astype(jnp.float32)

    input_low = swap_ranks(layer_input)
    inputs = input_low.astype(jnp.float32)
    attn_weights = fetch_weights((w_query, key_weight, value_weight, w_out_gate))
    cot = swap_ranks(after(cotangent, input_low)).astype(jnp.float32)
    lengths = swap_ranks(lengths)

    def slots_of(fsdp_index, tp_index):
        return (fsdp_index * tp_size + tp_index) * local_rows + jnp.arange(
            local_rows, dtype=jnp.int32
        )

    own_slots = slots_of(fsdp_at, tp_at)
    own_valid = (segment_of(own_slots, lengths) < 2).astype(jnp.float32)[:, None]
    slots = jnp.concatenate(
        [
            slots_of(fsdp_at ^ fsdp_mask ^ core, tp_at ^ tp_mask)
            for core in (0, 1)
            for fsdp_mask, tp_mask in PIECES
        ]
    )
    segment = segment_of(slots, lengths)
    position = position_of(slots, segment, lengths)

    first_own = apply_rms_norm(inputs, gain_one).astype(jnp.bfloat16)
    first_near = plane_pieces(first_own)
    first_normed = plane_gather(first_own, first_near)
    out_grad = cot * own_valid
    w_gate, w_up = after((w_gate, w_up), first_near)
    ffn_weights = fetch_weights((w_gate, w_up))

    projected = dot_nn(first_normed, attn_weights)
    query_raw = projected[:, :query_width].reshape(row_slots, query_heads, HEAD_SIZE)
    key_raw = projected[:, query_width : query_width + HEAD_SIZE].reshape(row_slots, 1, HEAD_SIZE)
    value_low = projected[:, query_width + HEAD_SIZE : query_width + 2 * HEAD_SIZE].astype(
        jnp.bfloat16
    )
    gate_logits = projected[:, query_width + 2 * HEAD_SIZE :]
    query_rot = apply_rotary(apply_rms_norm(query_raw, query_gain), position, 1.0).astype(
        jnp.bfloat16
    )
    key_rot = apply_rotary(apply_rms_norm(key_raw, key_gain), position, 1.0).astype(jnp.bfloat16)[
        :, 0
    ]

    allowed = (segment[:, None] == segment[None, :]) & (slots[None, :] <= slots[:, None])
    ffn_grad = plane_gather_slow(after(out_grad.astype(jnp.bfloat16), projected))
    raw_scores = jnp.einsum("qgd,kd->gqk", query_rot, key_rot, preferred_element_type=jnp.float32)
    scores = jnp.where(allowed, raw_scores * score_scale, NEG_FILL)
    top = jnp.max(scores, axis=-1, keepdims=True)
    weights = jnp.where(allowed, jnp.exp(scores - top), 0.0)
    total = jnp.sum(weights, axis=-1, keepdims=True)
    mixed = jnp.einsum(
        "gqk,kd->gqd", weights.astype(jnp.bfloat16), value_low, preferred_element_type=jnp.float32
    )
    log_total = top + jnp.log(total)
    attended = jnp.transpose(mixed / total, (1, 0, 2))
    attended_rows = attended.reshape(row_slots, query_width)
    gate_sig = jax.nn.sigmoid(gate_logits)
    gated_mix = (attended_rows * gate_sig).astype(jnp.bfloat16)
    attn_share = scatter_product(gated_mix, w_output, dot_nn)
    hidden_in = inputs + own_valid * attn_share
    normed_two = plane_gather(apply_rms_norm(hidden_in, gain_two).astype(jnp.bfloat16))

    hidden_grad = dot_nt(ffn_grad, w_down)
    pre = dot_nn(normed_two, ffn_weights)
    hidden_width = w_down.shape[0]
    gate_pre, up_pre = pre[:, :hidden_width], pre[:, hidden_width:]
    gate_sigmoid = jax.nn.sigmoid(gate_pre)
    activated = gate_pre * gate_sigmoid
    hidden_act = (activated * up_pre).astype(jnp.bfloat16)
    gate_grad = (
        hidden_grad * up_pre * gate_sigmoid * (1.0 + gate_pre * (1.0 - gate_sigmoid))
    ).astype(jnp.bfloat16)
    up_grad = (hidden_grad * activated).astype(jnp.bfloat16)
    ffn_in_grads = jnp.concatenate([gate_grad, up_grad], axis=1)

    sums = CtxSums()
    down_part = dot_tn(hidden_act, ffn_grad).astype(jnp.bfloat16)
    down_parts = [("down", i) for i in range(4)]
    down_parts = list(zip(down_parts, jnp.split(down_part, 4, axis=0)))
    hidden_act, ffn_in_grads, normed_two = sums.step(
        down_parts[:1], (hidden_act, ffn_in_grads, normed_two)
    )
    half = row_slots // 2
    two_far = dot_nt(ffn_in_grads[half:], ffn_weights)
    two_near = dot_nt(ffn_in_grads[:half], ffn_weights)
    two_far, two_near, hidden_act, ffn_in_grads = sums.step(
        down_parts[1:2], (two_far.astype(jnp.bfloat16), two_near, hidden_act, ffn_in_grads)
    )
    normed_two_grad = plane_scatter(two_near, two_far)
    ffn_parts = {
        mask: grad_part(normed_two, ffn_in_grads, mask) for mask in (2, 3, 1, 0)
    }
    normed_two_grad, ffn_parts[0] = sums.step(
        down_parts[2:3], (normed_two_grad, ffn_parts[0])
    )
    back_two, gain_two_grad = norm_back(hidden_in, gain_two, normed_two_grad)
    hidden_total_grad = out_grad + back_two
    attn_near = plane_pieces((own_valid * hidden_total_grad).astype(jnp.bfloat16))
    out_far = dot_nn(hidden_act[half:], w_down)
    out_near = dot_nn(hidden_act[:half], w_down)
    attn_near, out_far, out_near, ffn_parts[1] = sums.step(
        down_parts[3:], (attn_near, out_far.astype(jnp.bfloat16), out_near, ffn_parts[1])
    )
    ffn_chunks = []
    for mask in range(4):
        for i, part in enumerate(jnp.split(ffn_parts[mask], 2, axis=1)):
            ffn_chunks.append((("ffn", mask, i), part))
    attn_grad = plane_gather(attn_near[0], attn_near)
    gated_grad = dot_nt(attn_grad, w_output)
    output_part = dot_tn(gated_mix, attn_grad).astype(jnp.bfloat16)
    mixed_grad = (gated_grad * gate_sig).astype(jnp.bfloat16)
    gate_logit_grad = (gated_grad * attended_rows * gate_sig * (1.0 - gate_sig)).astype(
        jnp.bfloat16
    )
    mixed_grad, gate_logit_grad, output_part = sums.step(
        ffn_chunks[:1], (mixed_grad, gate_logit_grad, output_part)
    )
    mixed_grad_heads = mixed_grad.reshape(row_slots, query_heads, HEAD_SIZE)
    delta_rows = jnp.transpose(
        jnp.sum(mixed_grad_heads.astype(jnp.float32) * attended, axis=-1), (1, 0)
    )[..., None]
    raw_again = jnp.einsum("qgd,kd->gqk", query_rot, key_rot, preferred_element_type=jnp.float32)
    soft = jnp.where(allowed, jnp.exp(raw_again * score_scale - log_total), 0.0)
    prob_grad = jnp.einsum(
        "qgd,kd->gqk", mixed_grad_heads, value_low, preferred_element_type=jnp.float32
    )
    score_grad = (soft * (prob_grad - delta_rows) * score_scale).astype(jnp.bfloat16)
    query_rot_grad = jnp.einsum(
        "gqk,kd->qgd", score_grad, key_rot, preferred_element_type=jnp.float32
    )
    key_rot_grad = jnp.einsum(
        "gqk,qgd->kd", score_grad, query_rot, preferred_element_type=jnp.float32
    )
    value_grad = jnp.einsum(
        "gqk,qgd->kd",
        soft.astype(jnp.bfloat16),
        mixed_grad_heads,
        preferred_element_type=jnp.float32,
    ).astype(jnp.bfloat16)
    query_rot_grad, key_rot_grad, value_grad = sums.step(
        ffn_chunks[1:2], (query_rot_grad, key_rot_grad, value_grad)
    )
    key_back, key_gain_grad = norm_back(
        key_raw, key_gain, apply_rotary(key_rot_grad[:, None], position, -1.0)
    )
    query_back, query_gain_grad = norm_back(
        query_raw, query_gain, apply_rotary(query_rot_grad, position, -1.0)
    )
    attn_in_grads = jnp.concatenate(
        [
            query_back.reshape(row_slots, query_width).astype(jnp.bfloat16),
            key_back[:, 0].astype(jnp.bfloat16),
            value_grad,
            gate_logit_grad,
        ],
        axis=1,
    )
    one_far = dot_nt(attn_in_grads[half:], attn_weights)
    one_near = dot_nt(attn_in_grads[:half], attn_weights)
    one_far, one_near, attn_in_grads = sums.step(
        ffn_chunks[2:3], (one_far.astype(jnp.bfloat16), one_near, attn_in_grads)
    )
    normed_one_grad = plane_scatter(one_near, one_far)
    attn_parts = {mask: grad_part(first_normed, attn_in_grads, mask) for mask in (2, 3, 1, 0)}
    normed_one_grad, attn_parts[0] = sums.step(
        ffn_chunks[3:4], (normed_one_grad, attn_parts[0])
    )
    back_one, gain_one_grad = norm_back(inputs, gain_one, normed_one_grad)
    input_grad = swap_ranks((hidden_total_grad + back_one).astype(jnp.bfloat16))
    ffn_share = plane_scatter(out_near, out_far)
    layer_output = swap_ranks((hidden_in + own_valid * ffn_share).astype(jnp.bfloat16))
    gains = jnp.concatenate([gain_one_grad, gain_two_grad, query_gain_grad, key_gain_grad])[None]
    gains = all_sum(gains)[0]
    gains, input_grad, layer_output = sums.step(
        ffn_chunks[4:5], (gains, input_grad, layer_output)
    )
    attn_chunks = [(("attn", mask), attn_parts[mask]) for mask in range(4)]
    sums.drain(ffn_chunks[5:] + [("output", output_part)] + attn_chunks)

    grad_w_down = jnp.concatenate([sums.done["down", i] for i in range(4)], axis=0)
    grad_w_output = sums.done["output"]
    grad_w_gate, grad_w_up = (
        place_columns([sums.done["ffn", mask, i] for mask in range(4)], hidden_width)
        for i in range(2)
    )
    ends = [0, query_width, query_width + HEAD_SIZE, query_width + 2 * HEAD_SIZE]
    widths = (query_width, HEAD_SIZE, HEAD_SIZE, query_width)
    grad_w_query, grad_w_key, grad_w_value, grad_w_out_gate = (
        place_columns(
            [sums.done["attn", mask][:, start : start + width] for mask in range(4)], width
        )
        for start, width in zip(ends, widths)
    )
    model_width = layer_input.shape[1]
    ends = (model_width, 2 * model_width, 2 * model_width + HEAD_SIZE)
    return (
        layer_output,
        input_grad,
        gains[: ends[0]],
        gains[ends[1] : ends[2]],
        gains[ends[2] :],
        grad_w_query,
        grad_w_key,
        grad_w_value,
        grad_w_out_gate,
        grad_w_output,
        gains[ends[0] : ends[1]],
        grad_w_gate,
        grad_w_up,
        grad_w_down,
    )


def solution(mesh):
    sizes = dict(mesh.shape)
    plane = (sizes["fsdp"], sizes["ctx"], sizes["tp"]) == (4, 4, 2)
    return jax.shard_map(
        plane_body if plane else body,
        mesh=mesh,
        in_specs=(
            P(("fsdp", "ctx", "tp"), None),
            P(("fsdp", "ctx", "tp"), None),
            P("fsdp", None),
            P(),
            P(),
            P(),
            P("fsdp", "tp"),
            P("fsdp", "tp"),
            P("fsdp", "tp"),
            P("fsdp", "tp"),
            P(("tp", "fsdp"), None),
            P(),
            P("fsdp", "tp"),
            P("fsdp", "tp"),
            P(("tp", "fsdp"), None),
        ),
        out_specs=(
            P(("fsdp", "ctx", "tp"), None),
            P(("fsdp", "ctx", "tp"), None),
            P(),
            P(),
            P(),
            P("fsdp", "tp"),
            P("fsdp", "tp"),
            P("fsdp", "tp"),
            P("fsdp", "tp"),
            P(("tp", "fsdp"), None),
            P(),
            P("fsdp", "tp"),
            P("fsdp", "tp"),
            P(("tp", "fsdp"), None),
        ),
        check_vma=False,
    )
```

```python
import jax
import jax.numpy as jnp
from jax import lax
from jax.sharding import PartitionSpec as P

HEAD_SIZE = 128


EPSILON = 1e-06
ROPE_BASE = 1000000.0
NEG_FILL = -1e30


def as_sent(value):

    def short(part):
        return part.astype(jnp.bfloat16) if part.dtype == jnp.float32 else part

    return jax.tree.map(short, value)


def apply_rms_norm(values, gain_vec):
    return (
        values * lax.rsqrt(jnp.mean(values * values, axis=-1, keepdims=True) + EPSILON) * gain_vec
    )


def norm_back(values, gain_vec, grad_in):
    row_scale = lax.rsqrt(jnp.mean(values * values, axis=-1, keepdims=True) + EPSILON)
    unit_rows = values * row_scale
    scaled = grad_in * gain_vec
    back_rows = row_scale * (
        scaled - unit_rows * jnp.mean(scaled * unit_rows, axis=-1, keepdims=True)
    )
    gain_grad = jnp.sum((grad_in * unit_rows).reshape(-1, values.shape[-1]), axis=0)
    return (back_rows, gain_grad)


def apply_rotary(values, token_position, direction):
    half_size = values.shape[-1] // 2
    frequency = jnp.power(ROPE_BASE, -jnp.arange(half_size, dtype=jnp.float32) / half_size)
    angle = token_position.astype(jnp.float32)[:, None] * frequency[None, :]
    cosine = jnp.cos(angle)[:, None, :]
    sine = direction * jnp.sin(angle)[:, None, :]
    first_half = values[..., :half_size]
    second_half = values[..., half_size:]
    return jnp.concatenate(
        [first_half * cosine - second_half * sine, second_half * cosine + first_half * sine],
        axis=-1,
    )


def segment_of(slot_ids, lengths):
    first_len = lengths[0, 0]
    second_len = lengths[0, 1]
    return jnp.where(slot_ids < first_len, 0, jnp.where(slot_ids < first_len + second_len, 1, 2))


def position_of(slot_ids, segment, lengths):
    seg_begin = jnp.where(
        segment == 0, 0, jnp.where(segment == 1, lengths[0, 0], lengths[0, 0] + lengths[0, 1])
    )
    return slot_ids - seg_begin


def to_block(local_part):
    return lax.all_gather(local_part, "tp", axis=0, tiled=True)


def to_share(partial_rows):
    return lax.psum_scatter(
        partial_rows.astype(jnp.bfloat16), "tp", scatter_dimension=0, tiled=True
    ).astype(jnp.float32)


def fold_product(left_rows, weight_set):
    pieces = jax.tree.map(
        lambda a: lax.all_gather(a, "fsdp", axis=0, tiled=True), as_sent(weight_set)
    )
    return tuple(
        (
            jnp.dot(left_rows, weight_part, preferred_element_type=jnp.float32)
            for weight_part in pieces
        )
    )


def back_product(grad_rows, weight_set):
    pieces = jax.tree.map(
        lambda a: lax.all_gather(a, "fsdp", axis=0, tiled=True), as_sent(weight_set)
    )
    result = lax.dot_general(
        grad_rows[0], pieces[0], (((1,), (1,)), ((), ())), preferred_element_type=jnp.float32
    )
    for grad_part, weight_part in zip(grad_rows[1:], pieces[1:]):
        result = result + lax.dot_general(
            grad_part, weight_part, (((1,), (1,)), ((), ())), preferred_element_type=jnp.float32
        )
    return result


def weight_grads(left_rows, grad_rows):
    widths = [grad_part.shape[1] for grad_part in grad_rows]
    shared = lax.psum_scatter(
        jnp.concatenate(
            [
                lax.dot_general(
                    left_rows,
                    grad_part,
                    (((0,), (0,)), ((), ())),
                    preferred_element_type=jnp.float32,
                )
                for grad_part in grad_rows
            ],
            axis=1,
        ).astype(jnp.bfloat16),
        "fsdp",
        scatter_dimension=0,
        tiled=True,
    )
    summed = lax.psum(shared, "ctx").astype(jnp.float32)
    pieces = []
    offset = 0
    for column_width in widths:
        pieces.append(summed[:, offset : offset + column_width])
        offset = offset + column_width
    return tuple(pieces)


def body(
    layer_input,
    cotangent,
    lengths,
    attn_norm,
    query_norm_gain,
    k_norm,
    w_query,
    key_weight,
    value_weight,
    w_out_gate,
    w_output,
    ffn_norm,
    w_gate,
    w_up,
    w_down,
):
    local_rows = layer_input.shape[0]
    block_rows = local_rows * lax.axis_size("tp")
    query_heads = w_query.shape[1] // HEAD_SIZE
    kv_heads = key_weight.shape[1] // HEAD_SIZE
    groups = query_heads // kv_heads
    score_scale = HEAD_SIZE ** (-0.5)
    block_first = lax.axis_index("ctx") * block_rows
    own_slots = (
        block_first + lax.axis_index("tp") * local_rows + jnp.arange(local_rows, dtype=jnp.int32)
    )
    own_valid = (segment_of(own_slots, lengths) < 2).astype(jnp.float32)[:, None]
    query_slots = block_first + jnp.arange(block_rows, dtype=jnp.int32)
    query_segment = segment_of(query_slots, lengths)
    query_position = position_of(query_slots, query_segment, lengths)
    inputs = layer_input.astype(jnp.float32)
    gain_one = attn_norm.astype(jnp.float32)
    gain_two = ffn_norm.astype(jnp.float32)
    query_gain = query_norm_gain.astype(jnp.float32)
    key_gain = k_norm.astype(jnp.float32)
    first_normed = to_block(apply_rms_norm(inputs, gain_one).astype(jnp.bfloat16))
    query_rows, key_projected, value_proj, gate_logits = fold_product(
        first_normed, (w_query, key_weight, value_weight, w_out_gate)
    )
    query_heads_raw = query_rows.reshape(block_rows, query_heads, HEAD_SIZE)
    key_heads_raw = key_projected.reshape(block_rows, kv_heads, HEAD_SIZE)
    query_rotated = apply_rotary(
        apply_rms_norm(query_heads_raw, query_gain), query_position, 1.0
    ).astype(jnp.bfloat16)
    key_rot = apply_rotary(apply_rms_norm(key_heads_raw, key_gain), query_position, 1.0).astype(
        jnp.bfloat16
    )
    query_grouped = query_rotated.reshape(block_rows, kv_heads, groups, HEAD_SIZE)
    key_flat = key_rot.reshape(block_rows, kv_heads * HEAD_SIZE)
    value_reduced = value_proj.astype(jnp.bfloat16)

    def key_mask(piece_rows):
        key_slots = jnp.arange(piece_rows, dtype=jnp.int32)
        key_segment = segment_of(key_slots, lengths)
        return (query_segment[:, None] == key_segment[None, :]) & (
            key_slots[None, :] <= query_slots[:, None]
        )

    head_shape = (kv_heads, groups, block_rows)
    running_top = jnp.full(head_shape + (1,), NEG_FILL, jnp.float32)
    key_piece = lax.all_gather(key_flat, "ctx", axis=0, tiled=True)
    value_piece = lax.all_gather(value_reduced, "ctx", axis=0, tiled=True)
    piece_rows = key_piece.shape[0]
    allowed = key_mask(piece_rows)
    raw_scores = jnp.einsum(
        "qhgd,khd->hgqk",
        query_grouped,
        key_piece.reshape(piece_rows, kv_heads, HEAD_SIZE),
        preferred_element_type=jnp.float32,
    )
    scores = jnp.where(allowed, raw_scores * score_scale, NEG_FILL)
    new_top = jnp.maximum(running_top, jnp.max(scores, axis=-1, keepdims=True))
    weights = jnp.where(allowed, jnp.exp(scores - new_top), 0.0)
    running_total = jnp.sum(weights, axis=-1, keepdims=True)
    mixed_sum = jnp.einsum(
        "hgqk,khd->hgqd",
        weights.astype(jnp.bfloat16),
        value_piece.reshape(piece_rows, kv_heads, HEAD_SIZE),
        preferred_element_type=jnp.float32,
    )
    mixed_sum, running_top, running_total = (mixed_sum, new_top, running_total)
    log_total = running_top + jnp.log(running_total)
    attended = jnp.transpose(mixed_sum / running_total, (2, 0, 1, 3))
    attended_rows = attended.reshape(block_rows, query_heads * HEAD_SIZE)
    gate_sig = jax.nn.sigmoid(gate_logits)
    gated_mix = (attended_rows * gate_sig).astype(jnp.bfloat16)
    attn_share = to_share(fold_product(gated_mix, (w_output,))[0])
    hidden_in = inputs + own_valid * attn_share
    normed_two = to_block(apply_rms_norm(hidden_in, gain_two).astype(jnp.bfloat16))
    gate_pre, up_pre = fold_product(normed_two, (w_gate, w_up))
    gate_sigmoid = jax.nn.sigmoid(gate_pre)
    activated = gate_pre * gate_sigmoid
    hidden_act = (activated * up_pre).astype(jnp.bfloat16)
    ffn_share = to_share(fold_product(hidden_act, (w_down,))[0])
    layer_output = (hidden_in + own_valid * ffn_share).astype(jnp.bfloat16)
    out_grad = cotangent.astype(jnp.float32) * own_valid
    ffn_grad = to_block(out_grad.astype(jnp.bfloat16))
    hidden_grad = back_product((ffn_grad,), (w_down,))
    grad_w_down = weight_grads(hidden_act, (ffn_grad,))[0]
    gate_grad = (
        hidden_grad * up_pre * gate_sigmoid * (1.0 + gate_pre * (1.0 - gate_sigmoid))
    ).astype(jnp.bfloat16)
    up_grad = (hidden_grad * activated).astype(jnp.bfloat16)
    normed_two_grad = to_share(back_product((gate_grad, up_grad), (w_gate, w_up)))
    grad_w_gate, grad_w_up = weight_grads(normed_two, (gate_grad, up_grad))
    back_two, gain_two_grad = norm_back(hidden_in, gain_two, normed_two_grad)
    hidden_total_grad = out_grad + back_two
    attn_grad = to_block((own_valid * hidden_total_grad).astype(jnp.bfloat16))
    gated_grad = back_product((attn_grad,), (w_output,))
    grad_w_output = weight_grads(gated_mix, (attn_grad,))[0]
    mixed_grad = (gated_grad * gate_sig).astype(jnp.bfloat16)
    gate_logit_grad = (gated_grad * attended_rows * gate_sig * (1.0 - gate_sig)).astype(
        jnp.bfloat16
    )
    mixed_grad_heads = mixed_grad.reshape(block_rows, kv_heads, groups, HEAD_SIZE)
    delta_rows = jnp.transpose(
        jnp.sum(mixed_grad_heads.astype(jnp.float32) * attended, axis=-1), (1, 2, 0)
    )[..., None]
    key_piece = lax.all_gather(key_flat, "ctx", axis=0, tiled=True)
    value_piece = lax.all_gather(value_reduced, "ctx", axis=0, tiled=True)
    piece_rows = key_piece.shape[0]
    key_view = key_piece.reshape(piece_rows, kv_heads, HEAD_SIZE)
    value_view = value_piece.reshape(piece_rows, kv_heads, HEAD_SIZE)
    allowed = key_mask(piece_rows)
    raw_scores = jnp.einsum(
        "qhgd,khd->hgqk", query_grouped, key_view, preferred_element_type=jnp.float32
    )
    soft_vals = jnp.where(allowed, jnp.exp(raw_scores * score_scale - log_total), 0.0)
    prob_grad = jnp.einsum(
        "qhgd,khd->hgqk", mixed_grad_heads, value_view, preferred_element_type=jnp.float32
    )
    score_grad = (soft_vals * (prob_grad - delta_rows) * score_scale).astype(jnp.bfloat16)
    query_acc = jnp.einsum(
        "hgqk,khd->qhgd", score_grad, key_view, preferred_element_type=jnp.float32
    )
    key_part = jnp.einsum(
        "hgqk,qhgd->khd", score_grad, query_grouped, preferred_element_type=jnp.float32
    ).reshape(piece_rows, kv_heads * HEAD_SIZE)
    value_part = jnp.einsum(
        "hgqk,qhgd->khd",
        soft_vals.astype(jnp.bfloat16),
        mixed_grad_heads,
        preferred_element_type=jnp.float32,
    ).reshape(piece_rows, kv_heads * HEAD_SIZE)
    kv_acc = jnp.concatenate([key_part, value_part], axis=1)
    query_acc, kv_acc = (query_acc, kv_acc)
    kv_own = lax.psum_scatter(
        kv_acc.astype(jnp.bfloat16), "ctx", scatter_dimension=0, tiled=True
    ).astype(jnp.float32)
    key_rot_grad = kv_own[:, : kv_heads * HEAD_SIZE].reshape(block_rows, kv_heads, HEAD_SIZE)
    value_grad = kv_own[:, kv_heads * HEAD_SIZE :].astype(jnp.bfloat16)
    key_back, key_gain_grad = norm_back(
        key_heads_raw, key_gain, apply_rotary(key_rot_grad, query_position, -1.0)
    )
    query_back, query_gain_grad = norm_back(
        query_heads_raw,
        query_gain,
        apply_rotary(query_acc.reshape(block_rows, query_heads, HEAD_SIZE), query_position, -1.0),
    )
    query_grad = query_back.reshape(block_rows, query_heads * HEAD_SIZE).astype(jnp.bfloat16)
    key_grad = key_back.reshape(block_rows, kv_heads * HEAD_SIZE).astype(jnp.bfloat16)
    attn_in_grads = (query_grad, key_grad, value_grad, gate_logit_grad)
    normed_one_grad = to_share(
        back_product(attn_in_grads, (w_query, key_weight, value_weight, w_out_gate))
    )
    grad_w_query, grad_w_key, grad_w_value, grad_w_out_gate = weight_grads(
        first_normed, attn_in_grads
    )
    back_one, gain_one_grad = norm_back(inputs, gain_one, normed_one_grad)
    input_grad = (hidden_total_grad + back_one).astype(jnp.bfloat16)
    gain_totals = lax.psum(
        (gain_one_grad, query_gain_grad, key_gain_grad, gain_two_grad), ("fsdp", "ctx", "tp")
    )
    return (
        layer_output,
        input_grad,
        gain_totals[0],
        gain_totals[1],
        gain_totals[2],
        grad_w_query,
        grad_w_key,
        grad_w_value,
        grad_w_out_gate,
        grad_w_output,
        gain_totals[3],
        grad_w_gate,
        grad_w_up,
        grad_w_down,
    )


def xor_pairs(count, mask):
    return [(i, i ^ mask) for i in range(count)]


def swap_plane(value, fsdp_mask, tp_mask):
    fsdp_size, tp_size = lax.axis_size("fsdp"), lax.axis_size("tp")
    if tp_mask == 0:
        return lax.ppermute(value, "fsdp", xor_pairs(fsdp_size, fsdp_mask))
    if fsdp_mask == 0:
        return lax.ppermute(value, "tp", xor_pairs(tp_size, tp_mask))
    return lax.ppermute(
        value,
        ("fsdp", "tp"),
        xor_pairs(fsdp_size * tp_size, fsdp_mask * tp_size + tp_mask),
    )


def swap_ranks(value):
    size = lax.axis_size("fsdp")
    pairs = [(a * size + b, b * size + a) for a in range(size) for b in range(size)]
    return lax.ppermute(value, ("fsdp", "ctx"), pairs)


PIECES = ((0, 0), (0, 1), (2, 0), (2, 1))


def plane_near(own):
    rows = own.shape[0] // 2
    over_tp, over_x = swap_plane(own, 0, 1), swap_plane(own, 2, 0)
    three = jnp.concatenate([own, over_tp, over_x], axis=0)
    corner = [swap_plane(over_x[:rows], 0, 1), swap_plane(over_tp[rows:], 2, 0)]
    return three, swap_plane(three, 1, 0), jnp.concatenate(corner, axis=0)


def plane_join(near):
    three, three_far, corner = near
    return jnp.concatenate([three, corner, three_far, swap_plane(corner, 1, 0)], axis=0)


def scatter_half(near_part, far_part):
    return near_part + swap_plane(far_part.astype(jnp.bfloat16), 1, 0).astype(jnp.float32)


def scatter_plane(half):
    rows = half.shape[0] // 8
    piece = [half[at * rows : (at + 1) * rows] for at in range(8)]

    def sent(parts, *masks):
        low = jnp.concatenate(parts, axis=0).astype(jnp.bfloat16)
        return swap_plane(low, *masks).astype(jnp.float32)

    by_x = sent([piece[4], piece[6]], 2, 0)
    by_tp = sent([piece[3], piece[7]], 0, 1)
    top = sent([piece[2] + by_x[rows:]], 0, 1)
    bottom = sent([piece[5] + by_tp[rows:]], 2, 0)
    return jnp.concatenate([piece[0] + by_x[:rows], piece[1] + by_tp[:rows]], axis=0), [
        top.astype(jnp.bfloat16),
        bottom.astype(jnp.bfloat16),
    ]


def scatter_total(own, came):
    return own + jnp.concatenate(came, axis=0).astype(jnp.float32)


def dot_nn(a, b):
    return jnp.dot(a, b, preferred_element_type=jnp.float32)


def dot_nt(a, b):
    return lax.dot_general(a, b, (((1,), (1,)), ((), ())), preferred_element_type=jnp.float32)


def dot_tn(a, b):
    return lax.dot_general(a, b, (((0,), (0,)), ((), ())), preferred_element_type=jnp.float32)


INWARD, ACROSS, OUTWARD = [(0, 1), (3, 2)], [(1, 2), (2, 1)], [(1, 0), (2, 3)]


class CtxSums:
    def __init__(self):
        self.flight, self.arrived, self.done = [], [], {}

    def send(self, *fresh):
        place = lax.axis_index("ctx")
        inner = (place == 1) | (place == 2)
        sent, totals, fresh = [], [], list(fresh)
        for stage, name, here, came in self.arrived:
            if stage == 2:
                self.done[name] = jnp.where(inner, here, came).astype(jnp.float32)
                continue
            both = (here.astype(jnp.float32) + came.astype(jnp.float32)).astype(jnp.bfloat16)
            if stage:
                totals.append((name, both))
            else:
                sent.append(([(1, name, both)], lax.ppermute(both, "ctx", ACROSS)))
        while totals and fresh and totals[0][1].shape == fresh[0][1].shape:
            (out, total), (name, part) = totals.pop(0), fresh.pop(0)
            moved = swap_ctx(jnp.where(inner, total, part))
            sent.append(([(0, name, part), (2, out, total)], moved))
        for name, part in fresh:
            sent.append(([(0, name, part)], lax.ppermute(part, "ctx", INWARD)))
        for name, total in totals:
            sent.append(([(2, name, total)], lax.ppermute(total, "ctx", OUTWARD)))
        self.arrived = []
        self.flight.append(sent)

    def wait(self, kept, depth=1):
        old = []
        while len(self.flight) >= depth:
            old += self.flight.pop(0)
        heres = [[here for _, _, here in entry[0]] for entry in old]
        moved = [entry[1] for entry in old]
        heres, moved, kept = lax.optimization_barrier((heres, moved, kept))
        self.arrived = [
            (stage, name, here, came)
            for entry, parts, came in zip(old, heres, moved)
            for (stage, name, _), here in zip(entry[0], parts)
        ]
        return kept


def sum_hops():
    for axis, mask in (("fsdp", 1), ("fsdp", 2), ("tp", 1), ("ctx", 1), ("ctx", 2)):
        yield axis, xor_pairs(lax.axis_size(axis), mask)


def weight_columns(weights, owner):
    parts = []
    for weight in weights:
        width = weight.shape[1] // lax.axis_size("fsdp")
        parts.append(lax.dynamic_slice_in_dim(weight, owner * width, width, 1))
    return jnp.concatenate(parts, axis=1)


class Fetch:
    def __init__(self, weights):
        self.me, self.size = lax.axis_index("fsdp"), lax.axis_size("fsdp")
        self.side = lax.axis_index("ctx") % 2
        self.rows = weights[0].shape[0]
        self.half = self.rows // 2
        mine = [
            lax.dynamic_slice_in_dim(weight, self.side * self.half, self.half, 0)
            for weight in weights
        ]
        self.columns = [weight_columns(mine, self.me ^ mask) for mask in (2, 3)]
        self.own = weight_columns(weights, self.me)
        self.core = weight_columns(weights, self.me ^ 1)

    def along_x(self, at):
        return swap_plane(self.columns[at], (2, 3)[at], 0)

    def along_core(self):
        return swap_plane(self.core, 1, 0)

    def begin(self, core):
        whole = jnp.zeros((self.rows * self.size, self.own.shape[1]), self.own.dtype)
        for part, peer in ((self.own, self.me), (core, self.me ^ 1)):
            whole = lax.dynamic_update_slice_in_dim(whole, part, peer * self.rows, 0)
        return whole

    def add(self, whole, at, came, other):
        start = (self.me ^ (2, 3)[at]) * self.rows
        whole = lax.dynamic_update_slice_in_dim(whole, came, start + self.side * self.half, 0)
        return lax.dynamic_update_slice_in_dim(
            whole, other, start + (1 - self.side) * self.half, 0
        )


def swap_ctx(value):
    return lax.ppermute(value, "ctx", xor_pairs(lax.axis_size("ctx"), 1))


def grad_part(left, right, mask):
    owner = lax.axis_index("fsdp") ^ mask
    rows = left.shape[1] // lax.axis_size("fsdp")
    columns = lax.dynamic_slice_in_dim(left, owner * rows, rows, 1)
    return dot_tn(columns, right).astype(jnp.bfloat16)


def place_columns(parts, width):
    me, size = lax.axis_index("fsdp"), lax.axis_size("fsdp")
    whole = jnp.zeros((parts[0].shape[0], width * size), jnp.float32)
    for mask, part in enumerate(parts):
        whole = lax.dynamic_update_slice_in_dim(whole, part, (me ^ mask) * width, 1)
    return whole


def plane_body(
    layer_input,
    cotangent,
    lengths,
    attn_norm,
    query_norm_gain,
    k_norm,
    w_query,
    key_weight,
    value_weight,
    w_out_gate,
    w_output,
    ffn_norm,
    w_gate,
    w_up,
    w_down,
):
    fsdp_size, tp_size = lax.axis_size("fsdp"), lax.axis_size("tp")
    fsdp_at, tp_at = lax.axis_index("fsdp"), lax.axis_index("tp")
    local_rows = layer_input.shape[0]
    row_slots = local_rows * fsdp_size * tp_size
    query_heads = w_query.shape[1] // HEAD_SIZE // fsdp_size
    query_width = query_heads * HEAD_SIZE
    score_scale = HEAD_SIZE ** (-0.5)
    gain_one = attn_norm.astype(jnp.float32)
    gain_two = ffn_norm.astype(jnp.float32)
    query_gain = query_norm_gain.astype(jnp.float32)
    key_gain = k_norm.astype(jnp.float32)

    together = lax.optimization_barrier
    input_low = swap_ranks(layer_input)
    attn_fetch = Fetch((w_query, key_weight, value_weight, w_out_gate))
    attn_came = [attn_fetch.along_x(at) for at in range(2)]
    attn_core = attn_fetch.along_core()
    ffn_fetch = Fetch((w_gate, w_up))
    cot_low = swap_ranks(cotangent)
    lengths = swap_ranks(lengths)
    input_low, attn_came, ffn_fetch.columns[0] = together(
        (input_low, attn_came, ffn_fetch.columns[0])
    )
    inputs = input_low.astype(jnp.float32)

    def slots_of(fsdp_index, tp_index):
        return (fsdp_index * tp_size + tp_index) * local_rows + jnp.arange(
            local_rows, dtype=jnp.int32
        )

    own_slots = slots_of(fsdp_at, tp_at)
    own_valid = (segment_of(own_slots, lengths) < 2).astype(jnp.float32)[:, None]
    slots = jnp.concatenate(
        [
            slots_of(fsdp_at ^ fsdp_mask ^ core, tp_at ^ tp_mask)
            for core in (0, 1)
            for fsdp_mask, tp_mask in PIECES
        ]
    )
    segment = segment_of(slots, lengths)
    position = position_of(slots, segment, lengths)

    first_own = apply_rms_norm(inputs, gain_one).astype(jnp.bfloat16)
    first_near = plane_near(first_own)
    attn_other = [swap_ctx(came) for came in attn_came]
    attn_weights = attn_fetch.begin(attn_core)
    ffn_came = [ffn_fetch.along_x(0)]
    ffn_columns = (ffn_fetch.columns[1], ffn_fetch.core)
    first_near, attn_other, attn_weights, attn_came, cot_low, ffn_columns, ffn_came = together(
        (first_near, attn_other, attn_weights, attn_came, cot_low, ffn_columns, ffn_came)
    )
    ffn_fetch.columns[1], ffn_fetch.core = ffn_columns
    out_grad = cot_low.astype(jnp.float32) * own_valid
    cot_own = out_grad.astype(jnp.bfloat16)
    cot_across = swap_plane(cot_own, 2, 0)
    ffn_came.append(ffn_fetch.along_x(1))
    ffn_other = swap_ctx(ffn_came[0])
    ffn_core = ffn_fetch.along_core()
    first_normed = plane_join(first_near)
    for at in range(2):
        attn_weights = attn_fetch.add(attn_weights, at, attn_came[at], attn_other[at])

    projected = dot_nn(first_normed, attn_weights)
    query_raw = projected[:, :query_width].reshape(row_slots, query_heads, HEAD_SIZE)
    key_raw = projected[:, query_width : query_width + HEAD_SIZE].reshape(row_slots, 1, HEAD_SIZE)
    value_low = projected[:, query_width + HEAD_SIZE : query_width + 2 * HEAD_SIZE].astype(
        jnp.bfloat16
    )
    gate_logits = projected[:, query_width + 2 * HEAD_SIZE :]
    query_rot = apply_rotary(apply_rms_norm(query_raw, query_gain), position, 1.0).astype(
        jnp.bfloat16
    )
    key_rot = apply_rotary(apply_rms_norm(key_raw, key_gain), position, 1.0).astype(jnp.bfloat16)[
        :, 0
    ]

    query_rot, key_rot, value_low, cot_across = together(
        (query_rot, key_rot, value_low, cot_across)
    )
    cot_pair = jnp.stack([cot_own, cot_across])
    cot_near = jnp.stack([cot_pair, swap_plane(cot_pair, 0, 1)], axis=1).reshape(
        -1, cot_own.shape[1]
    )

    allowed = (segment[:, None] == segment[None, :]) & (slots[None, :] <= slots[:, None])
    raw_scores = jnp.einsum("qgd,kd->gqk", query_rot, key_rot, preferred_element_type=jnp.float32)
    scores = jnp.where(allowed, raw_scores * score_scale, NEG_FILL)
    top = jnp.max(scores, axis=-1, keepdims=True)
    weights = jnp.where(allowed, jnp.exp(scores - top), 0.0)
    total = jnp.sum(weights, axis=-1, keepdims=True)
    mixed = jnp.einsum(
        "gqk,kd->gqd", weights.astype(jnp.bfloat16), value_low, preferred_element_type=jnp.float32
    )
    log_total = top + jnp.log(total)
    attended = jnp.transpose(mixed / total, (1, 0, 2))
    attended_rows = attended.reshape(row_slots, query_width)
    gate_sig = jax.nn.sigmoid(gate_logits)
    gated_mix = (attended_rows * gate_sig).astype(jnp.bfloat16)
    gated_mix, ffn_other, ffn_came = together((gated_mix, ffn_other, ffn_came))
    ffn_others = [ffn_other, swap_ctx(ffn_came[1])]
    half = row_slots // 2
    far_part = dot_nn(gated_mix[half:], w_output)
    near_part = dot_nn(gated_mix[:half], w_output)
    own_part, came_parts = scatter_plane(scatter_half(near_part, far_part))
    ffn_weights = ffn_fetch.begin(ffn_core)
    ffn_weights = ffn_fetch.add(ffn_weights, 0, ffn_came[0], ffn_others[0])
    own_part, came_parts, cot_near, ffn_others, ffn_weights, ffn_came = together(
        (own_part, came_parts, cot_near, ffn_others, ffn_weights, ffn_came)
    )
    ffn_grad = jnp.concatenate([cot_near, swap_plane(cot_near, 1, 0)], axis=0)
    hidden_in = inputs + own_valid * scatter_total(own_part, came_parts)
    second_near = plane_near(apply_rms_norm(hidden_in, gain_two).astype(jnp.bfloat16))
    ffn_weights = ffn_fetch.add(ffn_weights, 1, ffn_came[1], ffn_others[1])
    second_near, ffn_grad, ffn_weights = together((second_near, ffn_grad, ffn_weights))
    normed_two = plane_join(second_near)

    hidden_grad = dot_nt(ffn_grad, w_down)
    pre = dot_nn(normed_two, ffn_weights)
    hidden_width = w_down.shape[0]
    gate_pre, up_pre = pre[:, :hidden_width], pre[:, hidden_width:]
    gate_sigmoid = jax.nn.sigmoid(gate_pre)
    activated = gate_pre * gate_sigmoid
    hidden_act = (activated * up_pre).astype(jnp.bfloat16)
    gate_grad = (
        hidden_grad * up_pre * gate_sigmoid * (1.0 + gate_pre * (1.0 - gate_sigmoid))
    ).astype(jnp.bfloat16)
    up_grad = (hidden_grad * activated).astype(jnp.bfloat16)
    ffn_in_grads = jnp.concatenate([gate_grad, up_grad], axis=1)

    sums = CtxSums()
    down_part = jnp.split(dot_tn(ffn_grad, hidden_act).astype(jnp.bfloat16), 4, axis=0)
    down_parts = [jnp.concatenate(down_part[at : at + 2], axis=1) for at in (0, 2)]
    down_parts, hidden_act, ffn_in_grads, normed_two = together(
        (down_parts, hidden_act, ffn_in_grads, normed_two)
    )
    sums.send((("down", 0), down_parts[0]))
    two_far = dot_nt(ffn_in_grads[half:], ffn_weights)
    two_near = dot_nt(ffn_in_grads[:half], ffn_weights)
    own_part, came_parts = scatter_plane(scatter_half(two_near, two_far))
    own_part, came_parts, hidden_act, ffn_in_grads, normed_two = sums.wait(
        (own_part, came_parts, hidden_act, ffn_in_grads, normed_two)
    )
    sums.send((("down", 1), down_parts[1]))
    normed_two_grad = scatter_total(own_part, came_parts)
    back_two, gain_two_grad = norm_back(hidden_in, gain_two, normed_two_grad)
    hidden_total_grad = out_grad + back_two
    attn_near = plane_near((own_valid * hidden_total_grad).astype(jnp.bfloat16))
    ffn_parts = {mask: grad_part(normed_two, ffn_in_grads, mask) for mask in (1, 0, 2, 3)}
    ffn_parts[1] = swap_plane(ffn_parts[1], 1, 0)
    attn_near, ffn_parts, hidden_act, query_rot = sums.wait(
        (attn_near, ffn_parts, hidden_act, query_rot)
    )
    sums.send((("ffn", 0), ffn_parts[0]))
    ffn_parts[2] = swap_plane(ffn_parts[2], 2, 0)
    attn_grad = plane_join(attn_near)
    gated_grad = dot_nt(attn_grad, w_output)
    output_part = dot_tn(attn_grad, gated_mix).astype(jnp.bfloat16)
    mixed_grad = (gated_grad * gate_sig).astype(jnp.bfloat16)
    gate_logit_grad = (gated_grad * attended_rows * gate_sig * (1.0 - gate_sig)).astype(
        jnp.bfloat16
    )
    mixed_grad_heads = mixed_grad.reshape(row_slots, query_heads, HEAD_SIZE)
    delta_rows = jnp.transpose(
        jnp.sum(mixed_grad_heads.astype(jnp.float32) * attended, axis=-1), (1, 0)
    )[..., None]
    raw_again = jnp.einsum("qgd,kd->gqk", query_rot, key_rot, preferred_element_type=jnp.float32)
    soft = jnp.where(allowed, jnp.exp(raw_again * score_scale - log_total), 0.0)
    prob_grad = jnp.einsum(
        "qgd,kd->gqk", mixed_grad_heads, value_low, preferred_element_type=jnp.float32
    )
    score_grad = (soft * (prob_grad - delta_rows) * score_scale).astype(jnp.bfloat16)
    score_grad, soft, ffn_parts, output_part, gate_logit_grad = sums.wait(
        (score_grad, soft.astype(jnp.bfloat16), ffn_parts, output_part, gate_logit_grad)
    )
    sums.send((("ffn", 1), ffn_parts[1]))
    ffn_parts[3] = swap_plane(ffn_parts[3], 3, 0)
    query_rot_grad = jnp.einsum(
        "gqk,kd->qgd", score_grad, key_rot, preferred_element_type=jnp.float32
    )
    key_rot_grad = jnp.einsum(
        "gqk,qgd->kd", score_grad, query_rot, preferred_element_type=jnp.float32
    )
    value_grad = jnp.einsum(
        "gqk,qgd->kd",
        soft,
        mixed_grad_heads,
        preferred_element_type=jnp.float32,
    ).astype(jnp.bfloat16)
    key_back, key_gain_grad = norm_back(
        key_raw, key_gain, apply_rotary(key_rot_grad[:, None], position, -1.0)
    )
    query_back, query_gain_grad = norm_back(
        query_raw, query_gain, apply_rotary(query_rot_grad, position, -1.0)
    )
    attn_in_grads = jnp.concatenate(
        [
            query_back.reshape(row_slots, query_width).astype(jnp.bfloat16),
            key_back[:, 0].astype(jnp.bfloat16),
            value_grad,
            gate_logit_grad,
        ],
        axis=1,
    )
    attn_in_grads, ffn_parts = sums.wait((attn_in_grads, ffn_parts))
    sums.send((("ffn", 2), ffn_parts[2]))
    one_far = dot_nt(attn_in_grads[half:], attn_weights)
    one_near = dot_nt(attn_in_grads[:half], attn_weights)
    own_part, came_parts = scatter_plane(scatter_half(one_near, one_far))
    attn_parts = {mask: grad_part(first_normed, attn_in_grads, mask) for mask in (2, 3, 1, 0)}
    attn_parts[1] = swap_plane(attn_parts[1], 1, 0)
    own_part, came_parts, attn_parts, hidden_act = sums.wait(
        (own_part, came_parts, attn_parts, hidden_act)
    )
    output_parts = jnp.split(output_part, 4, axis=0)

    def attn_sum(mask):
        return (("attn", mask), jnp.concatenate([attn_parts[mask], output_parts[mask]], axis=1))

    hops = sum_hops()

    def hop(value):
        axis, pairs = next(hops)
        return value + lax.ppermute(value, axis, pairs)

    sums.send((("ffn", 3), ffn_parts[3]))
    for mask in (2, 3):
        attn_parts[mask] = swap_plane(attn_parts[mask], mask, 0)
    normed_one_grad = scatter_total(own_part, came_parts)
    back_one, gain_one_grad = norm_back(inputs, gain_one, normed_one_grad)
    input_grad = (hidden_total_grad + back_one).astype(jnp.bfloat16)
    gains = jnp.concatenate([gain_one_grad, gain_two_grad, query_gain_grad, key_gain_grad])[None]
    out_far = dot_nn(hidden_act[half:], w_down).astype(jnp.bfloat16)
    out_near = dot_nn(hidden_act[:half], w_down)
    out_half = scatter_half(out_near, out_far)
    first_attn, second_attn = attn_sum(0), attn_sum(1)
    attn_parts, input_grad, gains, out_half, first_attn, second_attn = sums.wait(
        (
            attn_parts,
            input_grad,
            gains,
            out_half,
            dict([first_attn]),
            dict([second_attn]),
        )
    )
    sums.send(*first_attn.items())
    input_grad = swap_ranks(input_grad)
    gains = hop(gains)
    out_own, out_came = scatter_plane(out_half)
    sums.send(*second_attn.items())
    third_attn, fourth_attn = dict([attn_sum(2)]), dict([attn_sum(3)])
    gains, input_grad, out_own, out_came, third_attn, fourth_attn = sums.wait(
        (gains, input_grad, out_own, out_came, third_attn, fourth_attn), 2
    )
    sums.send(*third_attn.items())
    layer_output = hidden_in + own_valid * scatter_total(out_own, out_came)
    layer_output = swap_ranks(layer_output.astype(jnp.bfloat16))
    gains = sums.wait(hop(gains), 2)
    sums.send(*fourth_attn.items())
    gains, layer_output = sums.wait((hop(gains), layer_output), 2)
    sums.send()
    gains = sums.wait(hop(gains), 2)
    sums.send()
    gains = sums.wait(hop(gains), 2)[0]
    while any(sums.flight) or sums.arrived:
        sums.send()
        sums.wait((), 2)

    down_sums = [sums.done["down", at] for at in range(2)]
    down_sums = [part for pair in down_sums for part in jnp.split(pair, 2, axis=1)]
    grad_w_down = jnp.concatenate([part.T for part in down_sums], axis=1)
    grad_w_output = jnp.concatenate(
        [sums.done["attn", mask][:, -query_width:].T for mask in range(4)], axis=1
    )
    ffn_sums = [jnp.split(sums.done["ffn", mask], 2, axis=1) for mask in range(4)]
    grad_w_gate, grad_w_up = (
        place_columns([parts[i] for parts in ffn_sums], hidden_width) for i in range(2)
    )
    ends = [0, query_width, query_width + HEAD_SIZE, query_width + 2 * HEAD_SIZE]
    widths = (query_width, HEAD_SIZE, HEAD_SIZE, query_width)
    grad_w_query, grad_w_key, grad_w_value, grad_w_out_gate = (
        place_columns(
            [sums.done["attn", mask][:, start : start + width] for mask in range(4)], width
        )
        for start, width in zip(ends, widths)
    )
    model_width = layer_input.shape[1]
    ends = (model_width, 2 * model_width, 2 * model_width + HEAD_SIZE)
    return (
        layer_output,
        input_grad,
        gains[: ends[0]],
        gains[ends[1] : ends[2]],
        gains[ends[2] :],
        grad_w_query,
        grad_w_key,
        grad_w_value,
        grad_w_out_gate,
        grad_w_output,
        gains[ends[0] : ends[1]],
        grad_w_gate,
        grad_w_up,
        grad_w_down,
    )


def solution(mesh):
    sizes = dict(mesh.shape)
    plane = (sizes["fsdp"], sizes["ctx"], sizes["tp"]) == (4, 4, 2)
    return jax.shard_map(
        plane_body if plane else body,
        mesh=mesh,
        in_specs=(
            P(("fsdp", "ctx", "tp"), None),
            P(("fsdp", "ctx", "tp"), None),
            P("fsdp", None),
            P(),
            P(),
            P(),
            P("fsdp", "tp"),
            P("fsdp", "tp"),
            P("fsdp", "tp"),
            P("fsdp", "tp"),
            P(("tp", "fsdp"), None),
            P(),
            P("fsdp", "tp"),
            P("fsdp", "tp"),
            P(("tp", "fsdp"), None),
        ),
        out_specs=(
            P(("fsdp", "ctx", "tp"), None),
            P(("fsdp", "ctx", "tp"), None),
            P(),
            P(),
            P(),
            P("fsdp", "tp"),
            P("fsdp", "tp"),
            P("fsdp", "tp"),
            P("fsdp", "tp"),
            P(("tp", "fsdp"), None),
            P(),
            P("fsdp", "tp"),
            P("fsdp", "tp"),
            P(("tp", "fsdp"), None),
        ),
        check_vma=False,
    )
```

```python
import jax
import jax.numpy as jnp
from jax import lax
from jax.experimental import pallas as pl
from jax.experimental.pallas import tpu as pltpu
from jax.sharding import PartitionSpec as P

HEAD_SIZE = 128


EPSILON = 1e-06
ROPE_BASE = 1000000.0
NEG_FILL = -1e30


def as_sent(value):

    def short(part):
        return part.astype(jnp.bfloat16) if part.dtype == jnp.float32 else part

    return jax.tree.map(short, value)


def apply_rms_norm(values, gain_vec):
    return (
        values * lax.rsqrt(jnp.mean(values * values, axis=-1, keepdims=True) + EPSILON) * gain_vec
    )


def norm_back(values, gain_vec, grad_in):
    row_scale = lax.rsqrt(jnp.mean(values * values, axis=-1, keepdims=True) + EPSILON)
    unit_rows = values * row_scale
    scaled = grad_in * gain_vec
    back_rows = row_scale * (
        scaled - unit_rows * jnp.mean(scaled * unit_rows, axis=-1, keepdims=True)
    )
    gain_grad = jnp.sum((grad_in * unit_rows).reshape(-1, values.shape[-1]), axis=0)
    return (back_rows, gain_grad)


def apply_rotary(values, token_position, direction):
    half_size = values.shape[-1] // 2
    frequency = jnp.power(ROPE_BASE, -jnp.arange(half_size, dtype=jnp.float32) / half_size)
    angle = token_position.astype(jnp.float32)[:, None] * frequency[None, :]
    cosine = jnp.cos(angle)[:, None, :]
    sine = direction * jnp.sin(angle)[:, None, :]
    first_half = values[..., :half_size]
    second_half = values[..., half_size:]
    return jnp.concatenate(
        [first_half * cosine - second_half * sine, second_half * cosine + first_half * sine],
        axis=-1,
    )


def segment_of(slot_ids, lengths):
    first_len = lengths[0, 0]
    second_len = lengths[0, 1]
    return jnp.where(slot_ids < first_len, 0, jnp.where(slot_ids < first_len + second_len, 1, 2))


def position_of(slot_ids, segment, lengths):
    seg_begin = jnp.where(
        segment == 0, 0, jnp.where(segment == 1, lengths[0, 0], lengths[0, 0] + lengths[0, 1])
    )
    return slot_ids - seg_begin


def to_block(local_part):
    return lax.all_gather(local_part, "tp", axis=0, tiled=True)


def to_share(partial_rows):
    return lax.psum_scatter(
        partial_rows.astype(jnp.bfloat16), "tp", scatter_dimension=0, tiled=True
    ).astype(jnp.float32)


def fold_product(left_rows, weight_set):
    pieces = jax.tree.map(
        lambda a: lax.all_gather(a, "fsdp", axis=0, tiled=True), as_sent(weight_set)
    )
    return tuple(
        (
            jnp.dot(left_rows, weight_part, preferred_element_type=jnp.float32)
            for weight_part in pieces
        )
    )


def back_product(grad_rows, weight_set):
    pieces = jax.tree.map(
        lambda a: lax.all_gather(a, "fsdp", axis=0, tiled=True), as_sent(weight_set)
    )
    result = lax.dot_general(
        grad_rows[0], pieces[0], (((1,), (1,)), ((), ())), preferred_element_type=jnp.float32
    )
    for grad_part, weight_part in zip(grad_rows[1:], pieces[1:]):
        result = result + lax.dot_general(
            grad_part, weight_part, (((1,), (1,)), ((), ())), preferred_element_type=jnp.float32
        )
    return result


def weight_grads(left_rows, grad_rows):
    widths = [grad_part.shape[1] for grad_part in grad_rows]
    shared = lax.psum_scatter(
        jnp.concatenate(
            [
                lax.dot_general(
                    left_rows,
                    grad_part,
                    (((0,), (0,)), ((), ())),
                    preferred_element_type=jnp.float32,
                )
                for grad_part in grad_rows
            ],
            axis=1,
        ).astype(jnp.bfloat16),
        "fsdp",
        scatter_dimension=0,
        tiled=True,
    )
    summed = lax.psum(shared, "ctx").astype(jnp.float32)
    pieces = []
    offset = 0
    for column_width in widths:
        pieces.append(summed[:, offset : offset + column_width])
        offset = offset + column_width
    return tuple(pieces)


def body(
    layer_input,
    cotangent,
    lengths,
    attn_norm,
    query_norm_gain,
    k_norm,
    w_query,
    key_weight,
    value_weight,
    w_out_gate,
    w_output,
    ffn_norm,
    w_gate,
    w_up,
    w_down,
):
    local_rows = layer_input.shape[0]
    block_rows = local_rows * lax.axis_size("tp")
    query_heads = w_query.shape[1] // HEAD_SIZE
    kv_heads = key_weight.shape[1] // HEAD_SIZE
    groups = query_heads // kv_heads
    score_scale = HEAD_SIZE ** (-0.5)
    block_first = lax.axis_index("ctx") * block_rows
    own_slots = (
        block_first + lax.axis_index("tp") * local_rows + jnp.arange(local_rows, dtype=jnp.int32)
    )
    own_valid = (segment_of(own_slots, lengths) < 2).astype(jnp.float32)[:, None]
    query_slots = block_first + jnp.arange(block_rows, dtype=jnp.int32)
    query_segment = segment_of(query_slots, lengths)
    query_position = position_of(query_slots, query_segment, lengths)
    inputs = layer_input.astype(jnp.float32)
    gain_one = attn_norm.astype(jnp.float32)
    gain_two = ffn_norm.astype(jnp.float32)
    query_gain = query_norm_gain.astype(jnp.float32)
    key_gain = k_norm.astype(jnp.float32)
    first_normed = to_block(apply_rms_norm(inputs, gain_one).astype(jnp.bfloat16))
    query_rows, key_projected, value_proj, gate_logits = fold_product(
        first_normed, (w_query, key_weight, value_weight, w_out_gate)
    )
    query_heads_raw = query_rows.reshape(block_rows, query_heads, HEAD_SIZE)
    key_heads_raw = key_projected.reshape(block_rows, kv_heads, HEAD_SIZE)
    query_rotated = apply_rotary(
        apply_rms_norm(query_heads_raw, query_gain), query_position, 1.0
    ).astype(jnp.bfloat16)
    key_rot = apply_rotary(apply_rms_norm(key_heads_raw, key_gain), query_position, 1.0).astype(
        jnp.bfloat16
    )
    query_grouped = query_rotated.reshape(block_rows, kv_heads, groups, HEAD_SIZE)
    key_flat = key_rot.reshape(block_rows, kv_heads * HEAD_SIZE)
    value_reduced = value_proj.astype(jnp.bfloat16)

    def key_mask(piece_rows):
        key_slots = jnp.arange(piece_rows, dtype=jnp.int32)
        key_segment = segment_of(key_slots, lengths)
        return (query_segment[:, None] == key_segment[None, :]) & (
            key_slots[None, :] <= query_slots[:, None]
        )

    head_shape = (kv_heads, groups, block_rows)
    running_top = jnp.full(head_shape + (1,), NEG_FILL, jnp.float32)
    key_piece = lax.all_gather(key_flat, "ctx", axis=0, tiled=True)
    value_piece = lax.all_gather(value_reduced, "ctx", axis=0, tiled=True)
    piece_rows = key_piece.shape[0]
    allowed = key_mask(piece_rows)
    raw_scores = jnp.einsum(
        "qhgd,khd->hgqk",
        query_grouped,
        key_piece.reshape(piece_rows, kv_heads, HEAD_SIZE),
        preferred_element_type=jnp.float32,
    )
    scores = jnp.where(allowed, raw_scores * score_scale, NEG_FILL)
    new_top = jnp.maximum(running_top, jnp.max(scores, axis=-1, keepdims=True))
    weights = jnp.where(allowed, jnp.exp(scores - new_top), 0.0)
    running_total = jnp.sum(weights, axis=-1, keepdims=True)
    mixed_sum = jnp.einsum(
        "hgqk,khd->hgqd",
        weights.astype(jnp.bfloat16),
        value_piece.reshape(piece_rows, kv_heads, HEAD_SIZE),
        preferred_element_type=jnp.float32,
    )
    mixed_sum, running_top, running_total = (mixed_sum, new_top, running_total)
    log_total = running_top + jnp.log(running_total)
    attended = jnp.transpose(mixed_sum / running_total, (2, 0, 1, 3))
    attended_rows = attended.reshape(block_rows, query_heads * HEAD_SIZE)
    gate_sig = jax.nn.sigmoid(gate_logits)
    gated_mix = (attended_rows * gate_sig).astype(jnp.bfloat16)
    attn_share = to_share(fold_product(gated_mix, (w_output,))[0])
    hidden_in = inputs + own_valid * attn_share
    normed_two = to_block(apply_rms_norm(hidden_in, gain_two).astype(jnp.bfloat16))
    gate_pre, up_pre = fold_product(normed_two, (w_gate, w_up))
    gate_sigmoid = jax.nn.sigmoid(gate_pre)
    activated = gate_pre * gate_sigmoid
    hidden_act = (activated * up_pre).astype(jnp.bfloat16)
    ffn_share = to_share(fold_product(hidden_act, (w_down,))[0])
    layer_output = (hidden_in + own_valid * ffn_share).astype(jnp.bfloat16)
    out_grad = cotangent.astype(jnp.float32) * own_valid
    ffn_grad = to_block(out_grad.astype(jnp.bfloat16))
    hidden_grad = back_product((ffn_grad,), (w_down,))
    grad_w_down = weight_grads(hidden_act, (ffn_grad,))[0]
    gate_grad = (
        hidden_grad * up_pre * gate_sigmoid * (1.0 + gate_pre * (1.0 - gate_sigmoid))
    ).astype(jnp.bfloat16)
    up_grad = (hidden_grad * activated).astype(jnp.bfloat16)
    normed_two_grad = to_share(back_product((gate_grad, up_grad), (w_gate, w_up)))
    grad_w_gate, grad_w_up = weight_grads(normed_two, (gate_grad, up_grad))
    back_two, gain_two_grad = norm_back(hidden_in, gain_two, normed_two_grad)
    hidden_total_grad = out_grad + back_two
    attn_grad = to_block((own_valid * hidden_total_grad).astype(jnp.bfloat16))
    gated_grad = back_product((attn_grad,), (w_output,))
    grad_w_output = weight_grads(gated_mix, (attn_grad,))[0]
    mixed_grad = (gated_grad * gate_sig).astype(jnp.bfloat16)
    gate_logit_grad = (gated_grad * attended_rows * gate_sig * (1.0 - gate_sig)).astype(
        jnp.bfloat16
    )
    mixed_grad_heads = mixed_grad.reshape(block_rows, kv_heads, groups, HEAD_SIZE)
    delta_rows = jnp.transpose(
        jnp.sum(mixed_grad_heads.astype(jnp.float32) * attended, axis=-1), (1, 2, 0)
    )[..., None]
    key_piece = lax.all_gather(key_flat, "ctx", axis=0, tiled=True)
    value_piece = lax.all_gather(value_reduced, "ctx", axis=0, tiled=True)
    piece_rows = key_piece.shape[0]
    key_view = key_piece.reshape(piece_rows, kv_heads, HEAD_SIZE)
    value_view = value_piece.reshape(piece_rows, kv_heads, HEAD_SIZE)
    allowed = key_mask(piece_rows)
    raw_scores = jnp.einsum(
        "qhgd,khd->hgqk", query_grouped, key_view, preferred_element_type=jnp.float32
    )
    soft_vals = jnp.where(allowed, jnp.exp(raw_scores * score_scale - log_total), 0.0)
    prob_grad = jnp.einsum(
        "qhgd,khd->hgqk", mixed_grad_heads, value_view, preferred_element_type=jnp.float32
    )
    score_grad = (soft_vals * (prob_grad - delta_rows) * score_scale).astype(jnp.bfloat16)
    query_acc = jnp.einsum(
        "hgqk,khd->qhgd", score_grad, key_view, preferred_element_type=jnp.float32
    )
    key_part = jnp.einsum(
        "hgqk,qhgd->khd", score_grad, query_grouped, preferred_element_type=jnp.float32
    ).reshape(piece_rows, kv_heads * HEAD_SIZE)
    value_part = jnp.einsum(
        "hgqk,qhgd->khd",
        soft_vals.astype(jnp.bfloat16),
        mixed_grad_heads,
        preferred_element_type=jnp.float32,
    ).reshape(piece_rows, kv_heads * HEAD_SIZE)
    kv_acc = jnp.concatenate([key_part, value_part], axis=1)
    query_acc, kv_acc = (query_acc, kv_acc)
    kv_own = lax.psum_scatter(
        kv_acc.astype(jnp.bfloat16), "ctx", scatter_dimension=0, tiled=True
    ).astype(jnp.float32)
    key_rot_grad = kv_own[:, : kv_heads * HEAD_SIZE].reshape(block_rows, kv_heads, HEAD_SIZE)
    value_grad = kv_own[:, kv_heads * HEAD_SIZE :].astype(jnp.bfloat16)
    key_back, key_gain_grad = norm_back(
        key_heads_raw, key_gain, apply_rotary(key_rot_grad, query_position, -1.0)
    )
    query_back, query_gain_grad = norm_back(
        query_heads_raw,
        query_gain,
        apply_rotary(query_acc.reshape(block_rows, query_heads, HEAD_SIZE), query_position, -1.0),
    )
    query_grad = query_back.reshape(block_rows, query_heads * HEAD_SIZE).astype(jnp.bfloat16)
    key_grad = key_back.reshape(block_rows, kv_heads * HEAD_SIZE).astype(jnp.bfloat16)
    attn_in_grads = (query_grad, key_grad, value_grad, gate_logit_grad)
    normed_one_grad = to_share(
        back_product(attn_in_grads, (w_query, key_weight, value_weight, w_out_gate))
    )
    grad_w_query, grad_w_key, grad_w_value, grad_w_out_gate = weight_grads(
        first_normed, attn_in_grads
    )
    back_one, gain_one_grad = norm_back(inputs, gain_one, normed_one_grad)
    input_grad = (hidden_total_grad + back_one).astype(jnp.bfloat16)
    gain_totals = lax.psum(
        (gain_one_grad, query_gain_grad, key_gain_grad, gain_two_grad), ("fsdp", "ctx", "tp")
    )
    return (
        layer_output,
        input_grad,
        gain_totals[0],
        gain_totals[1],
        gain_totals[2],
        grad_w_query,
        grad_w_key,
        grad_w_value,
        grad_w_out_gate,
        grad_w_output,
        gain_totals[3],
        grad_w_gate,
        grad_w_up,
        grad_w_down,
    )


def xor_pairs(count, mask):
    return [(i, i ^ mask) for i in range(count)]


def swap_plane(value, fsdp_mask, tp_mask):
    fsdp_size, tp_size = lax.axis_size("fsdp"), lax.axis_size("tp")
    if tp_mask == 0:
        return lax.ppermute(value, "fsdp", xor_pairs(fsdp_size, fsdp_mask))
    if fsdp_mask == 0:
        return lax.ppermute(value, "tp", xor_pairs(tp_size, tp_mask))
    return lax.ppermute(
        value,
        ("fsdp", "tp"),
        xor_pairs(fsdp_size * tp_size, fsdp_mask * tp_size + tp_mask),
    )


def swap_ranks(value, by_neighbour=False):
    size = lax.axis_size("fsdp")
    mask = 2 if by_neighbour else 0
    pairs = [(a * size + b, (b ^ mask) * size + a) for a in range(size) for b in range(size)]
    moved = lax.ppermute(value, ("fsdp", "ctx"), pairs)
    return swap_plane(moved, mask, 0) if mask else moved


PIECES = ((0, 0), (0, 1), (2, 0), (2, 1))


def plane_beside(own):
    return own, swap_plane(own, 0, 1), swap_plane(own, 2, 0)


def plane_near(beside):
    own, over_tp, over_x = beside
    rows = own.shape[0] // 2
    three = jnp.concatenate([own, over_tp, over_x], axis=0)
    corner = [swap_plane(over_x[:rows], 0, 1), swap_plane(over_tp[rows:], 2, 0)]
    return three, swap_plane(three, 1, 0), jnp.concatenate(corner, axis=0)


def plane_join(near):
    three, three_far, corner = near
    return jnp.concatenate([three, corner, three_far, swap_plane(corner, 1, 0)], axis=0)


def scatter_half(near_part, far_part):
    return near_part + swap_plane(far_part.astype(jnp.bfloat16), 1, 0).astype(jnp.float32)


def scatter_plane(half, beside=()):
    rows = half.shape[0] // 8
    piece = [half[at * rows : (at + 1) * rows] for at in range(8)]

    def sent(parts, *masks):
        low = jnp.concatenate(parts, axis=0).astype(jnp.bfloat16)
        return swap_plane(low, *masks)

    by_x = sent([piece[4], piece[6]], 2, 0)
    by_tp = sent([piece[3], piece[7]], 0, 1)
    by_x, by_tp, beside = lax.optimization_barrier((by_x, by_tp, beside))
    by_x, by_tp = by_x.astype(jnp.float32), by_tp.astype(jnp.float32)
    top = sent([piece[2] + by_x[rows:]], 0, 1)
    bottom = sent([piece[5] + by_tp[rows:]], 2, 0)
    return jnp.concatenate([piece[0] + by_x[:rows], piece[1] + by_tp[:rows]], axis=0), [top, bottom], beside


def scatter_total(own, came):
    return own + jnp.concatenate(came, axis=0).astype(jnp.float32)


def dot_nn(a, b):
    return jnp.dot(a, b, preferred_element_type=jnp.float32)


def dot_nt(a, b):
    return lax.dot_general(a, b, (((1,), (1,)), ((), ())), preferred_element_type=jnp.float32)


def dot_tn(a, b):
    return lax.dot_general(a, b, (((0,), (0,)), ((), ())), preferred_element_type=jnp.float32)


INWARD, ACROSS, OUTWARD = [(0, 1), (3, 2)], [(1, 2), (2, 1)], [(1, 0), (2, 3)]


class CtxSums:
    def __init__(self):
        self.flight, self.arrived, self.done = [], [], {}

    def send(self, *fresh):
        place = lax.axis_index("ctx")
        inner = (place == 1) | (place == 2)
        sent, totals, fresh = [], [], list(fresh)
        for stage, name, here, came in self.arrived:
            if stage == 2:
                self.done[name] = here, came
                continue
            both = (here.astype(jnp.float32) + came.astype(jnp.float32)).astype(jnp.bfloat16)
            if stage:
                totals.append((name, both))
            else:
                sent.append(([(1, name, both)], lax.ppermute(both, "ctx", ACROSS)))
        while totals and fresh and totals[0][1].shape == fresh[0][1].shape:
            (out, total), (name, part) = totals.pop(0), fresh.pop(0)
            moved = swap_ctx(jnp.where(inner, total, part))
            sent.append(([(0, name, part), (2, out, total)], moved))
        for name, part in fresh:
            sent.append(([(0, name, part)], lax.ppermute(part, "ctx", INWARD)))
        for name, total in totals:
            sent.append(([(2, name, total)], lax.ppermute(total, "ctx", OUTWARD)))
        self.arrived = []
        self.flight.append(sent)

    def wait(self, kept, depth=1):
        old = []
        while len(self.flight) >= depth:
            old += self.flight.pop(0)
        heres = [[here for _, _, here in entry[0]] for entry in old]
        moved = [entry[1] for entry in old]
        heres, moved, kept = lax.optimization_barrier((heres, moved, kept))
        self.arrived = [
            (stage, name, here, came)
            for entry, parts, came in zip(old, heres, moved)
            for (stage, name, _), here in zip(entry[0], parts)
        ]
        return kept


def sum_hops():
    for axis, mask in (("fsdp", 1), ("fsdp", 2), ("tp", 1)):
        yield axis, xor_pairs(lax.axis_size(axis), mask)


def weight_columns(weights, owner):
    parts = []
    for weight in weights:
        width = weight.shape[1] // lax.axis_size("fsdp")
        parts.append(lax.dynamic_slice_in_dim(weight, owner * width, width, 1))
    return jnp.concatenate(parts, axis=1)


class Fetch:
    def __init__(self, weights):
        self.me, self.size = lax.axis_index("fsdp"), lax.axis_size("fsdp")
        self.side = lax.axis_index("ctx") % 2
        self.rows = weights[0].shape[0]
        self.half = self.rows // 2
        mine = [
            lax.dynamic_slice_in_dim(weight, self.side * self.half, self.half, 0)
            for weight in weights
        ]
        self.columns = [weight_columns(mine, self.me ^ mask) for mask in (2, 3)]
        self.own = weight_columns(weights, self.me)
        self.core = weight_columns(weights, self.me ^ 1)

    def along_x(self, at):
        return swap_plane(self.columns[at], (2, 3)[at], 0)

    def along_core(self):
        return swap_plane(self.core, 1, 0)

    def begin(self, core):
        whole = jnp.zeros((self.rows * self.size, self.own.shape[1]), self.own.dtype)
        for part, peer in ((self.own, self.me), (core, self.me ^ 1)):
            whole = lax.dynamic_update_slice_in_dim(whole, part, peer * self.rows, 0)
        return whole

    def add(self, whole, at, came, other):
        start = (self.me ^ (2, 3)[at]) * self.rows
        whole = lax.dynamic_update_slice_in_dim(whole, came, start + self.side * self.half, 0)
        return lax.dynamic_update_slice_in_dim(
            whole, other, start + (1 - self.side) * self.half, 0
        )


def swap_ctx(value):
    return lax.ppermute(value, "ctx", xor_pairs(lax.axis_size("ctx"), 1))


def grad_part(left, right, mask):
    owner = lax.axis_index("fsdp") ^ mask
    rows = left.shape[1] // lax.axis_size("fsdp")
    columns = lax.dynamic_slice_in_dim(left, owner * rows, rows, 1)
    return dot_tn(columns, right).astype(jnp.bfloat16)


def at_inner():
    place = lax.axis_index("ctx")
    return (place == 1) | (place == 2)


def chosen(pair):
    return jnp.where(at_inner(), *pair).astype(jnp.float32)


def place_columns(pairs, widths):
    size, rows, block = lax.axis_size("fsdp"), pairs[0][0].shape[0], 128
    scalars = jnp.stack([lax.axis_index("fsdp"), at_inner().astype(jnp.int32)])

    def kernel(scalars, *refs):
        parts, outs = refs[: 2 * size], refs[2 * size :]
        for mask in range(size):
            here, came = parts[2 * mask], parts[2 * mask + 1]
            value = jnp.where(
                scalars[1] == 1, here[...].astype(jnp.float32), came[...].astype(jnp.float32)
            )
            start = 0
            for out, width in zip(outs, widths):
                column = pl.multiple_of((scalars[0] ^ mask) * width, 128)
                out[:, pl.ds(column, width)] = value[:, start : start + width]
                start += width

    total = sum(widths)
    return pl.pallas_call(
        kernel,
        grid_spec=pltpu.PrefetchScalarGridSpec(
            num_scalar_prefetch=1,
            grid=(rows // block,),
            in_specs=[pl.BlockSpec((block, total), lambda i, _: (i, 0))] * (2 * size),
            out_specs=[pl.BlockSpec((block, width * size), lambda i, _: (i, 0)) for width in widths],
        ),
        out_shape=[jax.ShapeDtypeStruct((rows, width * size), jnp.float32) for width in widths],
    )(scalars, *(part for pair in pairs for part in pair))


def plane_body(
    layer_input,
    cotangent,
    lengths,
    attn_norm,
    query_norm_gain,
    k_norm,
    w_query,
    key_weight,
    value_weight,
    w_out_gate,
    w_output,
    ffn_norm,
    w_gate,
    w_up,
    w_down,
):
    fsdp_size, tp_size = lax.axis_size("fsdp"), lax.axis_size("tp")
    fsdp_at, tp_at = lax.axis_index("fsdp"), lax.axis_index("tp")
    local_rows = layer_input.shape[0]
    row_slots = local_rows * fsdp_size * tp_size
    query_heads = w_query.shape[1] // HEAD_SIZE // fsdp_size
    query_width = query_heads * HEAD_SIZE
    score_scale = HEAD_SIZE ** (-0.5)
    gain_one = attn_norm.astype(jnp.float32)
    gain_two = ffn_norm.astype(jnp.float32)
    query_gain = query_norm_gain.astype(jnp.float32)
    key_gain = k_norm.astype(jnp.float32)

    together = lax.optimization_barrier
    input_low = swap_ranks(layer_input)
    attn_fetch = Fetch((w_query, key_weight, value_weight, w_out_gate))
    attn_came = [attn_fetch.along_x(at) for at in range(2)]
    attn_core = attn_fetch.along_core()
    lengths = swap_ranks(lengths)
    input_low, attn_came, cotangent = together((input_low, attn_came, cotangent))
    inputs = input_low.astype(jnp.float32)

    def slots_of(fsdp_index, tp_index):
        return (fsdp_index * tp_size + tp_index) * local_rows + jnp.arange(
            local_rows, dtype=jnp.int32
        )

    own_slots = slots_of(fsdp_at, tp_at)
    own_valid = (segment_of(own_slots, lengths) < 2).astype(jnp.float32)[:, None]
    slots = jnp.concatenate(
        [
            slots_of(fsdp_at ^ fsdp_mask ^ core, tp_at ^ tp_mask)
            for core in (0, 1)
            for fsdp_mask, tp_mask in PIECES
        ]
    )
    segment = segment_of(slots, lengths)
    position = position_of(slots, segment, lengths)

    first_own = apply_rms_norm(inputs, gain_one).astype(jnp.bfloat16)
    first_beside = plane_beside(first_own)
    attn_other = [swap_ctx(came) for came in attn_came]
    cot_low = swap_ranks(cotangent)
    attn_weights = attn_fetch.begin(attn_core)
    first_beside, attn_other, attn_weights = together((first_beside, attn_other, attn_weights))
    first_near = plane_near(first_beside)
    for at in range(2):
        attn_weights = attn_fetch.add(attn_weights, at, attn_came[at], attn_other[at])
    ffn_fetch = Fetch((w_gate, w_up))
    ffn_columns = (ffn_fetch.columns, ffn_fetch.core)
    first_near, attn_weights, ffn_columns = together((first_near, attn_weights, ffn_columns))
    ffn_fetch.columns, ffn_fetch.core = ffn_columns
    ffn_came = [ffn_fetch.along_x(at) for at in range(2)]
    ffn_core = ffn_fetch.along_core()
    first_normed = plane_join(first_near)

    projected = dot_nn(first_normed, attn_weights)
    query_raw = projected[:, :query_width].reshape(row_slots, query_heads, HEAD_SIZE)
    key_raw = projected[:, query_width : query_width + HEAD_SIZE].reshape(row_slots, 1, HEAD_SIZE)
    value_low = projected[:, query_width + HEAD_SIZE : query_width + 2 * HEAD_SIZE].astype(
        jnp.bfloat16
    )
    gate_logits = projected[:, query_width + 2 * HEAD_SIZE :]
    query_rot = apply_rotary(apply_rms_norm(query_raw, query_gain), position, 1.0).astype(
        jnp.bfloat16
    )
    key_rot = apply_rotary(apply_rms_norm(key_raw, key_gain), position, 1.0).astype(jnp.bfloat16)[
        :, 0
    ]

    query_rot, key_rot, value_low, ffn_came[0], cot_low = together(
        (query_rot, key_rot, value_low, ffn_came[0], cot_low)
    )
    ffn_other = swap_ctx(ffn_came[0])
    out_grad = cot_low.astype(jnp.float32) * own_valid
    cot_beside = plane_beside(out_grad.astype(jnp.bfloat16))

    allowed = (segment[:, None] == segment[None, :]) & (slots[None, :] <= slots[:, None])
    raw_scores = jnp.einsum("qgd,kd->gqk", query_rot, key_rot, preferred_element_type=jnp.float32)
    scores = jnp.where(allowed, raw_scores * score_scale, NEG_FILL)
    top = jnp.max(scores, axis=-1, keepdims=True)
    weights = jnp.where(allowed, jnp.exp(scores - top), 0.0)
    total = jnp.sum(weights, axis=-1, keepdims=True)
    mixed = jnp.einsum(
        "gqk,kd->gqd", weights.astype(jnp.bfloat16), value_low, preferred_element_type=jnp.float32
    )
    log_total = top + jnp.log(total)
    attended = jnp.transpose(mixed / total, (1, 0, 2))
    attended_rows = attended.reshape(row_slots, query_width)
    gate_sig = jax.nn.sigmoid(gate_logits)
    gated_mix = (attended_rows * gate_sig).astype(jnp.bfloat16)
    gated_mix, ffn_came, cot_beside, ffn_other = together(
        (gated_mix, ffn_came, cot_beside, ffn_other)
    )
    ffn_others = [ffn_other, swap_ctx(ffn_came[1])]
    half = row_slots // 2
    far_part = dot_nn(gated_mix[half:], w_output)
    near_part = dot_nn(gated_mix[:half], w_output)
    own_part, came_parts, ffn_others[1] = scatter_plane(
        scatter_half(near_part, far_part), ffn_others[1]
    )
    ffn_weights = ffn_fetch.begin(ffn_core)
    ffn_weights = ffn_fetch.add(ffn_weights, 0, ffn_came[0], ffn_others[0])
    cot_near = plane_near(cot_beside)
    own_part, came_parts, cot_near, ffn_others, ffn_weights, ffn_came = together(
        (own_part, came_parts, cot_near, ffn_others, ffn_weights, ffn_came)
    )
    ffn_grad = plane_join(cot_near)
    hidden_in = inputs + own_valid * scatter_total(own_part, came_parts)
    second_near = plane_near(
        plane_beside(apply_rms_norm(hidden_in, gain_two).astype(jnp.bfloat16))
    )
    ffn_weights = ffn_fetch.add(ffn_weights, 1, ffn_came[1], ffn_others[1])
    second_near, ffn_grad, ffn_weights = together((second_near, ffn_grad, ffn_weights))
    normed_two = plane_join(second_near)

    hidden_grad = dot_nt(ffn_grad, w_down)
    pre = dot_nn(normed_two, ffn_weights)
    hidden_width = w_down.shape[0]
    gate_pre, up_pre = pre[:, :hidden_width], pre[:, hidden_width:]
    gate_sigmoid = jax.nn.sigmoid(gate_pre)
    activated = gate_pre * gate_sigmoid
    hidden_act = (activated * up_pre).astype(jnp.bfloat16)
    gate_grad = (
        hidden_grad * up_pre * gate_sigmoid * (1.0 + gate_pre * (1.0 - gate_sigmoid))
    ).astype(jnp.bfloat16)
    up_grad = (hidden_grad * activated).astype(jnp.bfloat16)
    ffn_in_grads = jnp.concatenate([gate_grad, up_grad], axis=1)

    sums = CtxSums()
    down_parts = jnp.split(dot_tn(hidden_act, ffn_grad).astype(jnp.bfloat16), 2, axis=0)
    down_parts, hidden_act, ffn_in_grads, normed_two = together(
        (down_parts, hidden_act, ffn_in_grads, normed_two)
    )
    sums.send((("down", 0), down_parts[0]))
    two_far = dot_nt(ffn_in_grads[half:], ffn_weights)
    two_near = dot_nt(ffn_in_grads[:half], ffn_weights)
    own_part, came_parts, _ = scatter_plane(scatter_half(two_near, two_far))
    own_part, came_parts, hidden_act, ffn_in_grads, normed_two = sums.wait(
        (own_part, came_parts, hidden_act, ffn_in_grads, normed_two)
    )
    sums.send((("down", 1), down_parts[1]))
    normed_two_grad = scatter_total(own_part, came_parts)
    back_two, gain_two_grad = norm_back(hidden_in, gain_two, normed_two_grad)
    hidden_total_grad = out_grad + back_two
    attn_near = plane_near(plane_beside((own_valid * hidden_total_grad).astype(jnp.bfloat16)))
    ffn_parts = {mask: grad_part(normed_two, ffn_in_grads, mask) for mask in (1, 0, 2, 3)}
    ffn_parts[1] = swap_plane(ffn_parts[1], 1, 0)
    attn_near, ffn_parts, hidden_act, query_rot = sums.wait(
        (attn_near, ffn_parts, hidden_act, query_rot)
    )
    sums.send((("ffn", 0), ffn_parts[0]))
    ffn_parts[2] = swap_plane(ffn_parts[2], 2, 0)
    attn_grad = plane_join(attn_near)
    gated_grad = dot_nt(attn_grad, w_output)
    output_part = dot_tn(gated_mix, attn_grad).astype(jnp.bfloat16)
    mixed_grad = (gated_grad * gate_sig).astype(jnp.bfloat16)
    gate_logit_grad = (gated_grad * attended_rows * gate_sig * (1.0 - gate_sig)).astype(
        jnp.bfloat16
    )
    mixed_grad_heads = mixed_grad.reshape(row_slots, query_heads, HEAD_SIZE)
    delta_rows = jnp.transpose(
        jnp.sum(mixed_grad_heads.astype(jnp.float32) * attended, axis=-1), (1, 0)
    )[..., None]
    raw_again = jnp.einsum("qgd,kd->gqk", query_rot, key_rot, preferred_element_type=jnp.float32)
    soft = jnp.where(allowed, jnp.exp(raw_again * score_scale - log_total), 0.0)
    prob_grad = jnp.einsum(
        "qgd,kd->gqk", mixed_grad_heads, value_low, preferred_element_type=jnp.float32
    )
    score_grad = (soft * (prob_grad - delta_rows) * score_scale).astype(jnp.bfloat16)
    score_grad, soft, ffn_parts, output_part, gate_logit_grad = sums.wait(
        (score_grad, soft.astype(jnp.bfloat16), ffn_parts, output_part, gate_logit_grad)
    )
    sums.send((("ffn", 1), ffn_parts[1]))
    ffn_parts[3] = swap_plane(ffn_parts[3], 3, 0)
    query_rot_grad = jnp.einsum(
        "gqk,kd->qgd", score_grad, key_rot, preferred_element_type=jnp.float32
    )
    key_rot_grad = jnp.einsum(
        "gqk,qgd->kd", score_grad, query_rot, preferred_element_type=jnp.float32
    )
    value_grad = jnp.einsum(
        "gqk,qgd->kd",
        soft,
        mixed_grad_heads,
        preferred_element_type=jnp.float32,
    ).astype(jnp.bfloat16)
    key_back, key_gain_grad = norm_back(
        key_raw, key_gain, apply_rotary(key_rot_grad[:, None], position, -1.0)
    )
    query_back, query_gain_grad = norm_back(
        query_raw, query_gain, apply_rotary(query_rot_grad, position, -1.0)
    )
    attn_in_grads = jnp.concatenate(
        [
            query_back.reshape(row_slots, query_width).astype(jnp.bfloat16),
            key_back[:, 0].astype(jnp.bfloat16),
            value_grad,
            gate_logit_grad,
        ],
        axis=1,
    )
    attn_in_grads, ffn_parts, query_gain_grad, key_gain_grad = sums.wait(
        (attn_in_grads, ffn_parts, query_gain_grad, key_gain_grad)
    )
    sums.send((("ffn", 2), ffn_parts[2]))
    one_far = dot_nt(attn_in_grads[half:], attn_weights)
    one_near = dot_nt(attn_in_grads[:half], attn_weights)
    own_part, came_parts, _ = scatter_plane(scatter_half(one_near, one_far))
    attn_parts = {mask: grad_part(first_normed, attn_in_grads, mask) for mask in (2, 3, 1, 0)}
    attn_parts[1] = swap_plane(attn_parts[1], 1, 0)
    own_part, came_parts, attn_parts, hidden_act = sums.wait(
        (own_part, came_parts, attn_parts, hidden_act)
    )
    hops = sum_hops()

    def hop(value):
        axis, pairs = next(hops)
        return value + lax.ppermute(value, axis, pairs)

    sums.send((("ffn", 3), ffn_parts[3]))
    for mask in (2, 3):
        attn_parts[mask] = swap_plane(attn_parts[mask], mask, 0)
    normed_one_grad = scatter_total(own_part, came_parts)
    back_one, gain_one_grad = norm_back(inputs, gain_one, normed_one_grad)
    input_grad = (hidden_total_grad + back_one).astype(jnp.bfloat16)
    gains = jnp.concatenate([gain_one_grad, gain_two_grad, query_gain_grad, key_gain_grad])[None]
    out_far = dot_nn(hidden_act[half:], w_down).astype(jnp.bfloat16)
    out_near = dot_nn(hidden_act[:half], w_down)
    out_half = scatter_half(out_near, out_far)
    input_grad, gains, out_half, attn_parts = sums.wait((input_grad, gains, out_half, attn_parts))
    sums.send((("output",), output_part))
    gains = hop(gains)
    out_own, out_came, _ = scatter_plane(out_half)
    sums.send((("attn", 0), attn_parts[0]))
    gains, out_own, out_came = sums.wait((gains, out_own, out_came), 2)
    sums.send((("attn", 1), attn_parts[1]))
    gains = sums.wait(hop(gains), 2)
    sums.send((("attn", 2), attn_parts[2]))
    layer_output = hidden_in + own_valid * scatter_total(out_own, out_came)
    gains, layer_output = sums.wait((hop(gains)[0], layer_output.astype(jnp.bfloat16)), 2)
    gain_rows = jnp.pad(gains, (0, 8 * attn_parts[3].shape[1] - gains.shape[0]))
    gain_rows = gain_rows.reshape(8, -1).astype(jnp.bfloat16)
    sums.send((("attn", 3), jnp.concatenate([attn_parts[3], gain_rows], axis=0)))
    grad_w_gate, grad_w_up = place_columns(
        [sums.done["ffn", mask] for mask in range(4)], (hidden_width, hidden_width)
    )
    grad_w_down = jnp.concatenate([chosen(sums.done["down", at]) for at in range(2)], axis=0)
    sums.wait((), 2)
    sums.send()
    grad_w_gate, grad_w_up, grad_w_down, input_grad, layer_output = sums.wait(
        (grad_w_gate, grad_w_up, grad_w_down, input_grad, layer_output), 2
    )
    sums.send()
    input_grad, layer_output = swap_ranks(input_grad), swap_ranks(layer_output, True)
    grad_w_output = chosen(sums.done["output",])
    grad_w_output = sums.wait(grad_w_output, 2)
    while any(sums.flight) or sums.arrived:
        sums.send()
        sums.wait((), 2)
    last_sum = chosen([part[-8:] for part in sums.done["attn", 3]])
    sums.done["attn", 3] = [part[:-8] for part in sums.done["attn", 3]]
    gains = last_sum.reshape(-1)[: gains.shape[0]]
    grad_w_query, grad_w_key, grad_w_value, grad_w_out_gate = place_columns(
        [sums.done["attn", mask] for mask in range(4)],
        (query_width, HEAD_SIZE, HEAD_SIZE, query_width),
    )
    model_width = layer_input.shape[1]
    ends = (model_width, 2 * model_width, 2 * model_width + HEAD_SIZE)
    return (
        layer_output,
        input_grad,
        gains[: ends[0]],
        gains[ends[1] : ends[2]],
        gains[ends[2] :],
        grad_w_query,
        grad_w_key,
        grad_w_value,
        grad_w_out_gate,
        grad_w_output,
        gains[ends[0] : ends[1]],
        grad_w_gate,
        grad_w_up,
        grad_w_down,
    )


def solution(mesh):
    sizes = dict(mesh.shape)
    plane = (sizes["fsdp"], sizes["ctx"], sizes["tp"]) == (4, 4, 2)
    return jax.shard_map(
        plane_body if plane else body,
        mesh=mesh,
        in_specs=(
            P(("fsdp", "ctx", "tp"), None),
            P(("fsdp", "ctx", "tp"), None),
            P("fsdp", None),
            P(),
            P(),
            P(),
            P("fsdp", "tp"),
            P("fsdp", "tp"),
            P("fsdp", "tp"),
            P("fsdp", "tp"),
            P(("tp", "fsdp"), None),
            P(),
            P("fsdp", "tp"),
            P("fsdp", "tp"),
            P(("tp", "fsdp"), None),
        ),
        out_specs=(
            P(("fsdp", "ctx", "tp"), None),
            P(("fsdp", "ctx", "tp"), None),
            P(),
            P(),
            P(),
            P("fsdp", "tp"),
            P("fsdp", "tp"),
            P("fsdp", "tp"),
            P("fsdp", "tp"),
            P(("tp", "fsdp"), None),
            P(),
            P("fsdp", "tp"),
            P("fsdp", "tp"),
            P(("tp", "fsdp"), None),
        ),
        check_vma=False,
    )
```

```python
import jax
import jax.numpy as jnp
from jax import lax
from jax.experimental import pallas as pl
from jax.experimental.pallas import tpu as pltpu
from jax.sharding import PartitionSpec as P

HEAD_SIZE = 128


EPSILON = 1e-06
ROPE_BASE = 1000000.0
NEG_FILL = -1e30


def as_sent(value):

    def short(part):
        return part.astype(jnp.bfloat16) if part.dtype == jnp.float32 else part

    return jax.tree.map(short, value)


def apply_rms_norm(values, gain_vec):
    return (
        values * lax.rsqrt(jnp.mean(values * values, axis=-1, keepdims=True) + EPSILON) * gain_vec
    )


def norm_back(values, gain_vec, grad_in):
    row_scale = lax.rsqrt(jnp.mean(values * values, axis=-1, keepdims=True) + EPSILON)
    unit_rows = values * row_scale
    scaled = grad_in * gain_vec
    back_rows = row_scale * (
        scaled - unit_rows * jnp.mean(scaled * unit_rows, axis=-1, keepdims=True)
    )
    gain_grad = jnp.sum((grad_in * unit_rows).reshape(-1, values.shape[-1]), axis=0)
    return (back_rows, gain_grad)


def apply_rotary(values, token_position, direction):
    half_size = values.shape[-1] // 2
    frequency = jnp.power(ROPE_BASE, -jnp.arange(half_size, dtype=jnp.float32) / half_size)
    angle = token_position.astype(jnp.float32)[:, None] * frequency[None, :]
    cosine = jnp.cos(angle)[:, None, :]
    sine = direction * jnp.sin(angle)[:, None, :]
    first_half = values[..., :half_size]
    second_half = values[..., half_size:]
    return jnp.concatenate(
        [first_half * cosine - second_half * sine, second_half * cosine + first_half * sine],
        axis=-1,
    )


def segment_of(slot_ids, lengths):
    first_len = lengths[0, 0]
    second_len = lengths[0, 1]
    return jnp.where(slot_ids < first_len, 0, jnp.where(slot_ids < first_len + second_len, 1, 2))


def position_of(slot_ids, segment, lengths):
    seg_begin = jnp.where(
        segment == 0, 0, jnp.where(segment == 1, lengths[0, 0], lengths[0, 0] + lengths[0, 1])
    )
    return slot_ids - seg_begin


def to_block(local_part):
    return lax.all_gather(local_part, "tp", axis=0, tiled=True)


def to_share(partial_rows):
    return lax.psum_scatter(
        partial_rows.astype(jnp.bfloat16), "tp", scatter_dimension=0, tiled=True
    ).astype(jnp.float32)


def fold_product(left_rows, weight_set):
    pieces = jax.tree.map(
        lambda a: lax.all_gather(a, "fsdp", axis=0, tiled=True), as_sent(weight_set)
    )
    return tuple(
        (
            jnp.dot(left_rows, weight_part, preferred_element_type=jnp.float32)
            for weight_part in pieces
        )
    )


def back_product(grad_rows, weight_set):
    pieces = jax.tree.map(
        lambda a: lax.all_gather(a, "fsdp", axis=0, tiled=True), as_sent(weight_set)
    )
    result = lax.dot_general(
        grad_rows[0], pieces[0], (((1,), (1,)), ((), ())), preferred_element_type=jnp.float32
    )
    for grad_part, weight_part in zip(grad_rows[1:], pieces[1:]):
        result = result + lax.dot_general(
            grad_part, weight_part, (((1,), (1,)), ((), ())), preferred_element_type=jnp.float32
        )
    return result


def weight_grads(left_rows, grad_rows):
    widths = [grad_part.shape[1] for grad_part in grad_rows]
    shared = lax.psum_scatter(
        jnp.concatenate(
            [
                lax.dot_general(
                    left_rows,
                    grad_part,
                    (((0,), (0,)), ((), ())),
                    preferred_element_type=jnp.float32,
                )
                for grad_part in grad_rows
            ],
            axis=1,
        ).astype(jnp.bfloat16),
        "fsdp",
        scatter_dimension=0,
        tiled=True,
    )
    summed = lax.psum(shared, "ctx").astype(jnp.float32)
    pieces = []
    offset = 0
    for column_width in widths:
        pieces.append(summed[:, offset : offset + column_width])
        offset = offset + column_width
    return tuple(pieces)


def body(
    layer_input,
    cotangent,
    lengths,
    attn_norm,
    query_norm_gain,
    k_norm,
    w_query,
    key_weight,
    value_weight,
    w_out_gate,
    w_output,
    ffn_norm,
    w_gate,
    w_up,
    w_down,
):
    local_rows = layer_input.shape[0]
    block_rows = local_rows * lax.axis_size("tp")
    query_heads = w_query.shape[1] // HEAD_SIZE
    kv_heads = key_weight.shape[1] // HEAD_SIZE
    groups = query_heads // kv_heads
    score_scale = HEAD_SIZE ** (-0.5)
    block_first = lax.axis_index("ctx") * block_rows
    own_slots = (
        block_first + lax.axis_index("tp") * local_rows + jnp.arange(local_rows, dtype=jnp.int32)
    )
    own_valid = (segment_of(own_slots, lengths) < 2).astype(jnp.float32)[:, None]
    query_slots = block_first + jnp.arange(block_rows, dtype=jnp.int32)
    query_segment = segment_of(query_slots, lengths)
    query_position = position_of(query_slots, query_segment, lengths)
    inputs = layer_input.astype(jnp.float32)
    gain_one = attn_norm.astype(jnp.float32)
    gain_two = ffn_norm.astype(jnp.float32)
    query_gain = query_norm_gain.astype(jnp.float32)
    key_gain = k_norm.astype(jnp.float32)
    first_normed = to_block(apply_rms_norm(inputs, gain_one).astype(jnp.bfloat16))
    query_rows, key_projected, value_proj, gate_logits = fold_product(
        first_normed, (w_query, key_weight, value_weight, w_out_gate)
    )
    query_heads_raw = query_rows.reshape(block_rows, query_heads, HEAD_SIZE)
    key_heads_raw = key_projected.reshape(block_rows, kv_heads, HEAD_SIZE)
    query_rotated = apply_rotary(
        apply_rms_norm(query_heads_raw, query_gain), query_position, 1.0
    ).astype(jnp.bfloat16)
    key_rot = apply_rotary(apply_rms_norm(key_heads_raw, key_gain), query_position, 1.0).astype(
        jnp.bfloat16
    )
    query_grouped = query_rotated.reshape(block_rows, kv_heads, groups, HEAD_SIZE)
    key_flat = key_rot.reshape(block_rows, kv_heads * HEAD_SIZE)
    value_reduced = value_proj.astype(jnp.bfloat16)

    def key_mask(piece_rows):
        key_slots = jnp.arange(piece_rows, dtype=jnp.int32)
        key_segment = segment_of(key_slots, lengths)
        return (query_segment[:, None] == key_segment[None, :]) & (
            key_slots[None, :] <= query_slots[:, None]
        )

    head_shape = (kv_heads, groups, block_rows)
    running_top = jnp.full(head_shape + (1,), NEG_FILL, jnp.float32)
    key_piece = lax.all_gather(key_flat, "ctx", axis=0, tiled=True)
    value_piece = lax.all_gather(value_reduced, "ctx", axis=0, tiled=True)
    piece_rows = key_piece.shape[0]
    allowed = key_mask(piece_rows)
    raw_scores = jnp.einsum(
        "qhgd,khd->hgqk",
        query_grouped,
        key_piece.reshape(piece_rows, kv_heads, HEAD_SIZE),
        preferred_element_type=jnp.float32,
    )
    scores = jnp.where(allowed, raw_scores * score_scale, NEG_FILL)
    new_top = jnp.maximum(running_top, jnp.max(scores, axis=-1, keepdims=True))
    weights = jnp.where(allowed, jnp.exp(scores - new_top), 0.0)
    running_total = jnp.sum(weights, axis=-1, keepdims=True)
    mixed_sum = jnp.einsum(
        "hgqk,khd->hgqd",
        weights.astype(jnp.bfloat16),
        value_piece.reshape(piece_rows, kv_heads, HEAD_SIZE),
        preferred_element_type=jnp.float32,
    )
    mixed_sum, running_top, running_total = (mixed_sum, new_top, running_total)
    log_total = running_top + jnp.log(running_total)
    attended = jnp.transpose(mixed_sum / running_total, (2, 0, 1, 3))
    attended_rows = attended.reshape(block_rows, query_heads * HEAD_SIZE)
    gate_sig = jax.nn.sigmoid(gate_logits)
    gated_mix = (attended_rows * gate_sig).astype(jnp.bfloat16)
    attn_share = to_share(fold_product(gated_mix, (w_output,))[0])
    hidden_in = inputs + own_valid * attn_share
    normed_two = to_block(apply_rms_norm(hidden_in, gain_two).astype(jnp.bfloat16))
    gate_pre, up_pre = fold_product(normed_two, (w_gate, w_up))
    gate_sigmoid = jax.nn.sigmoid(gate_pre)
    activated = gate_pre * gate_sigmoid
    hidden_act = (activated * up_pre).astype(jnp.bfloat16)
    ffn_share = to_share(fold_product(hidden_act, (w_down,))[0])
    layer_output = (hidden_in + own_valid * ffn_share).astype(jnp.bfloat16)
    out_grad = cotangent.astype(jnp.float32) * own_valid
    ffn_grad = to_block(out_grad.astype(jnp.bfloat16))
    hidden_grad = back_product((ffn_grad,), (w_down,))
    grad_w_down = weight_grads(hidden_act, (ffn_grad,))[0]
    gate_grad = (
        hidden_grad * up_pre * gate_sigmoid * (1.0 + gate_pre * (1.0 - gate_sigmoid))
    ).astype(jnp.bfloat16)
    up_grad = (hidden_grad * activated).astype(jnp.bfloat16)
    normed_two_grad = to_share(back_product((gate_grad, up_grad), (w_gate, w_up)))
    grad_w_gate, grad_w_up = weight_grads(normed_two, (gate_grad, up_grad))
    back_two, gain_two_grad = norm_back(hidden_in, gain_two, normed_two_grad)
    hidden_total_grad = out_grad + back_two
    attn_grad = to_block((own_valid * hidden_total_grad).astype(jnp.bfloat16))
    gated_grad = back_product((attn_grad,), (w_output,))
    grad_w_output = weight_grads(gated_mix, (attn_grad,))[0]
    mixed_grad = (gated_grad * gate_sig).astype(jnp.bfloat16)
    gate_logit_grad = (gated_grad * attended_rows * gate_sig * (1.0 - gate_sig)).astype(
        jnp.bfloat16
    )
    mixed_grad_heads = mixed_grad.reshape(block_rows, kv_heads, groups, HEAD_SIZE)
    delta_rows = jnp.transpose(
        jnp.sum(mixed_grad_heads.astype(jnp.float32) * attended, axis=-1), (1, 2, 0)
    )[..., None]
    key_piece = lax.all_gather(key_flat, "ctx", axis=0, tiled=True)
    value_piece = lax.all_gather(value_reduced, "ctx", axis=0, tiled=True)
    piece_rows = key_piece.shape[0]
    key_view = key_piece.reshape(piece_rows, kv_heads, HEAD_SIZE)
    value_view = value_piece.reshape(piece_rows, kv_heads, HEAD_SIZE)
    allowed = key_mask(piece_rows)
    raw_scores = jnp.einsum(
        "qhgd,khd->hgqk", query_grouped, key_view, preferred_element_type=jnp.float32
    )
    soft_vals = jnp.where(allowed, jnp.exp(raw_scores * score_scale - log_total), 0.0)
    prob_grad = jnp.einsum(
        "qhgd,khd->hgqk", mixed_grad_heads, value_view, preferred_element_type=jnp.float32
    )
    score_grad = (soft_vals * (prob_grad - delta_rows) * score_scale).astype(jnp.bfloat16)
    query_acc = jnp.einsum(
        "hgqk,khd->qhgd", score_grad, key_view, preferred_element_type=jnp.float32
    )
    key_part = jnp.einsum(
        "hgqk,qhgd->khd", score_grad, query_grouped, preferred_element_type=jnp.float32
    ).reshape(piece_rows, kv_heads * HEAD_SIZE)
    value_part = jnp.einsum(
        "hgqk,qhgd->khd",
        soft_vals.astype(jnp.bfloat16),
        mixed_grad_heads,
        preferred_element_type=jnp.float32,
    ).reshape(piece_rows, kv_heads * HEAD_SIZE)
    kv_acc = jnp.concatenate([key_part, value_part], axis=1)
    query_acc, kv_acc = (query_acc, kv_acc)
    kv_own = lax.psum_scatter(
        kv_acc.astype(jnp.bfloat16), "ctx", scatter_dimension=0, tiled=True
    ).astype(jnp.float32)
    key_rot_grad = kv_own[:, : kv_heads * HEAD_SIZE].reshape(block_rows, kv_heads, HEAD_SIZE)
    value_grad = kv_own[:, kv_heads * HEAD_SIZE :].astype(jnp.bfloat16)
    key_back, key_gain_grad = norm_back(
        key_heads_raw, key_gain, apply_rotary(key_rot_grad, query_position, -1.0)
    )
    query_back, query_gain_grad = norm_back(
        query_heads_raw,
        query_gain,
        apply_rotary(query_acc.reshape(block_rows, query_heads, HEAD_SIZE), query_position, -1.0),
    )
    query_grad = query_back.reshape(block_rows, query_heads * HEAD_SIZE).astype(jnp.bfloat16)
    key_grad = key_back.reshape(block_rows, kv_heads * HEAD_SIZE).astype(jnp.bfloat16)
    attn_in_grads = (query_grad, key_grad, value_grad, gate_logit_grad)
    normed_one_grad = to_share(
        back_product(attn_in_grads, (w_query, key_weight, value_weight, w_out_gate))
    )
    grad_w_query, grad_w_key, grad_w_value, grad_w_out_gate = weight_grads(
        first_normed, attn_in_grads
    )
    back_one, gain_one_grad = norm_back(inputs, gain_one, normed_one_grad)
    input_grad = (hidden_total_grad + back_one).astype(jnp.bfloat16)
    gain_totals = lax.psum(
        (gain_one_grad, query_gain_grad, key_gain_grad, gain_two_grad), ("fsdp", "ctx", "tp")
    )
    return (
        layer_output,
        input_grad,
        gain_totals[0],
        gain_totals[1],
        gain_totals[2],
        grad_w_query,
        grad_w_key,
        grad_w_value,
        grad_w_out_gate,
        grad_w_output,
        gain_totals[3],
        grad_w_gate,
        grad_w_up,
        grad_w_down,
    )


def xor_pairs(count, mask):
    return [(i, i ^ mask) for i in range(count)]


def swap_plane(value, fsdp_mask, tp_mask):
    fsdp_size, tp_size = lax.axis_size("fsdp"), lax.axis_size("tp")
    if tp_mask == 0:
        return lax.ppermute(value, "fsdp", xor_pairs(fsdp_size, fsdp_mask))
    if fsdp_mask == 0:
        return lax.ppermute(value, "tp", xor_pairs(tp_size, tp_mask))
    return lax.ppermute(
        value,
        ("fsdp", "tp"),
        xor_pairs(fsdp_size * tp_size, fsdp_mask * tp_size + tp_mask),
    )


def swap_ranks(value, mask=0):
    size = lax.axis_size("fsdp")
    pairs = [(a * size + b, b * size + (a ^ mask)) for a in range(size) for b in range(size)]
    return lax.ppermute(value, ("fsdp", "ctx"), pairs)


PIECES = ((0, 0), (0, 1), (2, 0), (2, 1))


def plane_beside(own):
    return own, swap_plane(own, 0, 1), swap_plane(own, 2, 0)


def plane_near(beside):
    own, over_tp, over_x = beside
    rows = own.shape[0] // 2
    three = jnp.concatenate([own, over_tp, over_x], axis=0)
    corner = [swap_plane(over_x[:rows], 0, 1), swap_plane(over_tp[rows:], 2, 0)]
    return three, swap_plane(three, 1, 0), jnp.concatenate(corner, axis=0)


def plane_join(near):
    three, three_far, corner = near
    return jnp.concatenate([three, corner, three_far, swap_plane(corner, 1, 0)], axis=0)


def scatter_half(near_part, far_part):
    return near_part + swap_plane(far_part.astype(jnp.bfloat16), 1, 0).astype(jnp.float32)


def scatter_plane(half, beside=()):
    rows = half.shape[0] // 8
    piece = [half[at * rows : (at + 1) * rows] for at in range(8)]

    def sent(parts, *masks):
        low = jnp.concatenate(parts, axis=0).astype(jnp.bfloat16)
        return swap_plane(low, *masks)

    by_x = sent([piece[4], piece[6]], 2, 0)
    by_tp = sent([piece[3], piece[7]], 0, 1)
    by_x, by_tp, beside = lax.optimization_barrier((by_x, by_tp, beside))
    by_x, by_tp = by_x.astype(jnp.float32), by_tp.astype(jnp.float32)
    top = sent([piece[2] + by_x[rows:]], 0, 1)
    bottom = sent([piece[5] + by_tp[rows:]], 2, 0)
    return jnp.concatenate([piece[0] + by_x[:rows], piece[1] + by_tp[:rows]], axis=0), [top, bottom], beside


def scatter_total(own, came):
    return own + jnp.concatenate(came, axis=0).astype(jnp.float32)


def dot_nn(a, b):
    return jnp.dot(a, b, preferred_element_type=jnp.float32)


def dot_nt(a, b):
    return lax.dot_general(a, b, (((1,), (1,)), ((), ())), preferred_element_type=jnp.float32)


def dot_tn(a, b):
    return lax.dot_general(a, b, (((0,), (0,)), ((), ())), preferred_element_type=jnp.float32)


INWARD, ACROSS, OUTWARD = [(0, 1), (3, 2)], [(1, 2), (2, 1)], [(1, 0), (2, 3)]


class CtxSums:
    def __init__(self):
        self.flight, self.arrived, self.done = [], [], {}

    def send(self, *fresh):
        place = lax.axis_index("ctx")
        inner = (place == 1) | (place == 2)
        sent, totals, fresh = [], [], list(fresh)
        for stage, name, here, came in self.arrived:
            if stage == 2:
                self.done[name] = here, came
                continue
            both = (here.astype(jnp.float32) + came.astype(jnp.float32)).astype(jnp.bfloat16)
            if stage:
                totals.append((name, both))
            else:
                sent.append(([(1, name, both)], lax.ppermute(both, "ctx", ACROSS)))
        while totals and fresh and totals[0][1].shape == fresh[0][1].shape:
            (out, total), (name, part) = totals.pop(0), fresh.pop(0)
            moved = swap_ctx(jnp.where(inner, total, part))
            sent.append(([(0, name, part), (2, out, total)], moved))
        for name, part in fresh:
            sent.append(([(0, name, part)], lax.ppermute(part, "ctx", INWARD)))
        for name, total in totals:
            sent.append(([(2, name, total)], lax.ppermute(total, "ctx", OUTWARD)))
        self.arrived = []
        self.flight.append(sent)

    def wait(self, kept, depth=1):
        old = []
        while len(self.flight) >= depth:
            old += self.flight.pop(0)
        heres = [[here for _, _, here in entry[0]] for entry in old]
        moved = [entry[1] for entry in old]
        heres, moved, kept = lax.optimization_barrier((heres, moved, kept))
        self.arrived = [
            (stage, name, here, came)
            for entry, parts, came in zip(old, heres, moved)
            for (stage, name, _), here in zip(entry[0], parts)
        ]
        return kept


def sum_hops():
    for axis, mask in (("fsdp", 1), ("fsdp", 2), ("tp", 1)):
        yield axis, xor_pairs(lax.axis_size(axis), mask)


def weight_columns(weights, owner):
    parts = []
    for weight in weights:
        width = weight.shape[1] // lax.axis_size("fsdp")
        parts.append(lax.dynamic_slice_in_dim(weight, owner * width, width, 1))
    return jnp.concatenate(parts, axis=1)


class Fetch:
    def __init__(self, weights):
        self.me, self.size = lax.axis_index("fsdp"), lax.axis_size("fsdp")
        self.side = lax.axis_index("ctx") % 2
        self.rows = weights[0].shape[0]
        self.half = self.rows // 2
        mine = [
            lax.dynamic_slice_in_dim(weight, self.side * self.half, self.half, 0)
            for weight in weights
        ]
        self.columns = [weight_columns(mine, self.me ^ mask) for mask in (2, 3)]
        self.own = weight_columns(weights, self.me)
        self.core = weight_columns(weights, self.me ^ 1)

    def along_x(self, at):
        return swap_plane(self.columns[at], (2, 3)[at], 0)

    def along_core(self):
        return swap_plane(self.core, 1, 0)

    def begin(self, core):
        whole = jnp.zeros((self.rows * self.size, self.own.shape[1]), self.own.dtype)
        for part, peer in ((self.own, self.me), (core, self.me ^ 1)):
            whole = lax.dynamic_update_slice_in_dim(whole, part, peer * self.rows, 0)
        return whole

    def add(self, whole, at, came, other):
        start = (self.me ^ (2, 3)[at]) * self.rows
        whole = lax.dynamic_update_slice_in_dim(whole, came, start + self.side * self.half, 0)
        return lax.dynamic_update_slice_in_dim(
            whole, other, start + (1 - self.side) * self.half, 0
        )


def swap_ctx(value):
    return lax.ppermute(value, "ctx", xor_pairs(lax.axis_size("ctx"), 1))


def grad_part(left, right, mask):
    owner = lax.axis_index("fsdp") ^ mask
    rows = left.shape[1] // lax.axis_size("fsdp")
    columns = lax.dynamic_slice_in_dim(left, owner * rows, rows, 1)
    return dot_tn(columns, right).astype(jnp.bfloat16)


def at_inner():
    place = lax.axis_index("ctx")
    return (place == 1) | (place == 2)


def chosen(pair):
    return jnp.where(at_inner(), *pair).astype(jnp.float32)


def place_columns(pairs, widths):
    size, rows, block = lax.axis_size("fsdp"), pairs[0][0].shape[0], 128
    scalars = jnp.stack([lax.axis_index("fsdp"), at_inner().astype(jnp.int32)])

    def kernel(scalars, *refs):
        parts, outs = refs[: 2 * size], refs[2 * size :]
        for mask in range(size):
            here, came = parts[2 * mask], parts[2 * mask + 1]
            value = jnp.where(
                scalars[1] == 1, here[...].astype(jnp.float32), came[...].astype(jnp.float32)
            )
            start = 0
            for out, width in zip(outs, widths):
                column = pl.multiple_of((scalars[0] ^ mask) * width, 128)
                out[:, pl.ds(column, width)] = value[:, start : start + width]
                start += width

    total = sum(widths)
    return pl.pallas_call(
        kernel,
        grid_spec=pltpu.PrefetchScalarGridSpec(
            num_scalar_prefetch=1,
            grid=(rows // block,),
            in_specs=[pl.BlockSpec((block, total), lambda i, _: (i, 0))] * (2 * size),
            out_specs=[pl.BlockSpec((block, width * size), lambda i, _: (i, 0)) for width in widths],
        ),
        out_shape=[jax.ShapeDtypeStruct((rows, width * size), jnp.float32) for width in widths],
        cost_estimate=pl.CostEstimate(
            flops=0, transcendentals=0, bytes_accessed=8 * rows * total * size
        ),
    )(scalars, *(part for pair in pairs for part in pair))


def plane_body(
    layer_input,
    cotangent,
    lengths,
    attn_norm,
    query_norm_gain,
    k_norm,
    w_query,
    key_weight,
    value_weight,
    w_out_gate,
    w_output,
    ffn_norm,
    w_gate,
    w_up,
    w_down,
):
    fsdp_size, tp_size = lax.axis_size("fsdp"), lax.axis_size("tp")
    fsdp_at, tp_at = lax.axis_index("fsdp"), lax.axis_index("tp")
    local_rows = layer_input.shape[0]
    row_slots = local_rows * fsdp_size * tp_size
    query_heads = w_query.shape[1] // HEAD_SIZE // fsdp_size
    query_width = query_heads * HEAD_SIZE
    score_scale = HEAD_SIZE ** (-0.5)
    gain_one = attn_norm.astype(jnp.float32)
    gain_two = ffn_norm.astype(jnp.float32)
    query_gain = query_norm_gain.astype(jnp.float32)
    key_gain = k_norm.astype(jnp.float32)

    together = lax.optimization_barrier
    input_low = swap_ranks(layer_input)
    attn_fetch = Fetch((w_query, key_weight, value_weight, w_out_gate))
    attn_came = [attn_fetch.along_x(at) for at in range(2)]
    attn_core = attn_fetch.along_core()
    lengths = swap_ranks(lengths)
    input_low, attn_came, cotangent = together((input_low, attn_came, cotangent))
    inputs = input_low.astype(jnp.float32)

    def slots_of(fsdp_index, tp_index):
        return (fsdp_index * tp_size + tp_index) * local_rows + jnp.arange(
            local_rows, dtype=jnp.int32
        )

    own_slots = slots_of(fsdp_at, tp_at)
    own_valid = (segment_of(own_slots, lengths) < 2).astype(jnp.float32)[:, None]
    slots = jnp.concatenate(
        [
            slots_of(fsdp_at ^ fsdp_mask ^ core, tp_at ^ tp_mask)
            for core in (0, 1)
            for fsdp_mask, tp_mask in PIECES
        ]
    )
    segment = segment_of(slots, lengths)
    position = position_of(slots, segment, lengths)

    first_own = apply_rms_norm(inputs, gain_one).astype(jnp.bfloat16)
    first_beside = plane_beside(first_own)
    attn_other = [swap_ctx(came) for came in attn_came]
    cot_low = swap_ranks(cotangent)
    attn_weights = attn_fetch.begin(attn_core)
    first_beside, attn_other, attn_weights = together((first_beside, attn_other, attn_weights))
    first_near = plane_near(first_beside)
    for at in range(2):
        attn_weights = attn_fetch.add(attn_weights, at, attn_came[at], attn_other[at])
    ffn_fetch = Fetch((w_gate, w_up))
    ffn_columns = (ffn_fetch.columns, ffn_fetch.core)
    first_near, attn_weights, ffn_columns = together((first_near, attn_weights, ffn_columns))
    ffn_fetch.columns, ffn_fetch.core = ffn_columns
    ffn_came = [ffn_fetch.along_x(at) for at in range(2)]
    ffn_core = ffn_fetch.along_core()
    first_normed = plane_join(first_near)

    projected = dot_nn(first_normed, attn_weights)
    query_raw = projected[:, :query_width].reshape(row_slots, query_heads, HEAD_SIZE)
    key_raw = projected[:, query_width : query_width + HEAD_SIZE].reshape(row_slots, 1, HEAD_SIZE)
    value_low = projected[:, query_width + HEAD_SIZE : query_width + 2 * HEAD_SIZE].astype(
        jnp.bfloat16
    )
    gate_logits = projected[:, query_width + 2 * HEAD_SIZE :]
    query_rot = apply_rotary(apply_rms_norm(query_raw, query_gain), position, 1.0).astype(
        jnp.bfloat16
    )
    key_rot = apply_rotary(apply_rms_norm(key_raw, key_gain), position, 1.0).astype(jnp.bfloat16)[
        :, 0
    ]

    query_rot, key_rot, value_low, ffn_came[0], cot_low = together(
        (query_rot, key_rot, value_low, ffn_came[0], cot_low)
    )
    ffn_other = swap_ctx(ffn_came[0])
    out_grad = cot_low.astype(jnp.float32) * own_valid
    cot_beside = plane_beside(out_grad.astype(jnp.bfloat16))

    allowed = (segment[:, None] == segment[None, :]) & (slots[None, :] <= slots[:, None])
    raw_scores = jnp.einsum("qgd,kd->gqk", query_rot, key_rot, preferred_element_type=jnp.float32)
    scores = jnp.where(allowed, raw_scores * score_scale, NEG_FILL)
    top = jnp.max(scores, axis=-1, keepdims=True)
    weights = jnp.where(allowed, jnp.exp(scores - top), 0.0)
    total = jnp.sum(weights, axis=-1, keepdims=True)
    mixed = jnp.einsum(
        "gqk,kd->gqd", weights.astype(jnp.bfloat16), value_low, preferred_element_type=jnp.float32
    )
    log_total = top + jnp.log(total)
    attended = jnp.transpose(mixed / total, (1, 0, 2))
    attended_rows = attended.reshape(row_slots, query_width)
    gate_sig = jax.nn.sigmoid(gate_logits)
    gated_mix = (attended_rows * gate_sig).astype(jnp.bfloat16)
    gated_mix, ffn_came, cot_beside, ffn_other = together(
        (gated_mix, ffn_came, cot_beside, ffn_other)
    )
    ffn_others = [ffn_other, swap_ctx(ffn_came[1])]
    half = row_slots // 2
    far_part = dot_nn(gated_mix[half:], w_output)
    near_part = dot_nn(gated_mix[:half], w_output)
    own_part, came_parts, ffn_others[1] = scatter_plane(
        scatter_half(near_part, far_part), ffn_others[1]
    )
    ffn_weights = ffn_fetch.begin(ffn_core)
    ffn_weights = ffn_fetch.add(ffn_weights, 0, ffn_came[0], ffn_others[0])
    cot_near = plane_near(cot_beside)
    own_part, came_parts, cot_near, ffn_others, ffn_weights, ffn_came = together(
        (own_part, came_parts, cot_near, ffn_others, ffn_weights, ffn_came)
    )
    ffn_grad = plane_join(cot_near)
    hidden_in = inputs + own_valid * scatter_total(own_part, came_parts)
    second_near = plane_near(
        plane_beside(apply_rms_norm(hidden_in, gain_two).astype(jnp.bfloat16))
    )
    ffn_weights = ffn_fetch.add(ffn_weights, 1, ffn_came[1], ffn_others[1])
    second_near, ffn_grad, ffn_weights = together((second_near, ffn_grad, ffn_weights))
    normed_two = plane_join(second_near)

    hidden_grad = dot_nt(ffn_grad, w_down)
    pre = dot_nn(normed_two, ffn_weights)
    hidden_width = w_down.shape[0]
    gate_pre, up_pre = pre[:, :hidden_width], pre[:, hidden_width:]
    gate_sigmoid = jax.nn.sigmoid(gate_pre)
    activated = gate_pre * gate_sigmoid
    hidden_act = (activated * up_pre).astype(jnp.bfloat16)
    gate_grad = (
        hidden_grad * up_pre * gate_sigmoid * (1.0 + gate_pre * (1.0 - gate_sigmoid))
    ).astype(jnp.bfloat16)
    up_grad = (hidden_grad * activated).astype(jnp.bfloat16)
    ffn_in_grads = jnp.concatenate([gate_grad, up_grad], axis=1)

    sums = CtxSums()
    down_parts = jnp.split(dot_tn(hidden_act, ffn_grad).astype(jnp.bfloat16), 2, axis=0)
    down_parts, hidden_act, ffn_in_grads, normed_two = together(
        (down_parts, hidden_act, ffn_in_grads, normed_two)
    )
    sums.send((("down", 0), down_parts[0]))
    two_far = dot_nt(ffn_in_grads[half:], ffn_weights)
    two_near = dot_nt(ffn_in_grads[:half], ffn_weights)
    own_part, came_parts, _ = scatter_plane(scatter_half(two_near, two_far))
    own_part, came_parts, hidden_act, ffn_in_grads, normed_two = sums.wait(
        (own_part, came_parts, hidden_act, ffn_in_grads, normed_two)
    )
    sums.send((("down", 1), down_parts[1]))
    normed_two_grad = scatter_total(own_part, came_parts)
    back_two, gain_two_grad = norm_back(hidden_in, gain_two, normed_two_grad)
    hidden_total_grad = out_grad + back_two
    attn_near = plane_near(plane_beside((own_valid * hidden_total_grad).astype(jnp.bfloat16)))
    ffn_parts = {mask: grad_part(normed_two, ffn_in_grads, mask) for mask in (1, 0, 2, 3)}
    ffn_parts[1] = swap_plane(ffn_parts[1], 1, 0)
    attn_near, ffn_parts, hidden_act, query_rot = sums.wait(
        (attn_near, ffn_parts, hidden_act, query_rot)
    )
    sums.send((("ffn", 0), ffn_parts[0]))
    ffn_parts[2] = swap_plane(ffn_parts[2], 2, 0)
    attn_grad = plane_join(attn_near)
    gated_grad = dot_nt(attn_grad, w_output)
    output_part = dot_tn(gated_mix, attn_grad).astype(jnp.bfloat16)
    mixed_grad = (gated_grad * gate_sig).astype(jnp.bfloat16)
    gate_logit_grad = (gated_grad * attended_rows * gate_sig * (1.0 - gate_sig)).astype(
        jnp.bfloat16
    )
    mixed_grad_heads = mixed_grad.reshape(row_slots, query_heads, HEAD_SIZE)
    delta_rows = jnp.transpose(
        jnp.sum(mixed_grad_heads.astype(jnp.float32) * attended, axis=-1), (1, 0)
    )[..., None]
    raw_again = jnp.einsum("qgd,kd->gqk", query_rot, key_rot, preferred_element_type=jnp.float32)
    soft = jnp.where(allowed, jnp.exp(raw_again * score_scale - log_total), 0.0)
    prob_grad = jnp.einsum(
        "qgd,kd->gqk", mixed_grad_heads, value_low, preferred_element_type=jnp.float32
    )
    score_grad = (soft * (prob_grad - delta_rows) * score_scale).astype(jnp.bfloat16)
    score_grad, soft, ffn_parts, output_part, gate_logit_grad = sums.wait(
        (score_grad, soft.astype(jnp.bfloat16), ffn_parts, output_part, gate_logit_grad)
    )
    sums.send((("ffn", 1), ffn_parts[1]))
    ffn_parts[3] = swap_plane(ffn_parts[3], 3, 0)
    query_rot_grad = jnp.einsum(
        "gqk,kd->qgd", score_grad, key_rot, preferred_element_type=jnp.float32
    )
    key_rot_grad = jnp.einsum(
        "gqk,qgd->kd", score_grad, query_rot, preferred_element_type=jnp.float32
    )
    value_grad = jnp.einsum(
        "gqk,qgd->kd",
        soft,
        mixed_grad_heads,
        preferred_element_type=jnp.float32,
    ).astype(jnp.bfloat16)
    key_back, key_gain_grad = norm_back(
        key_raw, key_gain, apply_rotary(key_rot_grad[:, None], position, -1.0)
    )
    query_back, query_gain_grad = norm_back(
        query_raw, query_gain, apply_rotary(query_rot_grad, position, -1.0)
    )
    attn_in_grads = jnp.concatenate(
        [
            query_back.reshape(row_slots, query_width).astype(jnp.bfloat16),
            key_back[:, 0].astype(jnp.bfloat16),
            value_grad,
            gate_logit_grad,
        ],
        axis=1,
    )
    attn_in_grads, ffn_parts, query_gain_grad, key_gain_grad = sums.wait(
        (attn_in_grads, ffn_parts, query_gain_grad, key_gain_grad)
    )
    sums.send((("ffn", 2), ffn_parts[2]))
    one_far = dot_nt(attn_in_grads[half:], attn_weights)
    one_near = dot_nt(attn_in_grads[:half], attn_weights)
    own_part, came_parts, _ = scatter_plane(scatter_half(one_near, one_far))
    attn_parts = {mask: grad_part(first_normed, attn_in_grads, mask) for mask in (2, 3, 1, 0)}
    attn_parts[1] = swap_plane(attn_parts[1], 1, 0)
    own_part, came_parts, attn_parts, hidden_act = sums.wait(
        (own_part, came_parts, attn_parts, hidden_act)
    )
    hops = sum_hops()

    def hop(value):
        axis, pairs = next(hops)
        return value + lax.ppermute(value, axis, pairs)

    sums.send((("ffn", 3), ffn_parts[3]))
    for mask in (2, 3):
        attn_parts[mask] = swap_plane(attn_parts[mask], mask, 0)
    normed_one_grad = scatter_total(own_part, came_parts)
    back_one, gain_one_grad = norm_back(inputs, gain_one, normed_one_grad)
    input_grad = (hidden_total_grad + back_one).astype(jnp.bfloat16)
    gains = jnp.concatenate([gain_one_grad, gain_two_grad, query_gain_grad, key_gain_grad])[None]
    out_far = dot_nn(hidden_act[half:], w_down).astype(jnp.bfloat16)
    out_near = dot_nn(hidden_act[:half], w_down)
    out_half = scatter_half(out_near, out_far)
    input_grad, gains, out_half, attn_parts = sums.wait((input_grad, gains, out_half, attn_parts))
    sums.send((("output",), output_part))
    gains = hop(gains)
    out_own, out_came, _ = scatter_plane(out_half)
    sums.send((("attn", 0), attn_parts[0]))
    gains, out_own, out_came = sums.wait((gains, out_own, out_came), 2)
    sums.send((("attn", 1), attn_parts[1]))
    gains = sums.wait(hop(gains), 2)
    sums.send((("attn", 2), attn_parts[2]))
    layer_output = hidden_in + own_valid * scatter_total(out_own, out_came)
    gains, layer_output = sums.wait((hop(gains)[0], layer_output.astype(jnp.bfloat16)), 2)
    gain_rows = jnp.pad(gains, (0, 8 * attn_parts[3].shape[1] - gains.shape[0]))
    gain_rows = gain_rows.reshape(8, -1).astype(jnp.bfloat16)
    sums.send((("attn", 3), jnp.concatenate([attn_parts[3], gain_rows], axis=0)))
    grad_w_gate, grad_w_up = place_columns(
        [sums.done["ffn", mask] for mask in range(4)], (hidden_width, hidden_width)
    )
    grad_w_down = jnp.concatenate([chosen(sums.done["down", at]) for at in range(2)], axis=0)
    layer_output = sums.wait(swap_plane(layer_output, 2, 0), 2)
    sums.send()
    grad_w_gate, grad_w_up, grad_w_down, input_grad, layer_output = sums.wait(
        (grad_w_gate, grad_w_up, grad_w_down, input_grad, layer_output), 2
    )
    sums.send()
    input_grad, layer_output = swap_ranks(input_grad), swap_ranks(layer_output, 2)
    grad_w_output = chosen(sums.done["output",])
    grad_w_output = sums.wait(grad_w_output, 2)
    sums.send()
    input_grad, layer_output = sums.wait((input_grad, layer_output))
    while any(sums.flight) or sums.arrived:
        sums.send()
        sums.wait((), 2)
    last_sum = chosen([part[-8:] for part in sums.done["attn", 3]])
    sums.done["attn", 3] = [part[:-8] for part in sums.done["attn", 3]]
    gains = last_sum.reshape(-1)[: gains.shape[0]]
    grad_w_query, grad_w_key, grad_w_value, grad_w_out_gate = place_columns(
        [sums.done["attn", mask] for mask in range(4)],
        (query_width, HEAD_SIZE, HEAD_SIZE, query_width),
    )
    model_width = layer_input.shape[1]
    ends = (model_width, 2 * model_width, 2 * model_width + HEAD_SIZE)
    return (
        layer_output,
        input_grad,
        gains[: ends[0]],
        gains[ends[1] : ends[2]],
        gains[ends[2] :],
        grad_w_query,
        grad_w_key,
        grad_w_value,
        grad_w_out_gate,
        grad_w_output,
        gains[ends[0] : ends[1]],
        grad_w_gate,
        grad_w_up,
        grad_w_down,
    )


def solution(mesh):
    sizes = dict(mesh.shape)
    plane = (sizes["fsdp"], sizes["ctx"], sizes["tp"]) == (4, 4, 2)
    return jax.shard_map(
        plane_body if plane else body,
        mesh=mesh,
        in_specs=(
            P(("fsdp", "ctx", "tp"), None),
            P(("fsdp", "ctx", "tp"), None),
            P("fsdp", None),
            P(),
            P(),
            P(),
            P("fsdp", "tp"),
            P("fsdp", "tp"),
            P("fsdp", "tp"),
            P("fsdp", "tp"),
            P(("tp", "fsdp"), None),
            P(),
            P("fsdp", "tp"),
            P("fsdp", "tp"),
            P(("tp", "fsdp"), None),
        ),
        out_specs=(
            P(("fsdp", "ctx", "tp"), None),
            P(("fsdp", "ctx", "tp"), None),
            P(),
            P(),
            P(),
            P("fsdp", "tp"),
            P("fsdp", "tp"),
            P("fsdp", "tp"),
            P("fsdp", "tp"),
            P(("tp", "fsdp"), None),
            P(),
            P("fsdp", "tp"),
            P("fsdp", "tp"),
            P(("tp", "fsdp"), None),
        ),
        check_vma=False,
    )
```

```python
import jax
import jax.numpy as jnp
from jax import lax
from jax.experimental import pallas as pl
from jax.experimental.pallas import tpu as pltpu
from jax.sharding import PartitionSpec as P

HEAD_SIZE = 128


EPSILON = 1e-06
ROPE_BASE = 1000000.0
NEG_FILL = -1e30


def as_sent(value):

    def short(part):
        return part.astype(jnp.bfloat16) if part.dtype == jnp.float32 else part

    return jax.tree.map(short, value)


def apply_rms_norm(values, gain_vec):
    return (
        values * lax.rsqrt(jnp.mean(values * values, axis=-1, keepdims=True) + EPSILON) * gain_vec
    )


def norm_back(values, gain_vec, grad_in):
    row_scale = lax.rsqrt(jnp.mean(values * values, axis=-1, keepdims=True) + EPSILON)
    unit_rows = values * row_scale
    scaled = grad_in * gain_vec
    back_rows = row_scale * (
        scaled - unit_rows * jnp.mean(scaled * unit_rows, axis=-1, keepdims=True)
    )
    gain_grad = jnp.sum((grad_in * unit_rows).reshape(-1, values.shape[-1]), axis=0)
    return (back_rows, gain_grad)


def apply_rotary(values, token_position, direction):
    half_size = values.shape[-1] // 2
    frequency = jnp.power(ROPE_BASE, -jnp.arange(half_size, dtype=jnp.float32) / half_size)
    angle = token_position.astype(jnp.float32)[:, None] * frequency[None, :]
    cosine = jnp.cos(angle)[:, None, :]
    sine = direction * jnp.sin(angle)[:, None, :]
    first_half = values[..., :half_size]
    second_half = values[..., half_size:]
    return jnp.concatenate(
        [first_half * cosine - second_half * sine, second_half * cosine + first_half * sine],
        axis=-1,
    )


def segment_of(slot_ids, lengths):
    first_len = lengths[0, 0]
    second_len = lengths[0, 1]
    return jnp.where(slot_ids < first_len, 0, jnp.where(slot_ids < first_len + second_len, 1, 2))


def position_of(slot_ids, segment, lengths):
    seg_begin = jnp.where(
        segment == 0, 0, jnp.where(segment == 1, lengths[0, 0], lengths[0, 0] + lengths[0, 1])
    )
    return slot_ids - seg_begin


def to_block(local_part):
    return lax.all_gather(local_part, "tp", axis=0, tiled=True)


def to_share(partial_rows):
    return lax.psum_scatter(
        partial_rows.astype(jnp.bfloat16), "tp", scatter_dimension=0, tiled=True
    ).astype(jnp.float32)


def fold_product(left_rows, weight_set):
    pieces = jax.tree.map(
        lambda a: lax.all_gather(a, "fsdp", axis=0, tiled=True), as_sent(weight_set)
    )
    return tuple(
        (
            jnp.dot(left_rows, weight_part, preferred_element_type=jnp.float32)
            for weight_part in pieces
        )
    )


def back_product(grad_rows, weight_set):
    pieces = jax.tree.map(
        lambda a: lax.all_gather(a, "fsdp", axis=0, tiled=True), as_sent(weight_set)
    )
    result = lax.dot_general(
        grad_rows[0], pieces[0], (((1,), (1,)), ((), ())), preferred_element_type=jnp.float32
    )
    for grad_part, weight_part in zip(grad_rows[1:], pieces[1:]):
        result = result + lax.dot_general(
            grad_part, weight_part, (((1,), (1,)), ((), ())), preferred_element_type=jnp.float32
        )
    return result


def weight_grads(left_rows, grad_rows):
    widths = [grad_part.shape[1] for grad_part in grad_rows]
    shared = lax.psum_scatter(
        jnp.concatenate(
            [
                lax.dot_general(
                    left_rows,
                    grad_part,
                    (((0,), (0,)), ((), ())),
                    preferred_element_type=jnp.float32,
                )
                for grad_part in grad_rows
            ],
            axis=1,
        ).astype(jnp.bfloat16),
        "fsdp",
        scatter_dimension=0,
        tiled=True,
    )
    summed = lax.psum(shared, "ctx").astype(jnp.float32)
    pieces = []
    offset = 0
    for column_width in widths:
        pieces.append(summed[:, offset : offset + column_width])
        offset = offset + column_width
    return tuple(pieces)


def body(
    layer_input,
    cotangent,
    lengths,
    attn_norm,
    query_norm_gain,
    k_norm,
    w_query,
    key_weight,
    value_weight,
    w_out_gate,
    w_output,
    ffn_norm,
    w_gate,
    w_up,
    w_down,
):
    local_rows = layer_input.shape[0]
    block_rows = local_rows * lax.axis_size("tp")
    query_heads = w_query.shape[1] // HEAD_SIZE
    kv_heads = key_weight.shape[1] // HEAD_SIZE
    groups = query_heads // kv_heads
    score_scale = HEAD_SIZE ** (-0.5)
    block_first = lax.axis_index("ctx") * block_rows
    own_slots = (
        block_first + lax.axis_index("tp") * local_rows + jnp.arange(local_rows, dtype=jnp.int32)
    )
    own_valid = (segment_of(own_slots, lengths) < 2).astype(jnp.float32)[:, None]
    query_slots = block_first + jnp.arange(block_rows, dtype=jnp.int32)
    query_segment = segment_of(query_slots, lengths)
    query_position = position_of(query_slots, query_segment, lengths)
    inputs = layer_input.astype(jnp.float32)
    gain_one = attn_norm.astype(jnp.float32)
    gain_two = ffn_norm.astype(jnp.float32)
    query_gain = query_norm_gain.astype(jnp.float32)
    key_gain = k_norm.astype(jnp.float32)
    first_normed = to_block(apply_rms_norm(inputs, gain_one).astype(jnp.bfloat16))
    query_rows, key_projected, value_proj, gate_logits = fold_product(
        first_normed, (w_query, key_weight, value_weight, w_out_gate)
    )
    query_heads_raw = query_rows.reshape(block_rows, query_heads, HEAD_SIZE)
    key_heads_raw = key_projected.reshape(block_rows, kv_heads, HEAD_SIZE)
    query_rotated = apply_rotary(
        apply_rms_norm(query_heads_raw, query_gain), query_position, 1.0
    ).astype(jnp.bfloat16)
    key_rot = apply_rotary(apply_rms_norm(key_heads_raw, key_gain), query_position, 1.0).astype(
        jnp.bfloat16
    )
    query_grouped = query_rotated.reshape(block_rows, kv_heads, groups, HEAD_SIZE)
    key_flat = key_rot.reshape(block_rows, kv_heads * HEAD_SIZE)
    value_reduced = value_proj.astype(jnp.bfloat16)

    def key_mask(piece_rows):
        key_slots = jnp.arange(piece_rows, dtype=jnp.int32)
        key_segment = segment_of(key_slots, lengths)
        return (query_segment[:, None] == key_segment[None, :]) & (
            key_slots[None, :] <= query_slots[:, None]
        )

    head_shape = (kv_heads, groups, block_rows)
    running_top = jnp.full(head_shape + (1,), NEG_FILL, jnp.float32)
    key_piece = lax.all_gather(key_flat, "ctx", axis=0, tiled=True)
    value_piece = lax.all_gather(value_reduced, "ctx", axis=0, tiled=True)
    piece_rows = key_piece.shape[0]
    allowed = key_mask(piece_rows)
    raw_scores = jnp.einsum(
        "qhgd,khd->hgqk",
        query_grouped,
        key_piece.reshape(piece_rows, kv_heads, HEAD_SIZE),
        preferred_element_type=jnp.float32,
    )
    scores = jnp.where(allowed, raw_scores * score_scale, NEG_FILL)
    new_top = jnp.maximum(running_top, jnp.max(scores, axis=-1, keepdims=True))
    weights = jnp.where(allowed, jnp.exp(scores - new_top), 0.0)
    running_total = jnp.sum(weights, axis=-1, keepdims=True)
    mixed_sum = jnp.einsum(
        "hgqk,khd->hgqd",
        weights.astype(jnp.bfloat16),
        value_piece.reshape(piece_rows, kv_heads, HEAD_SIZE),
        preferred_element_type=jnp.float32,
    )
    mixed_sum, running_top, running_total = (mixed_sum, new_top, running_total)
    log_total = running_top + jnp.log(running_total)
    attended = jnp.transpose(mixed_sum / running_total, (2, 0, 1, 3))
    attended_rows = attended.reshape(block_rows, query_heads * HEAD_SIZE)
    gate_sig = jax.nn.sigmoid(gate_logits)
    gated_mix = (attended_rows * gate_sig).astype(jnp.bfloat16)
    attn_share = to_share(fold_product(gated_mix, (w_output,))[0])
    hidden_in = inputs + own_valid * attn_share
    normed_two = to_block(apply_rms_norm(hidden_in, gain_two).astype(jnp.bfloat16))
    gate_pre, up_pre = fold_product(normed_two, (w_gate, w_up))
    gate_sigmoid = jax.nn.sigmoid(gate_pre)
    activated = gate_pre * gate_sigmoid
    hidden_act = (activated * up_pre).astype(jnp.bfloat16)
    ffn_share = to_share(fold_product(hidden_act, (w_down,))[0])
    layer_output = (hidden_in + own_valid * ffn_share).astype(jnp.bfloat16)
    out_grad = cotangent.astype(jnp.float32) * own_valid
    ffn_grad = to_block(out_grad.astype(jnp.bfloat16))
    hidden_grad = back_product((ffn_grad,), (w_down,))
    grad_w_down = weight_grads(hidden_act, (ffn_grad,))[0]
    gate_grad = (
        hidden_grad * up_pre * gate_sigmoid * (1.0 + gate_pre * (1.0 - gate_sigmoid))
    ).astype(jnp.bfloat16)
    up_grad = (hidden_grad * activated).astype(jnp.bfloat16)
    normed_two_grad = to_share(back_product((gate_grad, up_grad), (w_gate, w_up)))
    grad_w_gate, grad_w_up = weight_grads(normed_two, (gate_grad, up_grad))
    back_two, gain_two_grad = norm_back(hidden_in, gain_two, normed_two_grad)
    hidden_total_grad = out_grad + back_two
    attn_grad = to_block((own_valid * hidden_total_grad).astype(jnp.bfloat16))
    gated_grad = back_product((attn_grad,), (w_output,))
    grad_w_output = weight_grads(gated_mix, (attn_grad,))[0]
    mixed_grad = (gated_grad * gate_sig).astype(jnp.bfloat16)
    gate_logit_grad = (gated_grad * attended_rows * gate_sig * (1.0 - gate_sig)).astype(
        jnp.bfloat16
    )
    mixed_grad_heads = mixed_grad.reshape(block_rows, kv_heads, groups, HEAD_SIZE)
    delta_rows = jnp.transpose(
        jnp.sum(mixed_grad_heads.astype(jnp.float32) * attended, axis=-1), (1, 2, 0)
    )[..., None]
    key_piece = lax.all_gather(key_flat, "ctx", axis=0, tiled=True)
    value_piece = lax.all_gather(value_reduced, "ctx", axis=0, tiled=True)
    piece_rows = key_piece.shape[0]
    key_view = key_piece.reshape(piece_rows, kv_heads, HEAD_SIZE)
    value_view = value_piece.reshape(piece_rows, kv_heads, HEAD_SIZE)
    allowed = key_mask(piece_rows)
    raw_scores = jnp.einsum(
        "qhgd,khd->hgqk", query_grouped, key_view, preferred_element_type=jnp.float32
    )
    soft_vals = jnp.where(allowed, jnp.exp(raw_scores * score_scale - log_total), 0.0)
    prob_grad = jnp.einsum(
        "qhgd,khd->hgqk", mixed_grad_heads, value_view, preferred_element_type=jnp.float32
    )
    score_grad = (soft_vals * (prob_grad - delta_rows) * score_scale).astype(jnp.bfloat16)
    query_acc = jnp.einsum(
        "hgqk,khd->qhgd", score_grad, key_view, preferred_element_type=jnp.float32
    )
    key_part = jnp.einsum(
        "hgqk,qhgd->khd", score_grad, query_grouped, preferred_element_type=jnp.float32
    ).reshape(piece_rows, kv_heads * HEAD_SIZE)
    value_part = jnp.einsum(
        "hgqk,qhgd->khd",
        soft_vals.astype(jnp.bfloat16),
        mixed_grad_heads,
        preferred_element_type=jnp.float32,
    ).reshape(piece_rows, kv_heads * HEAD_SIZE)
    kv_acc = jnp.concatenate([key_part, value_part], axis=1)
    query_acc, kv_acc = (query_acc, kv_acc)
    kv_own = lax.psum_scatter(
        kv_acc.astype(jnp.bfloat16), "ctx", scatter_dimension=0, tiled=True
    ).astype(jnp.float32)
    key_rot_grad = kv_own[:, : kv_heads * HEAD_SIZE].reshape(block_rows, kv_heads, HEAD_SIZE)
    value_grad = kv_own[:, kv_heads * HEAD_SIZE :].astype(jnp.bfloat16)
    key_back, key_gain_grad = norm_back(
        key_heads_raw, key_gain, apply_rotary(key_rot_grad, query_position, -1.0)
    )
    query_back, query_gain_grad = norm_back(
        query_heads_raw,
        query_gain,
        apply_rotary(query_acc.reshape(block_rows, query_heads, HEAD_SIZE), query_position, -1.0),
    )
    query_grad = query_back.reshape(block_rows, query_heads * HEAD_SIZE).astype(jnp.bfloat16)
    key_grad = key_back.reshape(block_rows, kv_heads * HEAD_SIZE).astype(jnp.bfloat16)
    attn_in_grads = (query_grad, key_grad, value_grad, gate_logit_grad)
    normed_one_grad = to_share(
        back_product(attn_in_grads, (w_query, key_weight, value_weight, w_out_gate))
    )
    grad_w_query, grad_w_key, grad_w_value, grad_w_out_gate = weight_grads(
        first_normed, attn_in_grads
    )
    back_one, gain_one_grad = norm_back(inputs, gain_one, normed_one_grad)
    input_grad = (hidden_total_grad + back_one).astype(jnp.bfloat16)
    gain_totals = lax.psum(
        (gain_one_grad, query_gain_grad, key_gain_grad, gain_two_grad), ("fsdp", "ctx", "tp")
    )
    return (
        layer_output,
        input_grad,
        gain_totals[0],
        gain_totals[1],
        gain_totals[2],
        grad_w_query,
        grad_w_key,
        grad_w_value,
        grad_w_out_gate,
        grad_w_output,
        gain_totals[3],
        grad_w_gate,
        grad_w_up,
        grad_w_down,
    )


def xor_pairs(count, mask):
    return [(i, i ^ mask) for i in range(count)]


def swap_plane(value, fsdp_mask, tp_mask):
    fsdp_size, tp_size = lax.axis_size("fsdp"), lax.axis_size("tp")
    if tp_mask == 0:
        return lax.ppermute(value, "fsdp", xor_pairs(fsdp_size, fsdp_mask))
    if fsdp_mask == 0:
        return lax.ppermute(value, "tp", xor_pairs(tp_size, tp_mask))
    return lax.ppermute(
        value,
        ("fsdp", "tp"),
        xor_pairs(fsdp_size * tp_size, fsdp_mask * tp_size + tp_mask),
    )


def swap_ranks(value, mask=0):
    size = lax.axis_size("fsdp")
    pairs = [(a * size + b, b * size + (a ^ mask)) for a in range(size) for b in range(size)]
    return lax.ppermute(value, ("fsdp", "ctx"), pairs)


PIECES = ((0, 0), (0, 1), (2, 0), (2, 1))


def plane_beside(own):
    return own, swap_plane(own, 0, 1), swap_plane(own, 2, 0)


def plane_near(beside):
    own, over_tp, over_x = beside
    rows = own.shape[0] // 2
    three = jnp.concatenate([own, over_tp, over_x], axis=0)
    corner = [swap_plane(over_x[:rows], 0, 1), swap_plane(over_tp[rows:], 2, 0)]
    return three, swap_plane(three, 1, 0), jnp.concatenate(corner, axis=0)


def plane_join(near):
    three, three_far, corner = near
    return jnp.concatenate([three, corner, three_far, swap_plane(corner, 1, 0)], axis=0)


def plane_near_apart(beside):
    own, over_tp, over_x = beside
    rows = own.shape[0] // 2
    corner = [swap_plane(over_x[:rows], 0, 1), swap_plane(over_tp[rows:], 2, 0)]
    return list(beside), [swap_plane(piece, 1, 0) for piece in beside], corner


def plane_join_apart(near):
    pieces, far, corner = near
    far_corner = [swap_plane(piece, 1, 0) for piece in corner]
    return jnp.concatenate(pieces + corner + far + far_corner, axis=0)


def scatter_half(near_part, far_part):
    return near_part + swap_plane(far_part.astype(jnp.bfloat16), 1, 0).astype(jnp.float32)


def scatter_plane(half, beside=()):
    rows = half.shape[0] // 8
    piece = [half[at * rows : (at + 1) * rows] for at in range(8)]

    def sent(parts, *masks):
        low = jnp.concatenate(parts, axis=0).astype(jnp.bfloat16)
        return swap_plane(low, *masks)

    by_x = sent([piece[4], piece[6]], 2, 0)
    by_tp = sent([piece[3], piece[7]], 0, 1)
    by_x, by_tp, beside = lax.optimization_barrier((by_x, by_tp, beside))
    by_x, by_tp = by_x.astype(jnp.float32), by_tp.astype(jnp.float32)
    top = sent([piece[2] + by_x[rows:]], 0, 1)
    bottom = sent([piece[5] + by_tp[rows:]], 2, 0)
    return jnp.concatenate([piece[0] + by_x[:rows], piece[1] + by_tp[:rows]], axis=0), [top, bottom], beside


def scatter_total(own, came):
    return own + jnp.concatenate(came, axis=0).astype(jnp.float32)


def dot_nn(a, b):
    return jnp.dot(a, b, preferred_element_type=jnp.float32)


def dot_nt(a, b):
    return lax.dot_general(a, b, (((1,), (1,)), ((), ())), preferred_element_type=jnp.float32)


def dot_tn(a, b):
    return lax.dot_general(a, b, (((0,), (0,)), ((), ())), preferred_element_type=jnp.float32)


INWARD, ACROSS, OUTWARD = [(0, 1), (3, 2)], [(1, 2), (2, 1)], [(1, 0), (2, 3)]


class CtxSums:
    def __init__(self):
        self.flight, self.arrived, self.done = [], [], {}

    def send(self, *fresh):
        place = lax.axis_index("ctx")
        inner = (place == 1) | (place == 2)
        sent, totals, fresh = [], [], list(fresh)
        for stage, name, here, came in self.arrived:
            if stage == 2:
                self.done[name] = here, came
                continue
            both = (here.astype(jnp.float32) + came.astype(jnp.float32)).astype(jnp.bfloat16)
            if stage:
                totals.append((name, both))
            else:
                sent.append(([(1, name, both)], lax.ppermute(both, "ctx", ACROSS)))
        while totals and fresh and totals[0][1].shape == fresh[0][1].shape:
            (out, total), (name, part) = totals.pop(0), fresh.pop(0)
            moved = swap_ctx(jnp.where(inner, total, part))
            sent.append(([(0, name, part), (2, out, total)], moved))
        for name, part in fresh:
            sent.append(([(0, name, part)], lax.ppermute(part, "ctx", INWARD)))
        for name, total in totals:
            sent.append(([(2, name, total)], lax.ppermute(total, "ctx", OUTWARD)))
        self.arrived = []
        self.flight.append(sent)

    def wait(self, kept, depth=1):
        old = []
        while len(self.flight) >= depth:
            old += self.flight.pop(0)
        heres = [[here for _, _, here in entry[0]] for entry in old]
        moved = [entry[1] for entry in old]
        heres, moved, kept = lax.optimization_barrier((heres, moved, kept))
        self.arrived = [
            (stage, name, here, came)
            for entry, parts, came in zip(old, heres, moved)
            for (stage, name, _), here in zip(entry[0], parts)
        ]
        return kept


def sum_hops():
    for axis, mask in (("fsdp", 1), ("fsdp", 2), ("tp", 1)):
        yield axis, xor_pairs(lax.axis_size(axis), mask)


def weight_columns(weights, owner):
    parts = []
    for weight in weights:
        width = weight.shape[1] // lax.axis_size("fsdp")
        parts.append(lax.dynamic_slice_in_dim(weight, owner * width, width, 1))
    return jnp.concatenate(parts, axis=1)


class Fetch:
    def __init__(self, weights):
        self.me, self.size = lax.axis_index("fsdp"), lax.axis_size("fsdp")
        self.side = lax.axis_index("ctx") % 2
        self.rows = weights[0].shape[0]
        self.half = self.rows // 2
        mine = [
            lax.dynamic_slice_in_dim(weight, self.side * self.half, self.half, 0)
            for weight in weights
        ]
        self.columns = [weight_columns(mine, self.me ^ mask) for mask in (2, 3)]
        self.own = weight_columns(weights, self.me)
        self.core = weight_columns(weights, self.me ^ 1)

    def along_x(self, at):
        return swap_plane(self.columns[at], (2, 3)[at], 0)

    def along_core(self):
        return swap_plane(self.core, 1, 0)

    def begin(self, core):
        whole = jnp.zeros((self.rows * self.size, self.own.shape[1]), self.own.dtype)
        for part, peer in ((self.own, self.me), (core, self.me ^ 1)):
            whole = lax.dynamic_update_slice_in_dim(whole, part, peer * self.rows, 0)
        return whole

    def add(self, whole, at, came, other):
        start = (self.me ^ (2, 3)[at]) * self.rows
        whole = lax.dynamic_update_slice_in_dim(whole, came, start + self.side * self.half, 0)
        return lax.dynamic_update_slice_in_dim(
            whole, other, start + (1 - self.side) * self.half, 0
        )


def swap_ctx(value):
    return lax.ppermute(value, "ctx", xor_pairs(lax.axis_size("ctx"), 1))


def grad_part(left, right, mask):
    owner = lax.axis_index("fsdp") ^ mask
    rows = left.shape[1] // lax.axis_size("fsdp")
    columns = lax.dynamic_slice_in_dim(left, owner * rows, rows, 1)
    return dot_tn(columns, right).astype(jnp.bfloat16)


def at_inner():
    place = lax.axis_index("ctx")
    return (place == 1) | (place == 2)


def chosen(pair):
    return jnp.where(at_inner(), *pair).astype(jnp.float32)


def place_columns(pairs, widths):
    size, rows, block = lax.axis_size("fsdp"), pairs[0][0].shape[0], 128
    scalars = jnp.stack([lax.axis_index("fsdp"), at_inner().astype(jnp.int32)])

    def kernel(scalars, *refs):
        parts, outs = refs[: 2 * size], refs[2 * size :]
        for mask in range(size):
            here, came = parts[2 * mask], parts[2 * mask + 1]
            value = jnp.where(
                scalars[1] == 1, here[...].astype(jnp.float32), came[...].astype(jnp.float32)
            )
            start = 0
            for out, width in zip(outs, widths):
                column = pl.multiple_of((scalars[0] ^ mask) * width, 128)
                out[:, pl.ds(column, width)] = value[:, start : start + width]
                start += width

    total = sum(widths)
    return pl.pallas_call(
        kernel,
        grid_spec=pltpu.PrefetchScalarGridSpec(
            num_scalar_prefetch=1,
            grid=(rows // block,),
            in_specs=[pl.BlockSpec((block, total), lambda i, _: (i, 0))] * (2 * size),
            out_specs=[pl.BlockSpec((block, width * size), lambda i, _: (i, 0)) for width in widths],
        ),
        out_shape=[jax.ShapeDtypeStruct((rows, width * size), jnp.float32) for width in widths],
        cost_estimate=pl.CostEstimate(
            flops=0, transcendentals=0, bytes_accessed=8 * rows * total * size
        ),
    )(scalars, *(part for pair in pairs for part in pair))


def plane_body(
    layer_input,
    cotangent,
    lengths,
    attn_norm,
    query_norm_gain,
    k_norm,
    w_query,
    key_weight,
    value_weight,
    w_out_gate,
    w_output,
    ffn_norm,
    w_gate,
    w_up,
    w_down,
):
    fsdp_size, tp_size = lax.axis_size("fsdp"), lax.axis_size("tp")
    fsdp_at, tp_at = lax.axis_index("fsdp"), lax.axis_index("tp")
    local_rows = layer_input.shape[0]
    row_slots = local_rows * fsdp_size * tp_size
    query_heads = w_query.shape[1] // HEAD_SIZE // fsdp_size
    query_width = query_heads * HEAD_SIZE
    score_scale = HEAD_SIZE ** (-0.5)
    gain_one = attn_norm.astype(jnp.float32)
    gain_two = ffn_norm.astype(jnp.float32)
    query_gain = query_norm_gain.astype(jnp.float32)
    key_gain = k_norm.astype(jnp.float32)

    together = lax.optimization_barrier
    input_low = swap_ranks(layer_input)
    attn_fetch = Fetch((w_query, key_weight, value_weight, w_out_gate))
    attn_came = [attn_fetch.along_x(at) for at in range(2)]
    attn_core = attn_fetch.along_core()
    lengths = swap_ranks(lengths)
    input_low, attn_came, cotangent = together((input_low, attn_came, cotangent))
    inputs = input_low.astype(jnp.float32)

    def slots_of(fsdp_index, tp_index):
        return (fsdp_index * tp_size + tp_index) * local_rows + jnp.arange(
            local_rows, dtype=jnp.int32
        )

    own_slots = slots_of(fsdp_at, tp_at)
    own_valid = (segment_of(own_slots, lengths) < 2).astype(jnp.float32)[:, None]
    slots = jnp.concatenate(
        [
            slots_of(fsdp_at ^ fsdp_mask ^ core, tp_at ^ tp_mask)
            for core in (0, 1)
            for fsdp_mask, tp_mask in PIECES
        ]
    )
    segment = segment_of(slots, lengths)
    position = position_of(slots, segment, lengths)

    first_own = apply_rms_norm(inputs, gain_one).astype(jnp.bfloat16)
    first_beside = plane_beside(first_own)
    attn_other = [swap_ctx(came) for came in attn_came]
    cot_low = swap_ranks(cotangent)
    attn_weights = attn_fetch.begin(attn_core)
    first_beside, attn_other, attn_weights = together((first_beside, attn_other, attn_weights))
    first_near = plane_near_apart(first_beside)
    for at in range(2):
        attn_weights = attn_fetch.add(attn_weights, at, attn_came[at], attn_other[at])
    ffn_fetch = Fetch((w_gate, w_up))
    ffn_columns = (ffn_fetch.columns, ffn_fetch.core)
    first_near, attn_weights, ffn_columns = together((first_near, attn_weights, ffn_columns))
    ffn_fetch.columns, ffn_fetch.core = ffn_columns
    ffn_came = [ffn_fetch.along_x(at) for at in range(2)]
    ffn_core = ffn_fetch.along_core()
    first_normed = plane_join_apart(first_near)

    projected = dot_nn(first_normed, attn_weights)
    query_raw = projected[:, :query_width].reshape(row_slots, query_heads, HEAD_SIZE)
    key_raw = projected[:, query_width : query_width + HEAD_SIZE].reshape(row_slots, 1, HEAD_SIZE)
    value_low = projected[:, query_width + HEAD_SIZE : query_width + 2 * HEAD_SIZE].astype(
        jnp.bfloat16
    )
    gate_logits = projected[:, query_width + 2 * HEAD_SIZE :]
    query_rot = apply_rotary(apply_rms_norm(query_raw, query_gain), position, 1.0).astype(
        jnp.bfloat16
    )
    key_rot = apply_rotary(apply_rms_norm(key_raw, key_gain), position, 1.0).astype(jnp.bfloat16)[
        :, 0
    ]

    query_rot, key_rot, value_low, ffn_came[0], cot_low = together(
        (query_rot, key_rot, value_low, ffn_came[0], cot_low)
    )
    ffn_other = swap_ctx(ffn_came[0])
    out_grad = cot_low.astype(jnp.float32) * own_valid
    cot_beside = plane_beside(out_grad.astype(jnp.bfloat16))

    allowed = (segment[:, None] == segment[None, :]) & (slots[None, :] <= slots[:, None])
    raw_scores = jnp.einsum("qgd,kd->gqk", query_rot, key_rot, preferred_element_type=jnp.float32)
    scores = jnp.where(allowed, raw_scores * score_scale, NEG_FILL)
    top = jnp.max(scores, axis=-1, keepdims=True)
    weights = jnp.where(allowed, jnp.exp(scores - top), 0.0)
    total = jnp.sum(weights, axis=-1, keepdims=True)
    mixed = jnp.einsum(
        "gqk,kd->gqd", weights.astype(jnp.bfloat16), value_low, preferred_element_type=jnp.float32
    )
    log_total = top + jnp.log(total)
    attended = jnp.transpose(mixed / total, (1, 0, 2))
    attended_rows = attended.reshape(row_slots, query_width)
    gate_sig = jax.nn.sigmoid(gate_logits)
    gated_mix = (attended_rows * gate_sig).astype(jnp.bfloat16)
    gated_mix, ffn_came, ffn_other = together((gated_mix, ffn_came, ffn_other))
    ffn_others = [ffn_other, swap_ctx(ffn_came[1])]
    half = row_slots // 2
    far_part = dot_nn(gated_mix[half:], w_output)
    near_part = dot_nn(gated_mix[:half], w_output)
    own_part, came_parts, ffn_others[1] = scatter_plane(
        scatter_half(near_part, far_part), ffn_others[1]
    )
    ffn_weights = ffn_fetch.begin(ffn_core)
    ffn_weights = ffn_fetch.add(ffn_weights, 0, ffn_came[0], ffn_others[0])
    own_part, came_parts, cot_beside, ffn_others, ffn_weights, ffn_came = together(
        (own_part, came_parts, cot_beside, ffn_others, ffn_weights, ffn_came)
    )
    cot_near = plane_near(cot_beside)
    hidden_in = inputs + own_valid * scatter_total(own_part, came_parts)
    second_near = plane_near(
        plane_beside(apply_rms_norm(hidden_in, gain_two).astype(jnp.bfloat16))
    )
    ffn_weights = ffn_fetch.add(ffn_weights, 1, ffn_came[1], ffn_others[1])
    second_near, cot_near, ffn_weights = together((second_near, cot_near, ffn_weights))
    ffn_grad = plane_join(cot_near)
    normed_two = plane_join(second_near)

    hidden_grad = dot_nt(ffn_grad, w_down)
    pre = dot_nn(normed_two, ffn_weights)
    hidden_width = w_down.shape[0]
    gate_pre, up_pre = pre[:, :hidden_width], pre[:, hidden_width:]
    gate_sigmoid = jax.nn.sigmoid(gate_pre)
    activated = gate_pre * gate_sigmoid
    hidden_act = (activated * up_pre).astype(jnp.bfloat16)
    gate_grad = (
        hidden_grad * up_pre * gate_sigmoid * (1.0 + gate_pre * (1.0 - gate_sigmoid))
    ).astype(jnp.bfloat16)
    up_grad = (hidden_grad * activated).astype(jnp.bfloat16)
    ffn_in_grads = jnp.concatenate([gate_grad, up_grad], axis=1)

    sums = CtxSums()
    down_parts = jnp.split(dot_tn(hidden_act, ffn_grad).astype(jnp.bfloat16), 2, axis=0)
    down_parts, hidden_act, ffn_in_grads, normed_two = together(
        (down_parts, hidden_act, ffn_in_grads, normed_two)
    )
    sums.send((("down", 0), down_parts[0]))
    two_far = dot_nt(ffn_in_grads[half:], ffn_weights)
    two_near = dot_nt(ffn_in_grads[:half], ffn_weights)
    own_part, came_parts, _ = scatter_plane(scatter_half(two_near, two_far))
    own_part, came_parts, hidden_act, ffn_in_grads, normed_two = sums.wait(
        (own_part, came_parts, hidden_act, ffn_in_grads, normed_two)
    )
    sums.send((("down", 1), down_parts[1]))
    normed_two_grad = scatter_total(own_part, came_parts)
    back_two, gain_two_grad = norm_back(hidden_in, gain_two, normed_two_grad)
    hidden_total_grad = out_grad + back_two
    attn_near = plane_near(plane_beside((own_valid * hidden_total_grad).astype(jnp.bfloat16)))
    ffn_parts = {mask: grad_part(normed_two, ffn_in_grads, mask) for mask in (1, 0, 2, 3)}
    ffn_parts[1] = swap_plane(ffn_parts[1], 1, 0)
    attn_near, ffn_parts, hidden_act, query_rot = sums.wait(
        (attn_near, ffn_parts, hidden_act, query_rot)
    )
    sums.send((("ffn", 0), ffn_parts[0]))
    ffn_parts[2] = swap_plane(ffn_parts[2], 2, 0)
    attn_grad = plane_join(attn_near)
    gated_grad = dot_nt(attn_grad, w_output)
    output_part = dot_tn(gated_mix, attn_grad).astype(jnp.bfloat16)
    mixed_grad = (gated_grad * gate_sig).astype(jnp.bfloat16)
    gate_logit_grad = (gated_grad * attended_rows * gate_sig * (1.0 - gate_sig)).astype(
        jnp.bfloat16
    )
    mixed_grad_heads = mixed_grad.reshape(row_slots, query_heads, HEAD_SIZE)
    delta_rows = jnp.transpose(
        jnp.sum(mixed_grad_heads.astype(jnp.float32) * attended, axis=-1), (1, 0)
    )[..., None]
    raw_again = jnp.einsum("qgd,kd->gqk", query_rot, key_rot, preferred_element_type=jnp.float32)
    soft = jnp.where(allowed, jnp.exp(raw_again * score_scale - log_total), 0.0)
    prob_grad = jnp.einsum(
        "qgd,kd->gqk", mixed_grad_heads, value_low, preferred_element_type=jnp.float32
    )
    score_grad = (soft * (prob_grad - delta_rows) * score_scale).astype(jnp.bfloat16)
    score_grad, soft, ffn_parts, output_part, gate_logit_grad = sums.wait(
        (score_grad, soft.astype(jnp.bfloat16), ffn_parts, output_part, gate_logit_grad)
    )
    sums.send((("ffn", 1), ffn_parts[1]))
    ffn_parts[3] = swap_plane(ffn_parts[3], 3, 0)
    query_rot_grad = jnp.einsum(
        "gqk,kd->qgd", score_grad, key_rot, preferred_element_type=jnp.float32
    )
    key_rot_grad = jnp.einsum(
        "gqk,qgd->kd", score_grad, query_rot, preferred_element_type=jnp.float32
    )
    value_grad = jnp.einsum(
        "gqk,qgd->kd",
        soft,
        mixed_grad_heads,
        preferred_element_type=jnp.float32,
    ).astype(jnp.bfloat16)
    key_back, key_gain_grad = norm_back(
        key_raw, key_gain, apply_rotary(key_rot_grad[:, None], position, -1.0)
    )
    query_back, query_gain_grad = norm_back(
        query_raw, query_gain, apply_rotary(query_rot_grad, position, -1.0)
    )
    attn_in_grads = jnp.concatenate(
        [
            query_back.reshape(row_slots, query_width).astype(jnp.bfloat16),
            key_back[:, 0].astype(jnp.bfloat16),
            value_grad,
            gate_logit_grad,
        ],
        axis=1,
    )
    attn_in_grads, ffn_parts, query_gain_grad, key_gain_grad = sums.wait(
        (attn_in_grads, ffn_parts, query_gain_grad, key_gain_grad)
    )
    sums.send((("ffn", 2), ffn_parts[2]))
    one_far = dot_nt(attn_in_grads[half:], attn_weights)
    one_near = dot_nt(attn_in_grads[:half], attn_weights)
    own_part, came_parts, _ = scatter_plane(scatter_half(one_near, one_far))
    attn_parts = {mask: grad_part(first_normed, attn_in_grads, mask) for mask in (2, 3, 1, 0)}
    attn_parts[1] = swap_plane(attn_parts[1], 1, 0)
    own_part, came_parts, attn_parts, hidden_act = sums.wait(
        (own_part, came_parts, attn_parts, hidden_act)
    )
    hops = sum_hops()

    def hop(value):
        axis, pairs = next(hops)
        return value + lax.ppermute(value, axis, pairs)

    sums.send((("ffn", 3), ffn_parts[3]))
    for mask in (2, 3):
        attn_parts[mask] = swap_plane(attn_parts[mask], mask, 0)
    normed_one_grad = scatter_total(own_part, came_parts)
    back_one, gain_one_grad = norm_back(inputs, gain_one, normed_one_grad)
    input_grad = (hidden_total_grad + back_one).astype(jnp.bfloat16)
    gains = jnp.concatenate([gain_one_grad, gain_two_grad, query_gain_grad, key_gain_grad])[None]
    out_far = dot_nn(hidden_act[half:], w_down).astype(jnp.bfloat16)
    out_near = dot_nn(hidden_act[:half], w_down)
    out_half = scatter_half(out_near, out_far)
    input_grad, gains, out_half, attn_parts = sums.wait((input_grad, gains, out_half, attn_parts))
    sums.send((("output",), output_part))
    gains = hop(gains)
    out_own, out_came, _ = scatter_plane(out_half)
    sums.send((("attn", 0), attn_parts[0]))
    gains, out_own, out_came = sums.wait((gains, out_own, out_came), 2)
    sums.send((("attn", 1), attn_parts[1]))
    gains = sums.wait(hop(gains), 2)
    sums.send((("attn", 2), attn_parts[2]))
    layer_output = hidden_in + own_valid * scatter_total(out_own, out_came)
    gains, layer_output = sums.wait((hop(gains)[0], layer_output.astype(jnp.bfloat16)), 2)
    gain_rows = jnp.pad(gains, (0, 8 * attn_parts[3].shape[1] - gains.shape[0]))
    gain_rows = gain_rows.reshape(8, -1).astype(jnp.bfloat16)
    sums.send((("attn", 3), jnp.concatenate([attn_parts[3], gain_rows], axis=0)))
    grad_w_gate, grad_w_up = place_columns(
        [sums.done["ffn", mask] for mask in range(4)], (hidden_width, hidden_width)
    )
    grad_w_down = jnp.concatenate([chosen(sums.done["down", at]) for at in range(2)], axis=0)
    layer_output = sums.wait(swap_plane(layer_output, 2, 0), 2)
    sums.send()
    grad_w_gate, grad_w_up, grad_w_down, input_grad, layer_output = sums.wait(
        (grad_w_gate, grad_w_up, grad_w_down, input_grad, layer_output), 2
    )
    sums.send()
    input_grad, layer_output = swap_ranks(input_grad), swap_ranks(layer_output, 2)
    grad_w_output = chosen(sums.done["output",])
    grad_w_output = sums.wait(grad_w_output, 2)
    sums.send()
    input_grad, layer_output = sums.wait((input_grad, layer_output))
    while any(sums.flight) or sums.arrived:
        sums.send()
        sums.wait((), 2)
    last_sum = chosen([part[-8:] for part in sums.done["attn", 3]])
    sums.done["attn", 3] = [part[:-8] for part in sums.done["attn", 3]]
    gains = last_sum.reshape(-1)[: gains.shape[0]]
    grad_w_query, grad_w_key, grad_w_value, grad_w_out_gate = place_columns(
        [sums.done["attn", mask] for mask in range(4)],
        (query_width, HEAD_SIZE, HEAD_SIZE, query_width),
    )
    model_width = layer_input.shape[1]
    ends = (model_width, 2 * model_width, 2 * model_width + HEAD_SIZE)
    return (
        layer_output,
        input_grad,
        gains[: ends[0]],
        gains[ends[1] : ends[2]],
        gains[ends[2] :],
        grad_w_query,
        grad_w_key,
        grad_w_value,
        grad_w_out_gate,
        grad_w_output,
        gains[ends[0] : ends[1]],
        grad_w_gate,
        grad_w_up,
        grad_w_down,
    )


def solution(mesh):
    sizes = dict(mesh.shape)
    plane = (sizes["fsdp"], sizes["ctx"], sizes["tp"]) == (4, 4, 2)
    return jax.shard_map(
        plane_body if plane else body,
        mesh=mesh,
        in_specs=(
            P(("fsdp", "ctx", "tp"), None),
            P(("fsdp", "ctx", "tp"), None),
            P("fsdp", None),
            P(),
            P(),
            P(),
            P("fsdp", "tp"),
            P("fsdp", "tp"),
            P("fsdp", "tp"),
            P("fsdp", "tp"),
            P(("tp", "fsdp"), None),
            P(),
            P("fsdp", "tp"),
            P("fsdp", "tp"),
            P(("tp", "fsdp"), None),
        ),
        out_specs=(
            P(("fsdp", "ctx", "tp"), None),
            P(("fsdp", "ctx", "tp"), None),
            P(),
            P(),
            P(),
            P("fsdp", "tp"),
            P("fsdp", "tp"),
            P("fsdp", "tp"),
            P("fsdp", "tp"),
            P(("tp", "fsdp"), None),
            P(),
            P("fsdp", "tp"),
            P("fsdp", "tp"),
            P(("tp", "fsdp"), None),
        ),
        check_vma=False,
    )
```

```python
import jax
import jax.numpy as jnp
from jax import lax
from jax.experimental import pallas as pl
from jax.experimental.pallas import tpu as pltpu
from jax.sharding import PartitionSpec as P

HEAD_SIZE = 128


EPSILON = 1e-06
ROPE_BASE = 1000000.0
NEG_FILL = -1e30


def as_sent(value):

    def short(part):
        return part.astype(jnp.bfloat16) if part.dtype == jnp.float32 else part

    return jax.tree.map(short, value)


def apply_rms_norm(values, gain_vec):
    return (
        values * lax.rsqrt(jnp.mean(values * values, axis=-1, keepdims=True) + EPSILON) * gain_vec
    )


def norm_back(values, gain_vec, grad_in):
    row_scale = lax.rsqrt(jnp.mean(values * values, axis=-1, keepdims=True) + EPSILON)
    unit_rows = values * row_scale
    scaled = grad_in * gain_vec
    back_rows = row_scale * (
        scaled - unit_rows * jnp.mean(scaled * unit_rows, axis=-1, keepdims=True)
    )
    gain_grad = jnp.sum((grad_in * unit_rows).reshape(-1, values.shape[-1]), axis=0)
    return (back_rows, gain_grad)


def apply_rotary(values, token_position, direction):
    half_size = values.shape[-1] // 2
    frequency = jnp.power(ROPE_BASE, -jnp.arange(half_size, dtype=jnp.float32) / half_size)
    angle = token_position.astype(jnp.float32)[:, None] * frequency[None, :]
    cosine = jnp.cos(angle)[:, None, :]
    sine = direction * jnp.sin(angle)[:, None, :]
    first_half = values[..., :half_size]
    second_half = values[..., half_size:]
    return jnp.concatenate(
        [first_half * cosine - second_half * sine, second_half * cosine + first_half * sine],
        axis=-1,
    )


def segment_of(slot_ids, lengths):
    first_len = lengths[0, 0]
    second_len = lengths[0, 1]
    return jnp.where(slot_ids < first_len, 0, jnp.where(slot_ids < first_len + second_len, 1, 2))


def position_of(slot_ids, segment, lengths):
    seg_begin = jnp.where(
        segment == 0, 0, jnp.where(segment == 1, lengths[0, 0], lengths[0, 0] + lengths[0, 1])
    )
    return slot_ids - seg_begin


def to_block(local_part):
    return lax.all_gather(local_part, "tp", axis=0, tiled=True)


def to_share(partial_rows):
    return lax.psum_scatter(
        partial_rows.astype(jnp.bfloat16), "tp", scatter_dimension=0, tiled=True
    ).astype(jnp.float32)


def fold_product(left_rows, weight_set):
    pieces = jax.tree.map(
        lambda a: lax.all_gather(a, "fsdp", axis=0, tiled=True), as_sent(weight_set)
    )
    return tuple(
        (
            jnp.dot(left_rows, weight_part, preferred_element_type=jnp.float32)
            for weight_part in pieces
        )
    )


def back_product(grad_rows, weight_set):
    pieces = jax.tree.map(
        lambda a: lax.all_gather(a, "fsdp", axis=0, tiled=True), as_sent(weight_set)
    )
    result = lax.dot_general(
        grad_rows[0], pieces[0], (((1,), (1,)), ((), ())), preferred_element_type=jnp.float32
    )
    for grad_part, weight_part in zip(grad_rows[1:], pieces[1:]):
        result = result + lax.dot_general(
            grad_part, weight_part, (((1,), (1,)), ((), ())), preferred_element_type=jnp.float32
        )
    return result


def weight_grads(left_rows, grad_rows):
    widths = [grad_part.shape[1] for grad_part in grad_rows]
    shared = lax.psum_scatter(
        jnp.concatenate(
            [
                lax.dot_general(
                    left_rows,
                    grad_part,
                    (((0,), (0,)), ((), ())),
                    preferred_element_type=jnp.float32,
                )
                for grad_part in grad_rows
            ],
            axis=1,
        ).astype(jnp.bfloat16),
        "fsdp",
        scatter_dimension=0,
        tiled=True,
    )
    summed = lax.psum(shared, "ctx").astype(jnp.float32)
    pieces = []
    offset = 0
    for column_width in widths:
        pieces.append(summed[:, offset : offset + column_width])
        offset = offset + column_width
    return tuple(pieces)


def body(
    layer_input,
    cotangent,
    lengths,
    attn_norm,
    query_norm_gain,
    k_norm,
    w_query,
    key_weight,
    value_weight,
    w_out_gate,
    w_output,
    ffn_norm,
    w_gate,
    w_up,
    w_down,
):
    local_rows = layer_input.shape[0]
    block_rows = local_rows * lax.axis_size("tp")
    query_heads = w_query.shape[1] // HEAD_SIZE
    kv_heads = key_weight.shape[1] // HEAD_SIZE
    groups = query_heads // kv_heads
    score_scale = HEAD_SIZE ** (-0.5)
    block_first = lax.axis_index("ctx") * block_rows
    own_slots = (
        block_first + lax.axis_index("tp") * local_rows + jnp.arange(local_rows, dtype=jnp.int32)
    )
    own_valid = (segment_of(own_slots, lengths) < 2).astype(jnp.float32)[:, None]
    query_slots = block_first + jnp.arange(block_rows, dtype=jnp.int32)
    query_segment = segment_of(query_slots, lengths)
    query_position = position_of(query_slots, query_segment, lengths)
    inputs = layer_input.astype(jnp.float32)
    gain_one = attn_norm.astype(jnp.float32)
    gain_two = ffn_norm.astype(jnp.float32)
    query_gain = query_norm_gain.astype(jnp.float32)
    key_gain = k_norm.astype(jnp.float32)
    first_normed = to_block(apply_rms_norm(inputs, gain_one).astype(jnp.bfloat16))
    query_rows, key_projected, value_proj, gate_logits = fold_product(
        first_normed, (w_query, key_weight, value_weight, w_out_gate)
    )
    query_heads_raw = query_rows.reshape(block_rows, query_heads, HEAD_SIZE)
    key_heads_raw = key_projected.reshape(block_rows, kv_heads, HEAD_SIZE)
    query_rotated = apply_rotary(
        apply_rms_norm(query_heads_raw, query_gain), query_position, 1.0
    ).astype(jnp.bfloat16)
    key_rot = apply_rotary(apply_rms_norm(key_heads_raw, key_gain), query_position, 1.0).astype(
        jnp.bfloat16
    )
    query_grouped = query_rotated.reshape(block_rows, kv_heads, groups, HEAD_SIZE)
    key_flat = key_rot.reshape(block_rows, kv_heads * HEAD_SIZE)
    value_reduced = value_proj.astype(jnp.bfloat16)

    def key_mask(piece_rows):
        key_slots = jnp.arange(piece_rows, dtype=jnp.int32)
        key_segment = segment_of(key_slots, lengths)
        return (query_segment[:, None] == key_segment[None, :]) & (
            key_slots[None, :] <= query_slots[:, None]
        )

    head_shape = (kv_heads, groups, block_rows)
    running_top = jnp.full(head_shape + (1,), NEG_FILL, jnp.float32)
    key_piece = lax.all_gather(key_flat, "ctx", axis=0, tiled=True)
    value_piece = lax.all_gather(value_reduced, "ctx", axis=0, tiled=True)
    piece_rows = key_piece.shape[0]
    allowed = key_mask(piece_rows)
    raw_scores = jnp.einsum(
        "qhgd,khd->hgqk",
        query_grouped,
        key_piece.reshape(piece_rows, kv_heads, HEAD_SIZE),
        preferred_element_type=jnp.float32,
    )
    scores = jnp.where(allowed, raw_scores * score_scale, NEG_FILL)
    new_top = jnp.maximum(running_top, jnp.max(scores, axis=-1, keepdims=True))
    weights = jnp.where(allowed, jnp.exp(scores - new_top), 0.0)
    running_total = jnp.sum(weights, axis=-1, keepdims=True)
    mixed_sum = jnp.einsum(
        "hgqk,khd->hgqd",
        weights.astype(jnp.bfloat16),
        value_piece.reshape(piece_rows, kv_heads, HEAD_SIZE),
        preferred_element_type=jnp.float32,
    )
    mixed_sum, running_top, running_total = (mixed_sum, new_top, running_total)
    log_total = running_top + jnp.log(running_total)
    attended = jnp.transpose(mixed_sum / running_total, (2, 0, 1, 3))
    attended_rows = attended.reshape(block_rows, query_heads * HEAD_SIZE)
    gate_sig = jax.nn.sigmoid(gate_logits)
    gated_mix = (attended_rows * gate_sig).astype(jnp.bfloat16)
    attn_share = to_share(fold_product(gated_mix, (w_output,))[0])
    hidden_in = inputs + own_valid * attn_share
    normed_two = to_block(apply_rms_norm(hidden_in, gain_two).astype(jnp.bfloat16))
    gate_pre, up_pre = fold_product(normed_two, (w_gate, w_up))
    gate_sigmoid = jax.nn.sigmoid(gate_pre)
    activated = gate_pre * gate_sigmoid
    hidden_act = (activated * up_pre).astype(jnp.bfloat16)
    ffn_share = to_share(fold_product(hidden_act, (w_down,))[0])
    layer_output = (hidden_in + own_valid * ffn_share).astype(jnp.bfloat16)
    out_grad = cotangent.astype(jnp.float32) * own_valid
    ffn_grad = to_block(out_grad.astype(jnp.bfloat16))
    hidden_grad = back_product((ffn_grad,), (w_down,))
    grad_w_down = weight_grads(hidden_act, (ffn_grad,))[0]
    gate_grad = (
        hidden_grad * up_pre * gate_sigmoid * (1.0 + gate_pre * (1.0 - gate_sigmoid))
    ).astype(jnp.bfloat16)
    up_grad = (hidden_grad * activated).astype(jnp.bfloat16)
    normed_two_grad = to_share(back_product((gate_grad, up_grad), (w_gate, w_up)))
    grad_w_gate, grad_w_up = weight_grads(normed_two, (gate_grad, up_grad))
    back_two, gain_two_grad = norm_back(hidden_in, gain_two, normed_two_grad)
    hidden_total_grad = out_grad + back_two
    attn_grad = to_block((own_valid * hidden_total_grad).astype(jnp.bfloat16))
    gated_grad = back_product((attn_grad,), (w_output,))
    grad_w_output = weight_grads(gated_mix, (attn_grad,))[0]
    mixed_grad = (gated_grad * gate_sig).astype(jnp.bfloat16)
    gate_logit_grad = (gated_grad * attended_rows * gate_sig * (1.0 - gate_sig)).astype(
        jnp.bfloat16
    )
    mixed_grad_heads = mixed_grad.reshape(block_rows, kv_heads, groups, HEAD_SIZE)
    delta_rows = jnp.transpose(
        jnp.sum(mixed_grad_heads.astype(jnp.float32) * attended, axis=-1), (1, 2, 0)
    )[..., None]
    key_piece = lax.all_gather(key_flat, "ctx", axis=0, tiled=True)
    value_piece = lax.all_gather(value_reduced, "ctx", axis=0, tiled=True)
    piece_rows = key_piece.shape[0]
    key_view = key_piece.reshape(piece_rows, kv_heads, HEAD_SIZE)
    value_view = value_piece.reshape(piece_rows, kv_heads, HEAD_SIZE)
    allowed = key_mask(piece_rows)
    raw_scores = jnp.einsum(
        "qhgd,khd->hgqk", query_grouped, key_view, preferred_element_type=jnp.float32
    )
    soft_vals = jnp.where(allowed, jnp.exp(raw_scores * score_scale - log_total), 0.0)
    prob_grad = jnp.einsum(
        "qhgd,khd->hgqk", mixed_grad_heads, value_view, preferred_element_type=jnp.float32
    )
    score_grad = (soft_vals * (prob_grad - delta_rows) * score_scale).astype(jnp.bfloat16)
    query_acc = jnp.einsum(
        "hgqk,khd->qhgd", score_grad, key_view, preferred_element_type=jnp.float32
    )
    key_part = jnp.einsum(
        "hgqk,qhgd->khd", score_grad, query_grouped, preferred_element_type=jnp.float32
    ).reshape(piece_rows, kv_heads * HEAD_SIZE)
    value_part = jnp.einsum(
        "hgqk,qhgd->khd",
        soft_vals.astype(jnp.bfloat16),
        mixed_grad_heads,
        preferred_element_type=jnp.float32,
    ).reshape(piece_rows, kv_heads * HEAD_SIZE)
    kv_acc = jnp.concatenate([key_part, value_part], axis=1)
    query_acc, kv_acc = (query_acc, kv_acc)
    kv_own = lax.psum_scatter(
        kv_acc.astype(jnp.bfloat16), "ctx", scatter_dimension=0, tiled=True
    ).astype(jnp.float32)
    key_rot_grad = kv_own[:, : kv_heads * HEAD_SIZE].reshape(block_rows, kv_heads, HEAD_SIZE)
    value_grad = kv_own[:, kv_heads * HEAD_SIZE :].astype(jnp.bfloat16)
    key_back, key_gain_grad = norm_back(
        key_heads_raw, key_gain, apply_rotary(key_rot_grad, query_position, -1.0)
    )
    query_back, query_gain_grad = norm_back(
        query_heads_raw,
        query_gain,
        apply_rotary(query_acc.reshape(block_rows, query_heads, HEAD_SIZE), query_position, -1.0),
    )
    query_grad = query_back.reshape(block_rows, query_heads * HEAD_SIZE).astype(jnp.bfloat16)
    key_grad = key_back.reshape(block_rows, kv_heads * HEAD_SIZE).astype(jnp.bfloat16)
    attn_in_grads = (query_grad, key_grad, value_grad, gate_logit_grad)
    normed_one_grad = to_share(
        back_product(attn_in_grads, (w_query, key_weight, value_weight, w_out_gate))
    )
    grad_w_query, grad_w_key, grad_w_value, grad_w_out_gate = weight_grads(
        first_normed, attn_in_grads
    )
    back_one, gain_one_grad = norm_back(inputs, gain_one, normed_one_grad)
    input_grad = (hidden_total_grad + back_one).astype(jnp.bfloat16)
    gain_totals = lax.psum(
        (gain_one_grad, query_gain_grad, key_gain_grad, gain_two_grad), ("fsdp", "ctx", "tp")
    )
    return (
        layer_output,
        input_grad,
        gain_totals[0],
        gain_totals[1],
        gain_totals[2],
        grad_w_query,
        grad_w_key,
        grad_w_value,
        grad_w_out_gate,
        grad_w_output,
        gain_totals[3],
        grad_w_gate,
        grad_w_up,
        grad_w_down,
    )


def xor_pairs(count, mask):
    return [(i, i ^ mask) for i in range(count)]


def swap_plane(value, fsdp_mask, tp_mask):
    fsdp_size, tp_size = lax.axis_size("fsdp"), lax.axis_size("tp")
    if tp_mask == 0:
        return lax.ppermute(value, "fsdp", xor_pairs(fsdp_size, fsdp_mask))
    if fsdp_mask == 0:
        return lax.ppermute(value, "tp", xor_pairs(tp_size, tp_mask))
    return lax.ppermute(
        value,
        ("fsdp", "tp"),
        xor_pairs(fsdp_size * tp_size, fsdp_mask * tp_size + tp_mask),
    )


def swap_ranks(value, mask=0):
    size = lax.axis_size("fsdp")
    pairs = [(a * size + b, b * size + (a ^ mask)) for a in range(size) for b in range(size)]
    return lax.ppermute(value, ("fsdp", "ctx"), pairs)


PIECES = ((0, 0), (0, 1), (2, 0), (2, 1))


def plane_beside(own):
    return own, swap_plane(own, 0, 1), swap_plane(own, 2, 0)


def plane_near(beside):
    own, over_tp, over_x = beside
    rows = own.shape[0] // 2
    three = jnp.concatenate([own, over_tp, over_x], axis=0)
    corner = [swap_plane(over_x[:rows], 0, 1), swap_plane(over_tp[rows:], 2, 0)]
    return three, swap_plane(three, 1, 0), jnp.concatenate(corner, axis=0)


def plane_join(near):
    three, three_far, corner = near
    return jnp.concatenate([three, corner, three_far, swap_plane(corner, 1, 0)], axis=0)


def plane_near_apart(beside):
    own, over_tp, over_x = beside
    rows = own.shape[0] // 2
    corner = [swap_plane(over_x[:rows], 0, 1), swap_plane(over_tp[rows:], 2, 0)]
    return list(beside), [swap_plane(piece, 1, 0) for piece in beside], corner


def plane_join_apart(near):
    pieces, far, corner = near
    far_corner = [swap_plane(piece, 1, 0) for piece in corner]
    return jnp.concatenate(pieces + corner + far + far_corner, axis=0)


def scatter_half(near_part, far_part):
    return near_part + swap_plane(far_part.astype(jnp.bfloat16), 1, 0).astype(jnp.float32)


def scatter_plane(half, beside=()):
    rows = half.shape[0] // 8
    piece = [half[at * rows : (at + 1) * rows] for at in range(8)]

    def sent(parts, *masks):
        low = jnp.concatenate(parts, axis=0).astype(jnp.bfloat16)
        return swap_plane(low, *masks)

    by_x = sent([piece[4], piece[6]], 2, 0)
    by_tp = sent([piece[3], piece[7]], 0, 1)
    by_x, by_tp, beside = lax.optimization_barrier((by_x, by_tp, beside))
    by_x, by_tp = by_x.astype(jnp.float32), by_tp.astype(jnp.float32)
    top = sent([piece[2] + by_x[rows:]], 0, 1)
    bottom = sent([piece[5] + by_tp[rows:]], 2, 0)
    return jnp.concatenate([piece[0] + by_x[:rows], piece[1] + by_tp[:rows]], axis=0), [top, bottom], beside


def scatter_total(own, came):
    return own + jnp.concatenate(came, axis=0).astype(jnp.float32)


def dot_nn(a, b):
    return jnp.dot(a, b, preferred_element_type=jnp.float32)


def dot_nt(a, b):
    return lax.dot_general(a, b, (((1,), (1,)), ((), ())), preferred_element_type=jnp.float32)


def dot_tn(a, b):
    return lax.dot_general(a, b, (((0,), (0,)), ((), ())), preferred_element_type=jnp.float32)


INWARD, ACROSS, OUTWARD = [(0, 1), (3, 2)], [(1, 2), (2, 1)], [(1, 0), (2, 3)]


class CtxSums:
    def __init__(self):
        self.flight, self.arrived, self.done = [], [], {}

    def send(self, *fresh):
        place = lax.axis_index("ctx")
        inner = (place == 1) | (place == 2)
        sent, totals, fresh = [], [], list(fresh)
        for stage, name, here, came in self.arrived:
            if stage == 2:
                self.done[name] = here, came
                continue
            both = (here.astype(jnp.float32) + came.astype(jnp.float32)).astype(jnp.bfloat16)
            if stage:
                totals.append((name, both))
            else:
                sent.append(([(1, name, both)], lax.ppermute(both, "ctx", ACROSS)))
        while totals and fresh and totals[0][1].shape == fresh[0][1].shape:
            (out, total), (name, part) = totals.pop(0), fresh.pop(0)
            moved = swap_ctx(jnp.where(inner, total, part))
            sent.append(([(0, name, part), (2, out, total)], moved))
        for name, part in fresh:
            sent.append(([(0, name, part)], lax.ppermute(part, "ctx", INWARD)))
        for name, total in totals:
            sent.append(([(2, name, total)], lax.ppermute(total, "ctx", OUTWARD)))
        self.arrived = []
        self.flight.append(sent)

    def wait(self, kept, depth=1):
        old = []
        while len(self.flight) >= depth:
            old += self.flight.pop(0)
        heres = [[here for _, _, here in entry[0]] for entry in old]
        moved = [entry[1] for entry in old]
        heres, moved, kept = lax.optimization_barrier((heres, moved, kept))
        self.arrived = [
            (stage, name, here, came)
            for entry, parts, came in zip(old, heres, moved)
            for (stage, name, _), here in zip(entry[0], parts)
        ]
        return kept


def sum_hops():
    for axis, mask in (("fsdp", 1), ("fsdp", 2), ("tp", 1)):
        yield axis, xor_pairs(lax.axis_size(axis), mask)


def weight_columns(weights, owner):
    parts = []
    for weight in weights:
        width = weight.shape[1] // lax.axis_size("fsdp")
        parts.append(lax.dynamic_slice_in_dim(weight, owner * width, width, 1))
    return jnp.concatenate(parts, axis=1)


class Fetch:
    def __init__(self, weights):
        self.me, self.size = lax.axis_index("fsdp"), lax.axis_size("fsdp")
        self.side = lax.axis_index("ctx") % 2
        self.rows = weights[0].shape[0]
        self.half = self.rows // 2
        mine = [
            lax.dynamic_slice_in_dim(weight, self.side * self.half, self.half, 0)
            for weight in weights
        ]
        self.columns = [weight_columns(mine, self.me ^ mask) for mask in (2, 3)]
        self.own = weight_columns(weights, self.me)
        self.core = weight_columns(weights, self.me ^ 1)

    def along_x(self, at):
        return swap_plane(self.columns[at], (2, 3)[at], 0)

    def along_core(self):
        return swap_plane(self.core, 1, 0)

    def begin(self, core):
        whole = jnp.zeros((self.rows * self.size, self.own.shape[1]), self.own.dtype)
        for part, peer in ((self.own, self.me), (core, self.me ^ 1)):
            whole = lax.dynamic_update_slice_in_dim(whole, part, peer * self.rows, 0)
        return whole

    def add(self, whole, at, came, other):
        start = (self.me ^ (2, 3)[at]) * self.rows
        whole = lax.dynamic_update_slice_in_dim(whole, came, start + self.side * self.half, 0)
        return lax.dynamic_update_slice_in_dim(
            whole, other, start + (1 - self.side) * self.half, 0
        )


def swap_ctx(value):
    return lax.ppermute(value, "ctx", xor_pairs(lax.axis_size("ctx"), 1))


def grad_part(left, right, mask):
    owner = lax.axis_index("fsdp") ^ mask
    rows = left.shape[1] // lax.axis_size("fsdp")
    columns = lax.dynamic_slice_in_dim(left, owner * rows, rows, 1)
    return dot_tn(columns, right).astype(jnp.bfloat16)


def at_inner():
    place = lax.axis_index("ctx")
    return (place == 1) | (place == 2)


def chosen(pair):
    return jnp.where(at_inner(), *pair).astype(jnp.float32)


def place_columns(pairs, widths):
    size, rows, block = lax.axis_size("fsdp"), pairs[0][0].shape[0], 256
    scalars = jnp.stack([lax.axis_index("fsdp"), at_inner().astype(jnp.int32)])

    def kernel(scalars, *refs):
        parts, outs = refs[: 2 * size], refs[2 * size :]
        for mask in range(size):
            here, came = parts[2 * mask], parts[2 * mask + 1]
            value = jnp.where(
                scalars[1] == 1, here[...].astype(jnp.float32), came[...].astype(jnp.float32)
            )
            start = 0
            for out, width in zip(outs, widths):
                column = pl.multiple_of((scalars[0] ^ mask) * width, 128)
                out[:, pl.ds(column, width)] = value[:, start : start + width]
                start += width

    total = sum(widths)
    return pl.pallas_call(
        kernel,
        grid_spec=pltpu.PrefetchScalarGridSpec(
            num_scalar_prefetch=1,
            grid=(rows // block,),
            in_specs=[pl.BlockSpec((block, total), lambda i, _: (i, 0))] * (2 * size),
            out_specs=[pl.BlockSpec((block, width * size), lambda i, _: (i, 0)) for width in widths],
        ),
        out_shape=[jax.ShapeDtypeStruct((rows, width * size), jnp.float32) for width in widths],
        cost_estimate=pl.CostEstimate(
            flops=0, transcendentals=0, bytes_accessed=8 * rows * total * size
        ),
    )(scalars, *(part for pair in pairs for part in pair))


def plane_body(
    layer_input,
    cotangent,
    lengths,
    attn_norm,
    query_norm_gain,
    k_norm,
    w_query,
    key_weight,
    value_weight,
    w_out_gate,
    w_output,
    ffn_norm,
    w_gate,
    w_up,
    w_down,
):
    fsdp_size, tp_size = lax.axis_size("fsdp"), lax.axis_size("tp")
    fsdp_at, tp_at = lax.axis_index("fsdp"), lax.axis_index("tp")
    local_rows = layer_input.shape[0]
    row_slots = local_rows * fsdp_size * tp_size
    query_heads = w_query.shape[1] // HEAD_SIZE // fsdp_size
    query_width = query_heads * HEAD_SIZE
    score_scale = HEAD_SIZE ** (-0.5)
    gain_one = attn_norm.astype(jnp.float32)
    gain_two = ffn_norm.astype(jnp.float32)
    query_gain = query_norm_gain.astype(jnp.float32)
    key_gain = k_norm.astype(jnp.float32)

    together = lax.optimization_barrier
    input_low = swap_ranks(layer_input)
    attn_fetch = Fetch((w_query, key_weight, value_weight, w_out_gate))
    attn_came = [attn_fetch.along_x(at) for at in range(2)]
    attn_core = attn_fetch.along_core()
    lengths = swap_ranks(lengths)
    input_low, attn_came, cotangent = together((input_low, attn_came, cotangent))
    inputs = input_low.astype(jnp.float32)

    def slots_of(fsdp_index, tp_index):
        return (fsdp_index * tp_size + tp_index) * local_rows + jnp.arange(
            local_rows, dtype=jnp.int32
        )

    own_slots = slots_of(fsdp_at, tp_at)
    own_valid = (segment_of(own_slots, lengths) < 2).astype(jnp.float32)[:, None]
    slots = jnp.concatenate(
        [
            slots_of(fsdp_at ^ fsdp_mask ^ core, tp_at ^ tp_mask)
            for core in (0, 1)
            for fsdp_mask, tp_mask in PIECES
        ]
    )
    segment = segment_of(slots, lengths)
    position = position_of(slots, segment, lengths)

    first_own = apply_rms_norm(inputs, gain_one).astype(jnp.bfloat16)
    first_beside = plane_beside(first_own)
    attn_other = [swap_ctx(came) for came in attn_came]
    cot_low = swap_ranks(cotangent)
    attn_weights = attn_fetch.begin(attn_core)
    first_beside, attn_other, attn_weights = together((first_beside, attn_other, attn_weights))
    first_near = plane_near_apart(first_beside)
    for at in range(2):
        attn_weights = attn_fetch.add(attn_weights, at, attn_came[at], attn_other[at])
    ffn_fetch = Fetch((w_gate, w_up))
    ffn_columns = (ffn_fetch.columns, ffn_fetch.core)
    first_near, attn_weights, ffn_columns = together((first_near, attn_weights, ffn_columns))
    ffn_fetch.columns, ffn_fetch.core = ffn_columns
    ffn_came = [ffn_fetch.along_x(at) for at in range(2)]
    ffn_core = ffn_fetch.along_core()
    first_normed = plane_join_apart(first_near)

    projected = dot_nn(first_normed, attn_weights)
    query_raw = projected[:, :query_width].reshape(row_slots, query_heads, HEAD_SIZE)
    key_raw = projected[:, query_width : query_width + HEAD_SIZE].reshape(row_slots, 1, HEAD_SIZE)
    value_low = projected[:, query_width + HEAD_SIZE : query_width + 2 * HEAD_SIZE].astype(
        jnp.bfloat16
    )
    gate_logits = projected[:, query_width + 2 * HEAD_SIZE :]
    query_rot = apply_rotary(apply_rms_norm(query_raw, query_gain), position, 1.0).astype(
        jnp.bfloat16
    )
    key_rot = apply_rotary(apply_rms_norm(key_raw, key_gain), position, 1.0).astype(jnp.bfloat16)[
        :, 0
    ]

    query_rot, key_rot, value_low, ffn_came[0], cot_low = together(
        (query_rot, key_rot, value_low, ffn_came[0], cot_low)
    )
    ffn_other = swap_ctx(ffn_came[0])
    out_grad = cot_low.astype(jnp.float32) * own_valid
    cot_beside = plane_beside(out_grad.astype(jnp.bfloat16))

    allowed = (segment[:, None] == segment[None, :]) & (slots[None, :] <= slots[:, None])
    raw_scores = jnp.einsum("qgd,kd->gqk", query_rot, key_rot, preferred_element_type=jnp.float32)
    scores = jnp.where(allowed, raw_scores * score_scale, NEG_FILL)
    top = jnp.max(scores, axis=-1, keepdims=True)
    weights = jnp.where(allowed, jnp.exp(scores - top), 0.0)
    total = jnp.sum(weights, axis=-1, keepdims=True)
    mixed = jnp.einsum(
        "gqk,kd->gqd", weights.astype(jnp.bfloat16), value_low, preferred_element_type=jnp.float32
    )
    log_total = top + jnp.log(total)
    attended = jnp.transpose(mixed / total, (1, 0, 2))
    attended_rows = attended.reshape(row_slots, query_width)
    gate_sig = jax.nn.sigmoid(gate_logits)
    gated_mix = (attended_rows * gate_sig).astype(jnp.bfloat16)
    gated_mix, ffn_came, ffn_other = together((gated_mix, ffn_came, ffn_other))
    ffn_others = [ffn_other, swap_ctx(ffn_came[1])]
    half = row_slots // 2
    far_part = dot_nn(gated_mix[half:], w_output)
    near_part = dot_nn(gated_mix[:half], w_output)
    own_part, came_parts, ffn_others[1] = scatter_plane(
        scatter_half(near_part, far_part), ffn_others[1]
    )
    ffn_weights = ffn_fetch.begin(ffn_core)
    ffn_weights = ffn_fetch.add(ffn_weights, 0, ffn_came[0], ffn_others[0])
    own_part, came_parts, cot_beside, ffn_others, ffn_weights, ffn_came = together(
        (own_part, came_parts, cot_beside, ffn_others, ffn_weights, ffn_came)
    )
    cot_near = plane_near(cot_beside)
    hidden_in = inputs + own_valid * scatter_total(own_part, came_parts)
    second_near = plane_near(
        plane_beside(apply_rms_norm(hidden_in, gain_two).astype(jnp.bfloat16))
    )
    ffn_weights = ffn_fetch.add(ffn_weights, 1, ffn_came[1], ffn_others[1])
    second_near, cot_near, ffn_weights = together((second_near, cot_near, ffn_weights))
    ffn_grad = plane_join(cot_near)
    normed_two = plane_join(second_near)

    hidden_grad = dot_nt(ffn_grad, w_down)
    pre = dot_nn(normed_two, ffn_weights)
    hidden_width = w_down.shape[0]
    gate_pre, up_pre = pre[:, :hidden_width], pre[:, hidden_width:]
    gate_sigmoid = jax.nn.sigmoid(gate_pre)
    activated = gate_pre * gate_sigmoid
    hidden_act = (activated * up_pre).astype(jnp.bfloat16)
    gate_grad = (
        hidden_grad * up_pre * gate_sigmoid * (1.0 + gate_pre * (1.0 - gate_sigmoid))
    ).astype(jnp.bfloat16)
    up_grad = (hidden_grad * activated).astype(jnp.bfloat16)
    ffn_in_grads = jnp.concatenate([gate_grad, up_grad], axis=1)

    sums = CtxSums()
    down_parts = jnp.split(dot_tn(hidden_act, ffn_grad).astype(jnp.bfloat16), 2, axis=0)
    down_parts, hidden_act, ffn_in_grads, normed_two = together(
        (down_parts, hidden_act, ffn_in_grads, normed_two)
    )
    sums.send((("down", 0), down_parts[0]))
    two_far = dot_nt(ffn_in_grads[half:], ffn_weights)
    two_near = dot_nt(ffn_in_grads[:half], ffn_weights)
    own_part, came_parts, _ = scatter_plane(scatter_half(two_near, two_far))
    own_part, came_parts, hidden_act, ffn_in_grads, normed_two = sums.wait(
        (own_part, came_parts, hidden_act, ffn_in_grads, normed_two)
    )
    sums.send((("down", 1), down_parts[1]))
    normed_two_grad = scatter_total(own_part, came_parts)
    back_two, gain_two_grad = norm_back(hidden_in, gain_two, normed_two_grad)
    hidden_total_grad = out_grad + back_two
    attn_near = plane_near(plane_beside((own_valid * hidden_total_grad).astype(jnp.bfloat16)))
    ffn_parts = {mask: grad_part(normed_two, ffn_in_grads, mask) for mask in (1, 0, 2, 3)}
    ffn_parts[1] = swap_plane(ffn_parts[1], 1, 0)
    attn_near, ffn_parts, hidden_act, query_rot = sums.wait(
        (attn_near, ffn_parts, hidden_act, query_rot)
    )
    sums.send((("ffn", 0), ffn_parts[0]))
    ffn_parts[2] = swap_plane(ffn_parts[2], 2, 0)
    attn_grad = plane_join(attn_near)
    gated_grad = dot_nt(attn_grad, w_output)
    output_part = dot_tn(gated_mix, attn_grad).astype(jnp.bfloat16)
    mixed_grad = (gated_grad * gate_sig).astype(jnp.bfloat16)
    gate_logit_grad = (gated_grad * attended_rows * gate_sig * (1.0 - gate_sig)).astype(
        jnp.bfloat16
    )
    mixed_grad_heads = mixed_grad.reshape(row_slots, query_heads, HEAD_SIZE)
    delta_rows = jnp.transpose(
        jnp.sum(mixed_grad_heads.astype(jnp.float32) * attended, axis=-1), (1, 0)
    )[..., None]
    raw_again = jnp.einsum("qgd,kd->gqk", query_rot, key_rot, preferred_element_type=jnp.float32)
    soft = jnp.where(allowed, jnp.exp(raw_again * score_scale - log_total), 0.0)
    prob_grad = jnp.einsum(
        "qgd,kd->gqk", mixed_grad_heads, value_low, preferred_element_type=jnp.float32
    )
    score_grad = (soft * (prob_grad - delta_rows) * score_scale).astype(jnp.bfloat16)
    score_grad, soft, ffn_parts, output_part, gate_logit_grad = sums.wait(
        (score_grad, soft.astype(jnp.bfloat16), ffn_parts, output_part, gate_logit_grad)
    )
    sums.send((("ffn", 1), ffn_parts[1]))
    ffn_parts[3] = swap_plane(ffn_parts[3], 3, 0)
    query_rot_grad = jnp.einsum(
        "gqk,kd->qgd", score_grad, key_rot, preferred_element_type=jnp.float32
    )
    key_rot_grad = jnp.einsum(
        "gqk,qgd->kd", score_grad, query_rot, preferred_element_type=jnp.float32
    )
    value_grad = jnp.einsum(
        "gqk,qgd->kd",
        soft,
        mixed_grad_heads,
        preferred_element_type=jnp.float32,
    ).astype(jnp.bfloat16)
    key_back, key_gain_grad = norm_back(
        key_raw, key_gain, apply_rotary(key_rot_grad[:, None], position, -1.0)
    )
    query_back, query_gain_grad = norm_back(
        query_raw, query_gain, apply_rotary(query_rot_grad, position, -1.0)
    )
    attn_in_grads = jnp.concatenate(
        [
            query_back.reshape(row_slots, query_width).astype(jnp.bfloat16),
            key_back[:, 0].astype(jnp.bfloat16),
            value_grad,
            gate_logit_grad,
        ],
        axis=1,
    )
    attn_in_grads, ffn_parts, query_gain_grad, key_gain_grad = sums.wait(
        (attn_in_grads, ffn_parts, query_gain_grad, key_gain_grad)
    )
    sums.send((("ffn", 2), ffn_parts[2]))
    one_far = dot_nt(attn_in_grads[half:], attn_weights)
    one_near = dot_nt(attn_in_grads[:half], attn_weights)
    own_part, came_parts, _ = scatter_plane(scatter_half(one_near, one_far))
    attn_parts = {mask: grad_part(first_normed, attn_in_grads, mask) for mask in (2, 3, 1, 0)}
    attn_parts[1] = swap_plane(attn_parts[1], 1, 0)
    own_part, came_parts, attn_parts, hidden_act = sums.wait(
        (own_part, came_parts, attn_parts, hidden_act)
    )
    hops = sum_hops()

    def hop(value):
        axis, pairs = next(hops)
        return value + lax.ppermute(value, axis, pairs)

    sums.send((("ffn", 3), ffn_parts[3]))
    for mask in (2, 3):
        attn_parts[mask] = swap_plane(attn_parts[mask], mask, 0)
    normed_one_grad = scatter_total(own_part, came_parts)
    back_one, gain_one_grad = norm_back(inputs, gain_one, normed_one_grad)
    input_grad = (hidden_total_grad + back_one).astype(jnp.bfloat16)
    gains = jnp.concatenate([gain_one_grad, gain_two_grad, query_gain_grad, key_gain_grad])[None]
    out_far = dot_nn(hidden_act[half:], w_down).astype(jnp.bfloat16)
    out_near = dot_nn(hidden_act[:half], w_down)
    out_half = scatter_half(out_near, out_far)
    input_grad, gains, out_half, attn_parts = sums.wait((input_grad, gains, out_half, attn_parts))
    sums.send((("output",), output_part))
    gains = hop(gains)
    out_own, out_came, _ = scatter_plane(out_half)
    sums.send((("attn", 0), attn_parts[0]))
    gains, out_own, out_came = sums.wait((gains, out_own, out_came), 2)
    sums.send((("attn", 1), attn_parts[1]))
    gains = sums.wait(hop(gains), 2)
    sums.send((("attn", 2), attn_parts[2]))
    layer_output = hidden_in + own_valid * scatter_total(out_own, out_came)
    gains, layer_output = sums.wait((hop(gains)[0], layer_output.astype(jnp.bfloat16)), 2)
    gain_rows = jnp.pad(gains, (0, 8 * attn_parts[3].shape[1] - gains.shape[0]))
    gain_rows = gain_rows.reshape(8, -1).astype(jnp.bfloat16)
    sums.send((("attn", 3), jnp.concatenate([attn_parts[3], gain_rows], axis=0)))
    grad_w_gate, grad_w_up = place_columns(
        [sums.done["ffn", mask] for mask in range(4)], (hidden_width, hidden_width)
    )
    grad_w_down = jnp.concatenate([chosen(sums.done["down", at]) for at in range(2)], axis=0)
    layer_output = sums.wait(swap_plane(layer_output, 2, 0), 2)
    sums.send()
    grad_w_gate, grad_w_up, grad_w_down, input_grad, layer_output = sums.wait(
        (grad_w_gate, grad_w_up, grad_w_down, input_grad, layer_output), 2
    )
    sums.send()
    input_grad, layer_output = swap_ranks(input_grad), swap_ranks(layer_output, 2)
    grad_w_output = chosen(sums.done["output",])
    grad_w_output = sums.wait(grad_w_output, 2)
    sums.send()
    input_grad, layer_output = sums.wait((input_grad, layer_output))
    while any(sums.flight) or sums.arrived:
        sums.send()
        sums.wait((), 2)
    last_sum = chosen([part[-8:] for part in sums.done["attn", 3]])
    sums.done["attn", 3] = [part[:-8] for part in sums.done["attn", 3]]
    gains = last_sum.reshape(-1)[: gains.shape[0]]
    grad_w_query, grad_w_key, grad_w_value, grad_w_out_gate = place_columns(
        [sums.done["attn", mask] for mask in range(4)],
        (query_width, HEAD_SIZE, HEAD_SIZE, query_width),
    )
    model_width = layer_input.shape[1]
    ends = (model_width, 2 * model_width, 2 * model_width + HEAD_SIZE)
    return (
        layer_output,
        input_grad,
        gains[: ends[0]],
        gains[ends[1] : ends[2]],
        gains[ends[2] :],
        grad_w_query,
        grad_w_key,
        grad_w_value,
        grad_w_out_gate,
        grad_w_output,
        gains[ends[0] : ends[1]],
        grad_w_gate,
        grad_w_up,
        grad_w_down,
    )


def solution(mesh):
    sizes = dict(mesh.shape)
    plane = (sizes["fsdp"], sizes["ctx"], sizes["tp"]) == (4, 4, 2)
    return jax.shard_map(
        plane_body if plane else body,
        mesh=mesh,
        in_specs=(
            P(("fsdp", "ctx", "tp"), None),
            P(("fsdp", "ctx", "tp"), None),
            P("fsdp", None),
            P(),
            P(),
            P(),
            P("fsdp", "tp"),
            P("fsdp", "tp"),
            P("fsdp", "tp"),
            P("fsdp", "tp"),
            P(("tp", "fsdp"), None),
            P(),
            P("fsdp", "tp"),
            P("fsdp", "tp"),
            P(("tp", "fsdp"), None),
        ),
        out_specs=(
            P(("fsdp", "ctx", "tp"), None),
            P(("fsdp", "ctx", "tp"), None),
            P(),
            P(),
            P(),
            P("fsdp", "tp"),
            P("fsdp", "tp"),
            P("fsdp", "tp"),
            P("fsdp", "tp"),
            P(("tp", "fsdp"), None),
            P(),
            P("fsdp", "tp"),
            P("fsdp", "tp"),
            P(("tp", "fsdp"), None),
        ),
        check_vma=False,
    )
```
